32 devices in a mesh: dp: 8 (over z, y), db: 4 (over x, core).
Axes of the slice: x: 2, y: 2, z: 4, core: 2. Of those that a mesh axis runs over, the one named last changes fastest.
Arguments:
- queries: bfloat16 [8, 1024, 2048], P('dp', 'db'), may hold values from -6 to 6
- cotangent: bfloat16 [8, 1024, 2048], P('dp', 'db'), may hold values from -6 to 6
- w_key: bfloat16 [896, 2048], replicated, may hold values from -0.1875 to 0.1875
- w_value: bfloat16 [896, 2048], replicated, may hold values from -0.1875 to 0.1875
- database: bfloat16 [128, 128, 896], P('db'), may hold values from -6 to 6
- nb_shard: int32 [8, 16, 2], P('dp', 'db'), may hold values from 0 to 3, all different within a row; in each aligned block of 4 rows (0 to 3, 4 to 7, ..., all dimensions but the last counted through in order) at most 3 rows name the same one
- nb_row: int32 [8, 16, 2], P('dp', 'db'), may hold values from 0 to 31
Outputs:
- attn_out: bfloat16 [8, 1024, 2048], P('dp', 'db')
- grad_queries: bfloat16 [8, 1024, 2048], P('dp', 'db')
- grad_wkey: float32 [896, 2048], P(('dp', 'db'))
- grad_wvalue: float32 [896, 2048], P(('dp', 'db'))
- grad_database: bfloat16 [128, 128, 896], P('db', 'dp')
The draws below stay inside these ranges and needn't reach their ends.
Inputs may be any that keep to these rules, and one draw needn't show every extreme that they name: `nb_shard`: the 2 neighbours of a stretch lie on different shards; among the stretches of one device (aligned blocks of 4 stretches of a sequence) at most 3 name the same shard, a bound that some block reaches.
All inputs are finite; a program needn't handle non-finite values.
Results may differ from the reference program's by a relative error of at most 0.015.
Values may be sent and summed in bfloat16 or wider, within the bound.
A program may use at most 192 MiB of HBM per device.

```python
import math
import jax
import jax.numpy as jnp
import numpy as np
from jax import lax

HEADS = 16
HSIZE = 128
ENC = 896
STRETCH = 64
NEIGH = 2
NB_LEN = 128
CH_DEV = 4
DB_DEV = 32
HD = 2048
SEQS = 8
LENGTH = 1024
STRETCHES = 16
DB = 128
CAP = 3
N_DB = 4


def plant(drawn, own_key, least, high):
    extent = drawn.shape
    spot = [jax.random.randint(jax.random.fold_in(own_key, axis), (), 0, extent[axis]) for axis in range(len(extent))]
    drawn = drawn.at[tuple(spot)].set(least)
    longest = extent.index(max(extent))
    spot[longest] = (spot[longest] + 1) % extent[longest]
    return drawn.at[tuple(spot)].set(high)


def block_levels(own_key, extent, split, low, top_value):
    def one(position, blocks):
        draws = jax.random.uniform(jax.random.fold_in(jax.random.fold_in(own_key, 6), position), (blocks,), jnp.float32, low / len(split), top_value / len(split))
        return jnp.repeat(jnp.exp(draws), extent[position] // blocks).reshape((-1,) + (1,) * (len(extent) - position - 1))

    level = one(*split[0])
    for cut in split[1:]:
        level = level * one(*cut)
    return level


def assign_block(key, own, number, rows, count, top, bound, skew):
    order = jax.random.permutation(key, count)
    crowded, usual = load_shares(count, rows * top, bound, skew, True), load_shares(count, rows * top, bound, skew, False)
    places = jnp.arange(count)

    def named(tallies, turn):
        used = int((tallies > 0).sum())
        fixed = max(1, used // 4)
        moved = fixed + (places - fixed + turn * (used - fixed)) % max(1, count - fixed)
        return jnp.zeros((count,), jnp.int32).at[order[jnp.where(places < fixed, places, moved)]].set(jnp.asarray(tallies, jnp.int32))

    tallies = jnp.where(number % 4 == 0, named(crowded, number // 4), named(usual, number - number // 4 - 1))
    mixed = jax.random.permutation(jax.random.fold_in(own, 3), count)
    donor, receiver = mixed[0:count // 2 * 2:2], mixed[1:count // 2 * 2:2]
    slack = jnp.minimum(tallies[donor] - 1, bound - tallies[receiver]) // 2
    slack = jnp.where((donor == order[0]) | (receiver == order[0]) | (tallies[receiver] == 0), 0, jnp.maximum(slack, 0))
    moved = jax.random.randint(jax.random.fold_in(own, 4), (count // 2,), 0, 1 << 20) % (slack + 1)
    tallies = tallies.at[donor].add(-moved).at[receiver].add(moved)
    items = jnp.searchsorted(jnp.cumsum(tallies), jnp.arange(rows * top), side="right").astype(jnp.int32)
    grid = items.reshape(top, rows).T
    grid = grid[jax.random.permutation(jax.random.fold_in(own, 1), rows)]
    turn = jax.random.randint(jax.random.fold_in(own, 2), (rows, 1), 0, top)
    return jnp.take_along_axis(grid, (jnp.arange(top)[None, :] + turn) % top, axis=1)


def load_shares(count, total, most, lean, full):
    weights = [(1 << 20) // math.isqrt(standing ** lean) + 1 for standing in range(1, count + 1)]
    largest = most if full else min(most, max(-(-total // count), total * weights[0] // sum(weights)))
    least = 1 if total - largest >= count - 1 else 0
    counts, rest = [largest] + [least] * (count - 1), total - largest - least * (count - 1)
    while rest > 0:
        candidates = [i for i in range(1, count) if counts[i] < largest] or [i for i in range(1, count) if counts[i] < most]
        mass, remaining = sum([weights[i] for i in candidates]), rest
        for i in candidates:
            extra = min(most - counts[i], max(1, remaining * weights[i] // mass), rest)
            counts[i] = counts[i] + extra
            rest = rest - extra
    return np.array(counts)


def noise(own_key, extent, spread, most, shards=(), held_as=jnp.bfloat16):
    array = spread * jax.random.normal(own_key, extent, jnp.float32)
    if shards:
        array = array * block_levels(own_key, extent, shards, -0.22, 0.18)
    return jnp.clip(array, -most, most).astype(held_as)


def setup_inputs(seed: int = 0) -> dict:
    seeds = jax.random.split(jax.random.key(seed), 8)
    queries = noise(seeds[0], (SEQS, LENGTH, HD), 1.0, 6.0, ((0, 8), (1, 4)))
    cotangent = noise(seeds[1], (SEQS, LENGTH, HD), 1.0, 6.0, ((0, 8), (1, 4)))
    w_key = noise(seeds[2], (ENC, HD), ENC ** -0.5, 0.1875)
    w_value = noise(seeds[3], (ENC, HD), ENC ** -0.5, 0.1875)
    database = noise(seeds[4], (DB, NB_LEN, ENC), 1.0, 6.0, ((0, 4),))
    nb_shard_keys = jax.random.split(jax.random.fold_in(seeds[5], 1), SEQS * STRETCHES // CH_DEV)
    nb_shard_turns = jax.random.permutation(jax.random.fold_in(seeds[5], 3), SEQS * STRETCHES // CH_DEV)
    nb_shard = jax.vmap(lambda own, number: assign_block(jax.random.fold_in(seeds[5], 2), own, number, CH_DEV, N_DB, NEIGH, CAP, 2))(nb_shard_keys, nb_shard_turns).reshape((SEQS, STRETCHES, NEIGH))
    nb_row = plant(jax.random.randint(seeds[6], (SEQS, STRETCHES, NEIGH), 0, DB_DEV), jax.random.fold_in(seeds[6], 1), 0, DB_DEV - 1).astype(jnp.int32)
    return {"queries": queries, "cotangent": cotangent, "w_key": w_key, "w_value": w_value, "database": database, "nb_shard": nb_shard, "nb_row": nb_row}


def attend_blocks(block_q, block_g, states, w_key, w_value):
    blocks, length, width = block_q.shape
    span = states.shape[1]
    head_size = width // HEADS
    scale = 1.0 / math.sqrt(head_size)
    keys = jnp.einsum('bre,ef->brf', states.astype(jnp.float32), w_key.astype(jnp.float32)).astype(jnp.bfloat16)
    values = jnp.einsum('bre,ef->brf', states.astype(jnp.float32), w_value.astype(jnp.float32)).astype(jnp.bfloat16)
    q_four = block_q.reshape(blocks, length, HEADS, head_size).astype(jnp.float32)
    g_four = block_g.reshape(blocks, length, HEADS, head_size).astype(jnp.float32)
    k_four = keys.reshape(blocks, span, HEADS, head_size).astype(jnp.float32)
    v_four = values.reshape(blocks, span, HEADS, head_size).astype(jnp.float32)
    scores = jnp.einsum('bchd,brhd->bhcr', q_four, k_four) * scale
    top = lax.optimization_barrier(jnp.max(scores, axis=-1, keepdims=True))
    expo = jnp.exp(scores - top)
    prob = expo / lax.optimization_barrier(jnp.sum(expo, axis=-1, keepdims=True))
    prob_b = prob.astype(jnp.bfloat16)
    outputs = jnp.einsum('bhcr,brhd->bchd', prob_b.astype(jnp.float32), v_four).astype(jnp.bfloat16)
    dprob = jnp.einsum('bchd,brhd->bhcr', g_four, v_four)
    rowdot = lax.optimization_barrier(jnp.sum(prob * dprob, axis=-1, keepdims=True))
    dscore = (prob * (dprob - rowdot) * scale).astype(jnp.bfloat16).astype(jnp.float32)
    dquery = jnp.einsum('bhcr,brhd->bchd', dscore, k_four).astype(jnp.bfloat16)
    dkey = jnp.einsum('bhcr,bchd->brhd', dscore, q_four).astype(jnp.bfloat16).reshape(blocks, span, width)
    dvalue = jnp.einsum('bhcr,bchd->brhd', prob_b.astype(jnp.float32), g_four).astype(jnp.bfloat16).reshape(blocks, span, width)
    both = jnp.concatenate([dkey, dvalue], axis=-1)
    w_both = jnp.concatenate([w_key, w_value], axis=1)
    dstates = jnp.einsum('brf,ef->bre', both.astype(jnp.float32), w_both.astype(jnp.float32)).astype(jnp.bfloat16)
    return (outputs.reshape(blocks * length, width), dquery.reshape(blocks * length, width), both, dstates)

def reference(queries, cotangent, w_key, w_value, database, nb_shard, nb_row):
    width = HEADS * HSIZE
    total = DB_DEV * N_DB
    seq_count = queries.shape[0]
    length = queries.shape[1]
    stretch_count = length // STRETCH
    padding = jnp.zeros((seq_count, STRETCH - 1, width), queries.dtype)
    q_shift = jnp.concatenate([queries[:, STRETCH - 1:], padding], axis=1).reshape(seq_count, stretch_count, STRETCH, width)
    g_shift = jnp.concatenate([cotangent[:, STRETCH - 1:], padding], axis=1).reshape(seq_count, stretch_count, STRETCH, width)
    flat_ids = (nb_shard * DB_DEV + nb_row).astype(jnp.int32).reshape(seq_count, stretch_count * NEIGH)
    catalog = jnp.arange(total, dtype=jnp.int32)

    def per_sequence(carry, inputs):
        weight_sum, db_sum = carry
        block_q, block_g, idx = inputs
        states = jnp.take(database, idx, axis=0).reshape(stretch_count, NEIGH * NB_LEN, ENC)
        outputs, dquery, both, dstates = attend_blocks(block_q, block_g, states, w_key, w_value)
        weight_sum = weight_sum + jnp.einsum('bre,brf->ef', states.astype(jnp.float32), both.astype(jnp.float32))
        member = (idx[None, :] == catalog[:, None]).astype(jnp.float32)
        share = jnp.einsum('dk,kle->dle', member, dstates.reshape(stretch_count * NEIGH, NB_LEN, ENC).astype(jnp.float32))
        share = lax.optimization_barrier(share.astype(jnp.bfloat16))
        db_sum = db_sum + share.astype(jnp.float32)
        return ((weight_sum, db_sum), (outputs, dquery))
    start = (jnp.zeros((ENC, 2 * width), jnp.float32), jnp.zeros((total, NB_LEN, ENC), jnp.float32))
    (weight_sum, db_sum), (outs, dqs) = lax.scan(per_sequence, start, (q_shift, g_shift, flat_ids))
    leading = jnp.zeros((seq_count, STRETCH - 1, width), jnp.bfloat16)
    attn_out = jnp.concatenate([leading, outs[:, :length - STRETCH + 1]], axis=1)
    grad_queries = jnp.concatenate([leading, dqs[:, :length - STRETCH + 1]], axis=1)
    return (attn_out, grad_queries, weight_sum[:, :width], weight_sum[:, width:], db_sum.astype(jnp.bfloat16))
```

```python
import functools
import math
from types import SimpleNamespace

import jax
import jax.numpy as jnp
import numpy as np
from jax import lax
from jax.experimental import pallas as pl
from jax.experimental.pallas import tpu as pltpu
from jax.sharding import PartitionSpec as P

HSIZE = 128
BF, F32 = jnp.bfloat16, jnp.float32
MESH = pl.DeviceIdType.MESH


def dot(a, b, dims):
    return lax.dot_general(a, b, (dims, ((), ())), preferred_element_type=F32)


def choose(level, wanted, a, b):
    same = jnp.full(a.shape, level, jnp.int32) == wanted
    return jnp.where(same, a.astype(F32), b.astype(F32)).astype(BF)


def add(a, b):
    return (a.astype(F32) + b.astype(F32)).astype(BF)


def attend(r, u, states, group):
    width = r.qblk.shape[1]
    window = r.qblk.shape[0]
    span = states.shape[0]
    scale = 1.0 / math.sqrt(HSIZE)
    rows = pl.ds(pl.multiple_of(u * span, span), span)
    for first in range(0, width // HSIZE, group):
        many = slice(first * HSIZE, (first + group) * HSIZE)
        vmany = slice(width + first * HSIZE, width + (first + group) * HSIZE)
        keys = dot(states, r.wts[:, many], ((1,), (0,))).astype(BF)
        values = dot(states, r.wts[:, vmany], ((1,), (0,))).astype(BF)
        heads = range(group)
        local = [slice(h * HSIZE, (h + 1) * HSIZE) for h in heads]
        cols = [slice((first + h) * HSIZE, (first + h + 1) * HSIZE) for h in heads]
        vcols = [slice(width + (first + h) * HSIZE, width + (first + h + 1) * HSIZE) for h in heads]
        q = [r.qblk[:, cols[h]] for h in heads]
        g = [r.gblk[:, cols[h]] for h in heads]
        k = [keys[:, local[h]] for h in heads]
        v = [values[:, local[h]] for h in heads]
        scores = [dot(q[h], k[h], ((1,), (1,))) * scale for h in heads]
        dprob = [dot(g[h], v[h], ((1,), (1,))) for h in heads]
        expo = [jnp.exp(t - jnp.max(t, axis=-1, keepdims=True)) for t in scores]
        prob = [t * (1.0 / jnp.sum(t, axis=-1, keepdims=True)) for t in expo]
        rowdot = [jnp.sum(prob[h] * dprob[h], axis=-1, keepdims=True) for h in heads]
        dscore = [(prob[h] * (dprob[h] - rowdot[h]) * scale).astype(BF) for h in heads]
        prob_b = [t.astype(BF) for t in prob]
        for h in heads:
            r.owin[u + 1, :, cols[h]] = dot(prob_b[h], v[h], ((1,), (0,))).astype(BF)
            r.dwin[u + 1, :, cols[h]] = dot(dscore[h], k[h], ((1,), (0,))).astype(BF)
        for h in heads:
            r.both[rows, cols[h]] = dot(dscore[h], q[h], ((0,), (0,))).astype(BF)
            r.both[rows, vcols[h]] = dot(prob_b[h], g[h], ((0,), (0,))).astype(BF)
    last = lax.broadcasted_iota(jnp.int32, (16, width), 0) == 15
    for win in (r.owin, r.dwin):
        tail = slice(window - 16, window)
        win[u, tail, :] = jnp.where(
            last, win[u + 1, tail, :].astype(F32), win[u, tail, :].astype(F32)
        ).astype(BF)


def kernel(plan, *refs):
    r = SimpleNamespace(**dict(zip(plan["names"], refs)))
    fused, asks, neigh, slots = plan["fused"], plan["asks"], plan["neigh"], plan["slots"]
    piece = plan["piece"]
    count = asks // neigh
    dp, db = lax.axis_index("dp"), lax.axis_index("db")
    shards = r.recv0.shape[0]
    nb_len = r.recv0.shape[1]
    base = r.dbv.shape[0]
    enc, wide = r.wts.shape
    half = wide // 2
    span = neigh * nb_len
    window = r.qblk.shape[0]
    recvs = [r.recv0, r.recv1, r.recv2]

    c, x = lax.rem(db, 2), db // 2
    core, far = db + 1 - 2 * c, db + 2 - 4 * x
    cross = far + 1 - 2 * c
    near = [(dp, far), (dp, cross), (dp, core)]
    after, before = (dp, lax.rem(db + 1, shards)), (dp, lax.rem(db + shards - 1, shards))
    seqs = lax.axis_size("dp")
    others = [(lax.rem(dp + d, seqs), db) for d in range(1, seqs)] if fused else []

    loads = [
        pltpu.make_async_copy(r.db_any, r.dbv, r.load_sem.at[0]),
        pltpu.make_async_copy(r.q_any, r.qwin.at[0:count], r.load_sem.at[1]),
        pltpu.make_async_copy(r.g_any, r.gwin.at[0:count], r.load_sem.at[2]),
        pltpu.make_async_copy(r.wk_any, r.wts.at[:, 0:half], r.load_sem.at[3]),
        pltpu.make_async_copy(r.wv_any, r.wts.at[:, half:wide], r.load_sem.at[4]),
        pltpu.make_async_copy(r.shuffle_any, r.shuffle, r.load_sem.at[5]),
    ]
    for load in loads:
        load.start()
    barrier = pltpu.get_barrier_semaphore()
    for peer in near + others:
        pl.semaphore_signal(barrier, inc=1, device_id=peer, device_id_type=MESH)

    target = [r.shard_ref[a] for a in range(asks)]
    wanted = [r.row_ref[a] for a in range(asks)]
    rank = []
    for a in range(asks):
        seen = jnp.int32(0)
        for b in range(a):
            seen = seen + (target[b] == target[a]).astype(jnp.int32)
        rank.append(seen)
        r.rank_sm[a] = seen
    row = lax.broadcasted_iota(jnp.int32, (8, 128), 0)
    lane = lax.broadcasted_iota(jnp.int32, (8, 128), 1)
    mine = jnp.zeros((8, 128), jnp.int32)
    for a in range(asks):
        mine = jnp.where((row == target[a]) & (lane == rank[a]), wanted[a], mine)
    r.asksend[...] = mine
    r.askbox[db] = mine

    def remote(src, dst, send_sem, recv_sem, peer):
        return pltpu.make_async_remote_copy(
            src_ref=src,
            dst_ref=dst,
            send_sem=send_sem,
            recv_sem=recv_sem,
            device_id=peer,
            device_id_type=MESH,
        )

    asked = [
        remote(r.asksend, r.askbox.at[db], r.ask_send.at[d], r.ask_recv.at[d], near[d])
        for d in range(3)
    ]
    edges = [
        remote(src.at[0], dst.at[count], r.edge_send.at[e], r.edge_recv.at[e], before)
        for e, (src, dst) in enumerate(((r.q_any, r.qwin), (r.g_any, r.gwin)))
    ]
    pl.semaphore_wait(barrier, len(near) + len(others))
    for copy in asked + edges:
        copy.start()

    if fused:
        own = jnp.zeros((8, 128), jnp.int32)
        for a in range(asks):
            own = jnp.where(lane // piece == a, target[a] * base + wanted[a], own)
        r.ids[...] = own
        r.idbox[dp] = own
        named = [
            remote(r.ids, r.idbox.at[dp], r.id_send.at[d], r.id_recv.at[d], peer)
            for d, peer in enumerate(others)
        ]
        for copy in named:
            copy.start()

    for copy in asked:
        copy.wait_recv()
    to_scalar = pltpu.make_async_copy(r.askbox, r.ask_sm, r.load_sem.at[6])
    to_scalar.start()
    to_scalar.wait()
    loads[0].wait()
    rounds = []

    def entry(asker, k):
        return r.dbv[r.ask_sm[asker, db, k]]

    for k in range(slots):
        for d, peer in enumerate(near):
            r.fetch[k * 3 + d] = entry(peer[1], k)
        recvs[k][db] = entry(db, k)
        rounds.append(
            [
                remote(
                    r.fetch.at[k * 3 + d],
                    recvs[k].at[db],
                    r.fetch_send.at[k * 3 + d],
                    r.fetch_recv.at[k * 3 + d],
                    near[d],
                )
                for d in range(3)
            ]
        )
        if k == 0:
            for copy in rounds[0]:
                copy.start()
    for win in (r.owin, r.dwin):
        win[0, window - 16 : window, :] = jnp.zeros((16, half), BF)
    for load in loads[1:]:
        load.wait()

    cuts = plan["cuts"]

    def across(u, h, d):
        start = pl.multiple_of(u * neigh * piece, neigh * piece)
        rows = pl.ds(start, neigh * piece)
        return remote(
            r.dbv.at[others[d][0], rows, cuts[h]],
            r.arrived.at[dp, rows, cuts[h]],
            r.across_send.at[u, h * len(others) + d],
            r.across_recv.at[u, h * len(others) + d],
            others[d],
        )

    last = lax.broadcasted_iota(jnp.int32, (16, half), 0) == 15

    @pl.loop(0, count)
    def _(u):
        for k in range(slots):

            @pl.when(u == k)
            def _():
                for copy in rounds[k]:
                    copy.wait_recv()
                if k + 1 < slots:
                    for copy in rounds[k + 1]:
                        copy.start()
                for n in range(neigh):
                    a = u * neigh + n
                    t, level = r.shard_ref[a], r.rank_sm[a]
                    block = recvs[k][t]
                    for j in range(k):
                        block = choose(level, j, recvs[j][t], block)
                    r.states[n * nb_len : (n + 1) * nb_len] = block

        @pl.when(u >= slots)
        def _():
            for n in range(neigh):
                a = u * neigh + n
                t, level = r.shard_ref[a], r.rank_sm[a]
                block = recvs[slots - 1][t]
                for j in range(slots - 1):
                    block = choose(level, j, recvs[j][t], block)
                r.states[n * nb_len : (n + 1) * nb_len] = block

        @pl.when(u == count - 1)
        def _():
            for copy in edges:
                copy.wait_recv()

        real = (u < count - 1) | (db < shards - 1)
        for win, blk in ((r.qwin, r.qblk), (r.gwin, r.gblk)):
            keep = jnp.where(real, 1.0, 0.0)
            blk[0 : window - 16] = (win[u + 1, 0 : window - 16].astype(F32) * keep).astype(BF)
            tail = slice(window - 16, window)
            blk[tail] = jnp.where(
                last, win[u, tail].astype(F32), win[u + 1, tail].astype(F32) * keep
            ).astype(BF)

        states = r.states[...]
        r.lt[:, pl.ds(pl.multiple_of(u * span, span), span)] = dot(
            r.shuffle[...], states, ((0,), (1,))
        ).astype(BF)
        attend(r, u, states, 4)

        if fused:
            rows = pl.ds(pl.multiple_of(u * span, span), span)
            for h, cols in enumerate(cuts):
                out = dot(r.both[rows], r.wts[cols], ((1,), (1,))).astype(BF)
                for n in range(neigh):
                    for j in range(seqs):
                        into = pl.ds(pl.multiple_of((u * neigh + n) * piece, piece), piece)
                        start = n * nb_len + j * piece
                        r.dbv[j, into, cols] = out[start : start + piece]
                part = pl.ds(pl.multiple_of(u * neigh * piece, neigh * piece), neigh * piece)
                r.arrived[dp, part, cols] = r.dbv[dp, part, cols]
                for d in range(len(others)):
                    across(u, h, d).start()

    passed = [
        remote(win.at[count], got, r.edge_send.at[2 + e], r.edge_recv.at[2 + e], after)
        for e, (win, got) in enumerate(((r.owin, r.oprev), (r.dwin, r.dprev)))
    ]
    for copy in passed:
        copy.start()

    def edge_outputs():
        writes = []
        for e, (win, got, out) in enumerate(
            ((r.owin, r.oprev, r.out_any), (r.dwin, r.dprev, r.dq_any))
        ):
            passed[e].wait_recv()
            keep = jnp.where(db > 0, 1.0, 0.0)
            win[0, 0 : window - 16] = (got[0 : window - 16].astype(F32) * keep).astype(BF)
            tail = slice(window - 16, window)
            win[0, tail] = jnp.where(
                last, win[0, tail].astype(F32), got[tail].astype(F32) * keep
            ).astype(BF)
            writes.append(pltpu.make_async_copy(win.at[0:count], out, r.load_sem.at[7 + e]))
            writes[-1].start()
        return writes

    sent = asked + edges + passed + [copy for part in rounds for copy in part]
    if fused:
        finish(r, plan, remote, across, others, named, edge_outputs, sent)
        return
    writes = edge_outputs()
    for n, (src, dst) in enumerate(((r.both, r.both_any), (r.lt, r.lt_any))):
        writes.append(pltpu.make_async_copy(src, dst, r.load_sem.at[9 + n]))
        writes[-1].start()
    for copy in writes:
        copy.wait()
    for copy in sent:
        copy.wait_send()


def finish(r, plan, remote, across, others, named, edge_outputs, sent):
    piece = plan["piece"]
    cuts = plan["cuts"]
    dp, db = lax.axis_index("dp"), lax.axis_index("db")
    seqs = r.arrived.shape[0]
    enc, wide = r.wts.shape
    half = wide // 2
    quarter = enc // 8
    c, x = lax.rem(db, 2), db // 2
    y, z0, z1 = lax.rem(dp, 2), lax.rem(dp // 2, 2), dp // 4
    pc = (dp, db + 1 - 2 * c)
    px = (dp, db + 2 - 4 * x)
    py = (dp + 1 - 2 * y, db)
    pz0 = (dp + 2 - 4 * z0, db)
    pz1 = (dp + 4 - 8 * z1, db)
    copies = []
    tile = 512

    def send(src, dst, peer):
        number = len(copies)
        copy = remote(src, dst, r.send_sem.at[number], r.recv_sem.at[number], peer)
        copy.start()
        copies.append(copy)
        return copy

    def part(p, row, n=1):
        rows = pl.ds(pl.multiple_of(row * quarter, quarter), n * quarter)
        return r.both.at[rows, p * half : (p + 1) * half]

    def weight_grad(p):
        @pl.loop(0, half // tile)
        def _(t):
            cols = pl.ds(pl.multiple_of(p * half + t * tile, tile), tile)
            out = jnp.dot(r.lt[...], r.both[:, cols], preferred_element_type=F32)
            r.both[0:enc, cols] = out.astype(BF)

        return send(part(p, (1 - c) * 4, 4), r.got1.at[p], pc)

    def after_core(p, copy):
        copy.wait_recv()
        for i in range(4):
            here = part(p, c * 4 + i)
            here[...] = add(here[...], r.got1[p, i * quarter : (i + 1) * quarter])

    key1 = weight_grad(0)
    value1 = weight_grad(1)
    after_core(0, key1)
    key2 = send(part(0, c * 4 + (1 - x) * 2, 2), r.got2.at[0], px)
    after_core(1, value1)
    value2 = [
        send(
            part(1, c * 4 + i * 2 + 1 - y),
            r.got2.at[1, i * quarter : (i + 1) * quarter],
            py,
        )
        for i in range(2)
    ]
    writes = edge_outputs()

    block = r.gd_ref.shape[0]
    lanes = r.member.shape[1] // seqs
    for copy in named:
        copy.wait_recv()
    row = lax.broadcasted_iota(jnp.int32, (block, lanes), 0)
    lane = lax.broadcasted_iota(jnp.int32, (block, lanes), 1)
    place = jnp.where(row % piece == lane % piece, row // piece, -1)
    for i in range(r.member.shape[0] // block):
        for k in range(seqs):
            hit = place == r.idbox[k][0:1] - i * (block // piece)
            r.member[i * block : (i + 1) * block, k * lanes : (k + 1) * lanes] = jnp.where(
                hit & (place >= 0), 1.0, 0.0
            ).astype(BF)

    def expand(p, total):
        r.zed[p] = (
            jnp.dot(r.spread_ref[...], total, preferred_element_type=F32)
            .astype(BF)
            .reshape(r.zed.shape[1:])
        )
        return send(r.zed.at[p, 1 - z0], r.got4.at[p], pz0)

    def join(p, row, got):
        here = part(p, row)
        here[...] = add(here[...], got)

    key2.wait_recv()
    for j in range(2):
        join(0, c * 4 + x * 2 + j, r.got2[0, j * quarter : (j + 1) * quarter])
    key3 = send(part(0, c * 4 + x * 2 + 1 - y), r.got3.at[0], py)
    for i in range(2):
        value2[i].wait_recv()
        join(1, c * 4 + i * 2 + y, r.got2[1, i * quarter : (i + 1) * quarter])
    value3 = send(part(1, c * 4 + (1 - x) * 2 + y), r.got3.at[1], px)
    key3.wait_recv()
    key4 = expand(0, add(part(0, c * 4 + x * 2 + y)[...], r.got3[0]))
    value3.wait_recv()
    value4 = expand(1, add(part(1, c * 4 + x * 2 + y)[...], r.got3[1]))

    every = r.arrived.shape[0] * r.arrived.shape[1]
    count = r.across_send.shape[0]

    def dense(shard, cols):
        return jnp.dot(
            r.member[pl.ds(pl.multiple_of(shard * block, block), block)],
            r.arrived[:, :, cols].reshape(every, cols.stop - cols.start),
            preferred_element_type=F32,
        ).reshape(many, nb_len, cols.stop - cols.start)

    many, nb_len = r.dgot2.shape[0:2]
    give = [slice(seqs + n * many, seqs + (n + 1) * many) for n in range(3)]

    def core_start(h):
        cols = cuts[h]
        for u in range(count):
            for d in range(len(others)):
                across(u, h, d).wait_recv()
        started = []
        for far in (1, 0):
            side = x if far == 0 else 1 - x
            r.dbv[give[far], :, cols] = dense(2 * side + 1 - c, cols).astype(BF)
            started.append(send(r.dbv.at[give[far], :, cols], r.dgot1.at[far, :, :, cols], pc))
        for far in (1, 0):
            side = x if far == 0 else 1 - x
            r.mine[far, :, :, cols] = dense(2 * side + c, cols)
        return started

    def x_start(h, started):
        cols = cuts[h]
        started[0].wait_recv()
        summed = r.mine[1, :, :, cols] + r.dgot1[1, :, :, cols].astype(F32)
        r.dbv[give[2], :, cols] = summed.astype(BF)
        copy = send(r.dbv.at[give[2], :, cols], r.dgot2.at[:, :, cols], px)
        started[1].wait_recv()
        r.mine[0, :, :, cols] = r.mine[0, :, :, cols] + r.dgot1[0, :, :, cols].astype(F32)
        return copy

    def final(p, copy):
        copy.wait_recv()
        for j in range(2):
            r.zed[p, z0, j] = add(r.zed[p, z0, j], r.got4[p, j])
        return send(r.zed.at[p, z0, 1 - z1], r.got5.at[p], pz1)

    xcopy = [x_start(0, core_start(0))]
    key5 = final(0, key4)
    value5 = final(1, value4)
    for h in range(1, len(cuts)):
        xcopy.append(x_start(h, core_start(h)))
    for p, copy, out_ref in ((0, key5, r.gk_ref), (1, value5, r.gv_ref)):
        copy.wait_recv()
        summed = r.zed[p, z0, z1].astype(F32) + r.got5[p].astype(F32)
        out_ref[...] = summed[: out_ref.shape[0]]
    for h, cols in enumerate(cuts):
        xcopy[h].wait_recv()
        summed = r.mine[0, :, :, cols] + r.dgot2[:, :, cols].astype(F32)
        r.gd_ref[:, cols] = summed.astype(BF).reshape(block, cols.stop - cols.start)
    for copy in copies + named + sent:
        copy.wait_send()
    for u in range(count):
        for h in range(len(cuts)):
            for d in range(len(others)):
                across(u, h, d).wait_send()
    for copy in writes:
        copy.wait()


def reversed_order(count):
    bits = count.bit_length() - 1
    return np.array([int(format(i, "b").zfill(bits)[::-1], 2) if bits else 0 for i in range(count)])


def run(queries, cotangent, w_key, w_value, database, nb_shard, nb_row):
    shards, seqs = lax.axis_size("db"), lax.axis_size("dp")
    _, rows, width = queries.shape
    _, count, neigh = nb_shard.shape
    base, nb_len, enc = database.shape
    window = rows // count
    asks = count * neigh
    slots = 3 * asks // (2 * shards)
    fused = shards == 4 and seqs == 8
    devices = shards * seqs
    share = enc // devices
    piece = nb_len // seqs
    wide = 2 * width
    quarter = enc // 8
    padded = -(-share // 16) * 16
    block = base * piece
    source = (reversed_order(devices)[:, None] * share + np.arange(share)[None, :]).reshape(-1)
    shuffle = (np.arange(enc)[:, None] == source[None, :]).astype(jnp.bfloat16)
    cuts = [slice(0, 512), slice(512, enc)]

    anywhere = pl.BlockSpec(memory_space=pl.ANY)
    vmem = pl.BlockSpec(memory_space=pltpu.VMEM)
    smem = pl.BlockSpec(memory_space=pltpu.SMEM)
    sem = pltpu.SemaphoreType.DMA
    names, inputs, specs = [], [], []

    def give(name, value, spec):
        names.append(name)
        inputs.append(value)
        specs.append(spec)

    give("shard_ref", nb_shard.reshape(asks), smem)
    give("row_ref", nb_row.reshape(asks), smem)
    give("q_any", queries.reshape(count, window, width), anywhere)
    give("g_any", cotangent.reshape(count, window, width), anywhere)
    give("wk_any", w_key, anywhere)
    give("wv_any", w_value, anywhere)
    give("db_any", database, anywhere)
    give("shuffle_any", jnp.asarray(shuffle), anywhere)
    if fused:
        row = np.arange(4 * padded)[:, None]
        col = np.arange(4 * share)[None, :]
        spread = (row // padded == col // share) & (row % padded == col % share)
        give("spread_ref", jnp.asarray(spread.astype(jnp.bfloat16)), vmem)

    outs = [
        ("out_any", (count, window, width), BF, anywhere),
        ("dq_any", (count, window, width), BF, anywhere),
    ]
    if fused:
        outs += [
            ("gk_ref", (share, width), F32, vmem),
            ("gv_ref", (share, width), F32, vmem),
            ("gd_ref", (block, enc), BF, vmem),
        ]
    else:
        outs += [
            ("both_any", (asks * nb_len, wide), BF, anywhere),
            ("lt_any", (enc, asks * nb_len), BF, anywhere),
        ]
    scratch = [
        ("dbv", pltpu.VMEM((base, nb_len, enc), BF)),
        ("qwin", pltpu.VMEM((count + 1, window, width), BF)),
        ("gwin", pltpu.VMEM((count + 1, window, width), BF)),
        ("owin", pltpu.VMEM((count + 1, window, width), BF)),
        ("dwin", pltpu.VMEM((count + 1, window, width), BF)),
        ("oprev", pltpu.VMEM((window, width), BF)),
        ("dprev", pltpu.VMEM((window, width), BF)),
        ("qblk", pltpu.VMEM((window, width), BF)),
        ("gblk", pltpu.VMEM((window, width), BF)),
        ("wts", pltpu.VMEM((enc, wide), BF)),
        ("shuffle", pltpu.VMEM((enc, enc), BF)),
        ("states", pltpu.VMEM((neigh * nb_len, enc), BF)),
        ("both", pltpu.VMEM((asks * nb_len, wide), BF)),
        ("lt", pltpu.VMEM((enc, asks * nb_len), BF)),
        ("fetch", pltpu.VMEM((slots * 3, nb_len, enc), BF)),
        ("recv0", pltpu.VMEM((shards, nb_len, enc), BF)),
        ("recv1", pltpu.VMEM((shards, nb_len, enc), BF)),
        ("recv2", pltpu.VMEM((shards, nb_len, enc), BF)),
        ("asksend", pltpu.VMEM((8, 128), jnp.int32)),
        ("askbox", pltpu.VMEM((shards, 8, 128), jnp.int32)),
        ("ask_sm", pltpu.SMEM((shards, 8, 128), jnp.int32)),
        ("rank_sm", pltpu.SMEM((asks,), jnp.int32)),
        ("load_sem", sem((12,))),
        ("ask_send", sem((3,))),
        ("ask_recv", sem((3,))),
        ("edge_send", sem((4,))),
        ("edge_recv", sem((4,))),
        ("fetch_send", sem((slots * 3,))),
        ("fetch_recv", sem((slots * 3,))),
    ]
    if fused:
        peers = seqs - 1
        scratch += [
            ("ids", pltpu.VMEM((8, 128), jnp.int32)),
            ("idbox", pltpu.VMEM((seqs, 8, 128), jnp.int32)),
            ("member", pltpu.VMEM((shards * block, seqs * asks * piece), BF)),
            ("got1", pltpu.VMEM((2, 4 * quarter, width), BF)),
            ("got2", pltpu.VMEM((2, 2 * quarter, width), BF)),
            ("got3", pltpu.VMEM((2, quarter, width), BF)),
            ("zed", pltpu.VMEM((2, 2, 2, padded, width), BF)),
            ("got4", pltpu.VMEM((2, 2, padded, width), BF)),
            ("got5", pltpu.VMEM((2, padded, width), BF)),
            ("arrived", pltpu.VMEM((seqs, asks * piece, enc), BF)),
            ("dgot1", pltpu.VMEM((2, block // nb_len, nb_len, enc), BF)),
            ("mine", pltpu.VMEM((2, block // nb_len, nb_len, enc), F32)),
            ("dgot2", pltpu.VMEM((block // nb_len, nb_len, enc), BF)),
            ("send_sem", sem((24,))),
            ("recv_sem", sem((24,))),
            ("across_send", sem((count, len(cuts) * peers))),
            ("across_recv", sem((count, len(cuts) * peers))),
            ("id_send", sem((peers,))),
            ("id_recv", sem((peers,))),
        ]
    names += [o[0] for o in outs] + [s[0] for s in scratch]
    plan = dict(
        names=names, fused=fused, asks=asks, neigh=neigh, slots=slots, piece=piece, cuts=cuts
    )
    results = pl.pallas_call(
        functools.partial(kernel, plan),
        in_specs=specs,
        out_specs=[o[3] for o in outs],
        out_shape=[jax.ShapeDtypeStruct(o[1], o[2]) for o in outs],
        scratch_shapes=[s[1] for s in scratch],
        compiler_params=pltpu.CompilerParams(
            vmem_limit_bytes=62 << 20, collective_id=0, has_side_effects=True
        ),
        cost_estimate=pl.CostEstimate(
            flops=28 * 10**9, bytes_accessed=40 << 20, transcendentals=1 << 20
        ),
    )(*inputs)
    attn_out = results[0].reshape(1, rows, width)
    grad_queries = results[1].reshape(1, rows, width)
    if fused:
        grad_database = results[4].reshape(base, piece, enc)
        return (attn_out, grad_queries, results[2], results[3], grad_database)

    both, lt = results[2:]
    own_ids = (nb_shard * base + nb_row).reshape(asks)
    ids = jnp.broadcast_to(own_ids[None], (seqs, asks))
    ids = lax.all_to_all(ids, "dp", split_axis=0, concat_axis=0, tiled=True)
    ids = ids.reshape(seqs * asks)
    member = (ids[None, :] == jnp.arange(shards * base, dtype=jnp.int32)[:, None]).astype(BF)
    steps = [("db", b) for b in bits_of("db")] + [("dp", b) for b in bits_of("dp")]
    grads = []
    for part in range(2):
        grad = dot(lt, both[:, part * width : (part + 1) * width], ((1,), (0,)))
        grads.append(halve_all(grad.astype(BF), steps))
    w_both = jnp.concatenate([w_key, w_value], axis=1)
    dstates = dot(both, w_both, ((1,), (1,))).astype(BF)
    dstates = dstates.reshape(asks, seqs, piece, enc).transpose(1, 0, 2, 3)
    arrived = lax.all_to_all(dstates, "dp", split_axis=0, concat_axis=0, tiled=True)
    dense = dot(member, arrived.reshape(seqs * asks, piece * enc), ((1,), (0,)))
    dense = dense.astype(BF).reshape(shards, base, piece, enc)
    dense = jnp.stack([dense[i] for i in reversed_order(shards)])
    grad_database = halve_all(dense, [("db", b) for b in bits_of("db")])[0].astype(BF)
    return (attn_out, grad_queries, grads[0], grads[1], grad_database)


def halve(block, axis, bit):
    size = lax.axis_size(axis)
    half = block.shape[0] // 2
    side = lax.rem(lax.axis_index(axis) // bit, 2)
    give = lax.dynamic_slice_in_dim(block, (1 - side) * half, half, 0)
    mine = lax.dynamic_slice_in_dim(block, side * half, half, 0)
    got = lax.ppermute(give, axis, [(i, i ^ bit) for i in range(size)])
    return mine.astype(F32) + got.astype(F32)


def bits_of(axis):
    size = lax.axis_size(axis)
    return [1 << b for b in range(size.bit_length() - 1)]


def halve_all(block, steps):
    for axis, bit in steps[:-1]:
        block = halve(block, axis, bit).astype(BF)
    return halve(block, *steps[-1])


def solution(mesh):
    return jax.shard_map(
        run,
        mesh=mesh,
        in_specs=(
            P("dp", "db", None),
            P("dp", "db", None),
            P(),
            P(),
            P("db", None, None),
            P("dp", "db", None),
            P("dp", "db", None),
        ),
        out_specs=(
            P("dp", "db", None),
            P("dp", "db", None),
            P(("dp", "db"), None),
            P(("dp", "db"), None),
            P("db", "dp", None),
        ),
        check_vma=False,
    )
```

```python
import functools
import math
from types import SimpleNamespace

import jax
import jax.numpy as jnp
import numpy as np
from jax import lax
from jax.experimental import pallas as pl
from jax.experimental.pallas import tpu as pltpu
from jax.sharding import PartitionSpec as P

HSIZE = 128
BF, F32 = jnp.bfloat16, jnp.float32
MESH = pl.DeviceIdType.MESH


def dot(a, b, dims):
    return lax.dot_general(a, b, (dims, ((), ())), preferred_element_type=F32)


def choose(level, wanted, a, b):
    same = jnp.full(a.shape, level, jnp.int32) == wanted
    return jnp.where(same, a.astype(F32), b.astype(F32)).astype(BF)


def add(a, b):
    return (a.astype(F32) + b.astype(F32)).astype(BF)


def attend(r, u, states, group):
    width = r.qblk.shape[1]
    window = r.qblk.shape[0]
    span = states.shape[0]
    scale = 1.0 / math.sqrt(HSIZE)
    rows = pl.ds(pl.multiple_of(u * span, span), span)
    for first in range(0, width // HSIZE, group):
        many = slice(first * HSIZE, (first + group) * HSIZE)
        vmany = slice(width + first * HSIZE, width + (first + group) * HSIZE)
        keys = dot(states, r.wts[:, many], ((1,), (0,))).astype(BF)
        values = dot(states, r.wts[:, vmany], ((1,), (0,))).astype(BF)
        heads = range(group)
        local = [slice(h * HSIZE, (h + 1) * HSIZE) for h in heads]
        cols = [slice((first + h) * HSIZE, (first + h + 1) * HSIZE) for h in heads]
        vcols = [slice(width + (first + h) * HSIZE, width + (first + h + 1) * HSIZE) for h in heads]
        q = [r.qblk[:, cols[h]] for h in heads]
        g = [r.gblk[:, cols[h]] for h in heads]
        k = [keys[:, local[h]] for h in heads]
        v = [values[:, local[h]] for h in heads]
        scores = [dot(q[h], k[h], ((1,), (1,))) * scale for h in heads]
        dprob = [dot(g[h], v[h], ((1,), (1,))) for h in heads]
        expo = [jnp.exp(t - jnp.max(t, axis=-1, keepdims=True)) for t in scores]
        prob = [t * (1.0 / jnp.sum(t, axis=-1, keepdims=True)) for t in expo]
        rowdot = [jnp.sum(prob[h] * dprob[h], axis=-1, keepdims=True) for h in heads]
        dscore = [(prob[h] * (dprob[h] - rowdot[h]) * scale).astype(BF) for h in heads]
        prob_b = [t.astype(BF) for t in prob]
        for h in heads:
            r.owin[u + 1, :, cols[h]] = dot(prob_b[h], v[h], ((1,), (0,))).astype(BF)
            r.dwin[u + 1, :, cols[h]] = dot(dscore[h], k[h], ((1,), (0,))).astype(BF)
        for h in heads:
            r.both[rows, cols[h]] = dot(dscore[h], q[h], ((0,), (0,))).astype(BF)
            r.both[rows, vcols[h]] = dot(prob_b[h], g[h], ((0,), (0,))).astype(BF)
    last = lax.broadcasted_iota(jnp.int32, (16, width), 0) == 15
    for win in (r.owin, r.dwin):
        tail = slice(window - 16, window)
        win[u, tail, :] = jnp.where(
            last, win[u + 1, tail, :].astype(F32), win[u, tail, :].astype(F32)
        ).astype(BF)


def kernel(plan, *refs):
    r = SimpleNamespace(**dict(zip(plan["names"], refs)))
    fused, asks, neigh, slots = plan["fused"], plan["asks"], plan["neigh"], plan["slots"]
    piece = plan["piece"]
    count = asks // neigh
    dp, db = lax.axis_index("dp"), lax.axis_index("db")
    shards = r.recv0.shape[0]
    nb_len = r.recv0.shape[1]
    base = r.dbv.shape[0]
    enc, wide = r.wts.shape
    half = wide // 2
    span = neigh * nb_len
    window = r.qblk.shape[0]
    recvs = [r.recv0, r.recv1, r.recv2]

    c, x = lax.rem(db, 2), db // 2
    core, far = db + 1 - 2 * c, db + 2 - 4 * x
    cross = far + 1 - 2 * c
    near = [(dp, far), (dp, cross), (dp, core)]
    after, before = (dp, lax.rem(db + 1, shards)), (dp, lax.rem(db + shards - 1, shards))
    seqs = lax.axis_size("dp")
    others = [(lax.rem(dp + d, seqs), db) for d in range(1, seqs)] if fused else []

    loads = [
        pltpu.make_async_copy(r.db_any, r.dbv, r.load_sem.at[0]),
        pltpu.make_async_copy(r.q_any, r.qwin.at[0:count], r.load_sem.at[1]),
        pltpu.make_async_copy(r.g_any, r.gwin.at[0:count], r.load_sem.at[2]),
        pltpu.make_async_copy(r.wk_any, r.wts.at[:, 0:half], r.load_sem.at[3]),
        pltpu.make_async_copy(r.wv_any, r.wts.at[:, half:wide], r.load_sem.at[4]),
        pltpu.make_async_copy(r.shuffle_any, r.shuffle, r.load_sem.at[5]),
    ]
    for load in loads:
        load.start()
    barrier = pltpu.get_barrier_semaphore()
    for peer in near + others:
        pl.semaphore_signal(barrier, inc=1, device_id=peer, device_id_type=MESH)

    target = [r.shard_ref[a % neigh, a // neigh] for a in range(asks)]
    wanted = [r.row_ref[a % neigh, a // neigh] for a in range(asks)]
    rank = []
    for a in range(asks):
        seen = jnp.int32(0)
        for b in range(a):
            seen = seen + (target[b] == target[a]).astype(jnp.int32)
        rank.append(seen)
        r.rank_sm[a] = seen
    row = lax.broadcasted_iota(jnp.int32, (8, 128), 0)
    lane = lax.broadcasted_iota(jnp.int32, (8, 128), 1)
    mine = jnp.zeros((8, 128), jnp.int32)
    for a in range(asks):
        mine = jnp.where((row == target[a]) & (lane == rank[a]), wanted[a], mine)
    r.asksend[...] = mine
    r.askbox[db] = mine

    def remote(src, dst, send_sem, recv_sem, peer):
        return pltpu.make_async_remote_copy(
            src_ref=src,
            dst_ref=dst,
            send_sem=send_sem,
            recv_sem=recv_sem,
            device_id=peer,
            device_id_type=MESH,
        )

    asked = [
        remote(r.asksend, r.askbox.at[db], r.ask_send.at[d], r.ask_recv.at[d], near[d])
        for d in range(3)
    ]
    edges = [
        remote(src.at[0], dst.at[count], r.edge_send.at[e], r.edge_recv.at[e], before)
        for e, (src, dst) in enumerate(((r.q_any, r.qwin), (r.g_any, r.gwin)))
    ]
    pl.semaphore_wait(barrier, len(near) + len(others))
    for copy in asked + edges:
        copy.start()

    if fused:
        own = jnp.zeros((8, 128), jnp.int32)
        for a in range(asks):
            own = jnp.where(lane // piece == a, target[a] * base + wanted[a], own)
        r.ids[...] = own
        r.idbox[dp] = own
        named = [
            remote(r.ids, r.idbox.at[dp], r.id_send.at[d], r.id_recv.at[d], peer)
            for d, peer in enumerate(others)
        ]
        for copy in named:
            copy.start()

    for copy in asked:
        copy.wait_recv()
    to_scalar = pltpu.make_async_copy(r.askbox, r.ask_sm, r.load_sem.at[6])
    to_scalar.start()
    to_scalar.wait()
    loads[0].wait()
    rounds = []

    def entry(asker, k):
        return r.dbv[r.ask_sm[asker, db, k]]

    for k in range(slots):
        for d, peer in enumerate(near):
            r.fetch[k * 3 + d] = entry(peer[1], k)
        recvs[k][db] = entry(db, k)
        rounds.append(
            [
                remote(
                    r.fetch.at[k * 3 + d],
                    recvs[k].at[db],
                    r.fetch_send.at[k * 3 + d],
                    r.fetch_recv.at[k * 3 + d],
                    near[d],
                )
                for d in range(3)
            ]
        )
        if k == 0:
            for copy in rounds[0]:
                copy.start()
    for win in (r.owin, r.dwin):
        win[0, window - 16 : window, :] = jnp.zeros((16, half), BF)
    if fused:
        block = r.gd_ref.shape[0]
        lanes = r.member.shape[1] // seqs
        for copy in named:
            copy.wait_recv()
        row = lax.broadcasted_iota(jnp.int32, (block, lanes), 0)
        lane = lax.broadcasted_iota(jnp.int32, (block, lanes), 1)
        place = jnp.where(row % piece == lane % piece, row // piece, -1)

        @pl.loop(0, shards)
        def _(i):
            rows = pl.ds(pl.multiple_of(i * block, block), block)
            for k in range(seqs):
                hit = place == r.idbox[k][0:1] - i * (block // piece)
                r.member[rows, k * lanes : (k + 1) * lanes] = jnp.where(
                    hit & (place >= 0), 1.0, 0.0
                ).astype(BF)

    for load in loads[1:]:
        load.wait()

    cuts = plan["cuts"]

    def across(u, h, d):
        start = pl.multiple_of(u * neigh * piece, neigh * piece)
        rows = pl.ds(start, neigh * piece)
        return remote(
            r.dbv.at[others[d][0], rows, cuts[h]],
            r.arrived.at[dp, rows, cuts[h]],
            r.across_send.at[u, h * len(others) + d],
            r.across_recv.at[u, h * len(others) + d],
            others[d],
        )

    last = lax.broadcasted_iota(jnp.int32, (16, half), 0) == 15

    @pl.loop(0, count)
    def _(u):
        for k in range(slots):

            @pl.when(u == k)
            def _():
                for copy in rounds[k]:
                    copy.wait_recv()
                if k + 1 < slots:
                    for copy in rounds[k + 1]:
                        copy.start()
                for n in range(neigh):
                    a = u * neigh + n
                    t, level = r.shard_ref[n, u], r.rank_sm[a]
                    block = recvs[k][t]
                    for j in range(k):
                        block = choose(level, j, recvs[j][t], block)
                    r.states[n * nb_len : (n + 1) * nb_len] = block

        @pl.when(u >= slots)
        def _():
            for n in range(neigh):
                a = u * neigh + n
                t, level = r.shard_ref[n, u], r.rank_sm[a]
                block = recvs[slots - 1][t]
                for j in range(slots - 1):
                    block = choose(level, j, recvs[j][t], block)
                r.states[n * nb_len : (n + 1) * nb_len] = block

        @pl.when(u == count - 1)
        def _():
            for copy in edges:
                copy.wait_recv()

        real = (u < count - 1) | (db < shards - 1)
        for win, blk in ((r.qwin, r.qblk), (r.gwin, r.gblk)):
            keep = jnp.where(real, 1.0, 0.0)
            blk[0 : window - 16] = (win[u + 1, 0 : window - 16].astype(F32) * keep).astype(BF)
            tail = slice(window - 16, window)
            blk[tail] = jnp.where(
                last, win[u, tail].astype(F32), win[u + 1, tail].astype(F32) * keep
            ).astype(BF)

        states = r.states[...]
        r.lt[:, pl.ds(pl.multiple_of(u * span, span), span)] = dot(
            r.shuffle[...], states, ((0,), (1,))
        ).astype(BF)
        attend(r, u, states, 4)

        if fused:
            rows = pl.ds(pl.multiple_of(u * span, span), span)
            for h, cols in enumerate(cuts):
                out = dot(r.both[rows], r.wts[cols], ((1,), (1,))).astype(BF)
                for n in range(neigh):
                    for j in range(seqs):
                        into = pl.ds(pl.multiple_of((u * neigh + n) * piece, piece), piece)
                        start = n * nb_len + j * piece
                        r.dbv[j, into, cols] = out[start : start + piece]
                part = pl.ds(pl.multiple_of(u * neigh * piece, neigh * piece), neigh * piece)
                r.arrived[dp, part, cols] = r.dbv[dp, part, cols]
                for d in range(len(others)):
                    across(u, h, d).start()

    passed = [
        remote(win.at[count], got, r.edge_send.at[2 + e], r.edge_recv.at[2 + e], after)
        for e, (win, got) in enumerate(((r.owin, r.oprev), (r.dwin, r.dprev)))
    ]
    for copy in passed:
        copy.start()

    def edge_outputs():
        writes = []
        for e, (win, got, out) in enumerate(
            ((r.owin, r.oprev, r.out_any), (r.dwin, r.dprev, r.dq_any))
        ):
            passed[e].wait_recv()
            keep = jnp.where(db > 0, 1.0, 0.0)
            win[0, 0 : window - 16] = (got[0 : window - 16].astype(F32) * keep).astype(BF)
            tail = slice(window - 16, window)
            win[0, tail] = jnp.where(
                last, win[0, tail].astype(F32), got[tail].astype(F32) * keep
            ).astype(BF)
            writes.append(pltpu.make_async_copy(win.at[0:count], out, r.load_sem.at[7 + e]))
            writes[-1].start()
        return writes

    sent = asked + edges + passed + [copy for part in rounds for copy in part]
    if fused:
        finish(r, plan, remote, across, others, named, edge_outputs, sent)
        return
    writes = edge_outputs()
    for n, (src, dst) in enumerate(((r.both, r.both_any), (r.lt, r.lt_any))):
        writes.append(pltpu.make_async_copy(src, dst, r.load_sem.at[9 + n]))
        writes[-1].start()
    for copy in writes:
        copy.wait()
    for copy in sent:
        copy.wait_send()


def finish(r, plan, remote, across, others, named, edge_outputs, sent):
    piece = plan["piece"]
    cuts = plan["cuts"]
    dp, db = lax.axis_index("dp"), lax.axis_index("db")
    seqs = r.arrived.shape[0]
    enc, wide = r.wts.shape
    half = wide // 2
    quarter = enc // 8
    c, x = lax.rem(db, 2), db // 2
    y, z0, z1 = lax.rem(dp, 2), lax.rem(dp // 2, 2), dp // 4
    pc = (dp, db + 1 - 2 * c)
    px = (dp, db + 2 - 4 * x)
    py = (dp + 1 - 2 * y, db)
    pz0 = (dp + 2 - 4 * z0, db)
    pz1 = (dp + 4 - 8 * z1, db)
    copies = []
    tile = 512

    def send(src, dst, peer):
        number = len(copies)
        copy = remote(src, dst, r.send_sem.at[number], r.recv_sem.at[number], peer)
        copy.start()
        copies.append(copy)
        return copy

    chunks = plan["chunks"]
    thin = wide // chunks

    def part(p, row, n=1):
        rows = pl.ds(pl.multiple_of(row * quarter, quarter), n * quarter)
        return r.both.at[rows, p * thin : (p + 1) * thin]

    def weight_grad(p):
        @pl.loop(0, thin // tile)
        def _(t):
            cols = pl.ds(pl.multiple_of(p * thin + t * tile, tile), tile)
            out = jnp.dot(r.lt[...], r.both[:, cols], preferred_element_type=F32)
            r.both[0:enc, cols] = out.astype(BF)

        return send(part(p, (1 - c) * 4, 4), r.got1.at[p], pc)

    def join(p, row, got):
        here = part(p, row)
        here[...] = add(here[...], got)

    def first(p, copy):
        copy.wait_recv()
        for i in range(4):
            join(p, c * 4 + i, r.got1[p, i * quarter : (i + 1) * quarter])
        if p % 2 == 0:
            return [send(part(p, c * 4 + (1 - y) * 2, 2), r.got2.at[p], py)]
        return [
            send(
                part(p, c * 4 + i * 2 + 1 - z0),
                r.got2.at[p, i * quarter : (i + 1) * quarter],
                pz0,
            )
            for i in range(2)
        ]

    def second(p, arrivals):
        for copy in arrivals:
            copy.wait_recv()
        for i in range(2):
            into = c * 4 + y * 2 + i if p % 2 == 0 else c * 4 + i * 2 + z0
            join(p, into, r.got2[p, i * quarter : (i + 1) * quarter])
        if p % 2 == 0:
            return send(part(p, c * 4 + y * 2 + 1 - z0), r.got3.at[p], pz0)
        return send(part(p, c * 4 + (1 - y) * 2 + z0), r.got3.at[p], py)

    def third(p, copy):
        copy.wait_recv()
        total = add(part(p, c * 4 + y * 2 + z0)[...], r.got3[p])
        r.zed[p] = (
            jnp.dot(r.spread_ref[...], total, preferred_element_type=F32)
            .astype(BF)
            .reshape(r.zed.shape[1:])
        )
        return send(r.zed.at[p, 1 - x], r.got4.at[p], px)

    def fourth(p, copy):
        copy.wait_recv()
        for j in range(2):
            r.zed[p, x, j] = add(r.zed[p, x, j], r.got4[p, j])
        return send(r.zed.at[p, x, 1 - z1], r.got5.at[p], pz1)

    def fifth(p, copy):
        copy.wait_recv()
        out_ref = r.gk_ref if p < chunks // 2 else r.gv_ref
        where = p % (chunks // 2) * thin
        summed = r.zed[p, x, z1].astype(F32) + r.got5[p].astype(F32)
        out_ref[:, where : where + thin] = summed[: out_ref.shape[0]]

    block = r.gd_ref.shape[0]
    every = r.arrived.shape[0] * r.arrived.shape[1]
    count = r.across_send.shape[0]

    def dense(shard, cols):
        return jnp.dot(
            r.member[pl.ds(pl.multiple_of(shard * block, block), block)],
            r.arrived[:, :, cols].reshape(every, cols.stop - cols.start),
            preferred_element_type=F32,
        ).reshape(many, nb_len, cols.stop - cols.start)

    many, nb_len = r.dgot2.shape[0:2]
    give = [slice(seqs + n * many, seqs + (n + 1) * many) for n in range(3)]

    def core_start(h):
        cols = cuts[h]
        for u in range(count):
            for d in range(len(others)):
                across(u, h, d).wait_recv()
        started = []
        for far in (1, 0):
            side = x if far == 0 else 1 - x
            r.dbv[give[far], :, cols] = dense(2 * side + 1 - c, cols).astype(BF)
            started.append(send(r.dbv.at[give[far], :, cols], r.dgot1.at[far, :, :, cols], pc))
        for far in (1, 0):
            side = x if far == 0 else 1 - x
            r.mine[far, :, :, cols] = dense(2 * side + c, cols)
        return started

    def x_start(h, started):
        cols = cuts[h]
        started[0].wait_recv()
        summed = r.mine[1, :, :, cols] + r.dgot1[1, :, :, cols].astype(F32)
        r.dbv[give[2], :, cols] = summed.astype(BF)
        copy = send(r.dbv.at[give[2], :, cols], r.dgot2.at[:, :, cols], px)
        started[1].wait_recv()
        r.mine[0, :, :, cols] = r.mine[0, :, :, cols] + r.dgot1[0, :, :, cols].astype(F32)
        return copy

    every_chunk = range(chunks)
    ones, ways = [], []
    for p in every_chunk:
        ones.append(weight_grad(p))
        if p > 0:
            ways.append(first(p - 1, ones[p - 1]))
    ways.append(first(chunks - 1, ones[-1]))
    writes = edge_outputs()
    cores = [core_start(h) for h in range(len(cuts))]
    xcopy = [x_start(h, cores[h]) for h in range(len(cuts))]
    ways = [second(p, ways[p]) for p in every_chunk]
    ways = [third(p, ways[p]) for p in every_chunk]
    ways = [fourth(p, ways[p]) for p in every_chunk]
    for h, cols in enumerate(cuts):
        xcopy[h].wait_recv()
        summed = r.mine[0, :, :, cols] + r.dgot2[:, :, cols].astype(F32)
        r.gd_ref[:, cols] = summed.astype(BF).reshape(block, cols.stop - cols.start)
    for p in every_chunk:
        fifth(p, ways[p])
    for copy in copies + named + sent:
        copy.wait_send()
    for u in range(count):
        for h in range(len(cuts)):
            for d in range(len(others)):
                across(u, h, d).wait_send()
    for copy in writes:
        copy.wait()


def settle_kernel(count, pieces, *refs):
    sources, targets, held = refs[:count], refs[count : 2 * count], refs[2 * count : 3 * count]
    in_sem, out_sem = refs[3 * count :]
    loads, stores = [], []
    for src, dst, mid in zip(sources, targets, held):
        size = src.shape[0]
        cut = pieces if len(src.shape) == 3 else 1
        step = size // cut
        for i in range(cut):
            rows = pl.ds(i * step, step)
            n = len(loads)
            loads.append(pltpu.make_async_copy(src.at[rows], mid.at[rows], in_sem.at[n]))
            stores.append(pltpu.make_async_copy(mid.at[rows], dst.at[rows], out_sem.at[n]))
    for copy in loads:
        copy.start()
    for load, store in zip(loads, stores):
        load.wait()
        store.start()
    for copy in stores:
        copy.wait()


def settle(results):
    anywhere = pl.BlockSpec(memory_space=pl.ANY)
    sem = pltpu.SemaphoreType.DMA((4 * len(results),))
    return pl.pallas_call(
        functools.partial(settle_kernel, len(results), 4),
        in_specs=[anywhere] * len(results),
        out_specs=[anywhere] * len(results),
        out_shape=[jax.ShapeDtypeStruct(a.shape, a.dtype) for a in results],
        scratch_shapes=[pltpu.VMEM(a.shape, a.dtype) for a in results] + [sem, sem],
        compiler_params=pltpu.CompilerParams(vmem_limit_bytes=62 << 20),
    )(*results)


def reversed_order(count):
    bits = count.bit_length() - 1
    return np.array([int(format(i, "b").zfill(bits)[::-1], 2) if bits else 0 for i in range(count)])


def run(queries, cotangent, w_key, w_value, database, nb_shard, nb_row):
    shards, seqs = lax.axis_size("db"), lax.axis_size("dp")
    _, rows, width = queries.shape
    _, count, neigh = nb_shard.shape
    base, nb_len, enc = database.shape
    window = rows // count
    asks = count * neigh
    slots = 3 * asks // (2 * shards)
    fused = shards == 4 and seqs == 8
    devices = shards * seqs
    share = enc // devices
    piece = nb_len // seqs
    wide = 2 * width
    quarter = enc // 8
    padded = -(-share // 16) * 16
    block = base * piece
    order = reversed_order(devices)
    if fused:
        bits = np.arange(devices)[:, None] // np.array([16, 8, 4, 2, 1])[None, :] % 2
        order = bits @ np.array([1, 4, 8, 2, 16])
    chunks = 4
    thin = wide // chunks
    source = (order[:, None] * share + np.arange(share)[None, :]).reshape(-1)
    shuffle = (np.arange(enc)[:, None] == source[None, :]).astype(jnp.bfloat16)
    cuts = [slice(0, 512), slice(512, enc)]

    anywhere = pl.BlockSpec(memory_space=pl.ANY)
    vmem = pl.BlockSpec(memory_space=pltpu.VMEM)
    smem = pl.BlockSpec(memory_space=pltpu.SMEM)
    sem = pltpu.SemaphoreType.DMA
    names, inputs, specs = [], [], []

    def give(name, value, spec):
        names.append(name)
        inputs.append(value)
        specs.append(spec)

    give("shard_ref", nb_shard[0].T, smem)
    give("row_ref", nb_row[0].T, smem)
    give("q_any", queries.reshape(count, window, width), anywhere)
    give("g_any", cotangent.reshape(count, window, width), anywhere)
    give("wk_any", w_key, anywhere)
    give("wv_any", w_value, anywhere)
    give("db_any", database, anywhere)
    give("shuffle_any", jnp.asarray(shuffle), anywhere)
    if fused:
        row = np.arange(4 * padded)[:, None]
        col = np.arange(4 * share)[None, :]
        spread = (row // padded == col // share) & (row % padded == col % share)
        give("spread_ref", jnp.asarray(spread.astype(jnp.bfloat16)), vmem)

    outs = [
        ("out_any", (count, window, width), BF, anywhere),
        ("dq_any", (count, window, width), BF, anywhere),
    ]
    if fused:
        outs += [
            ("gk_ref", (share, width), F32, vmem),
            ("gv_ref", (share, width), F32, vmem),
            ("gd_ref", (block, enc), BF, vmem),
        ]
    else:
        outs += [
            ("both_any", (asks * nb_len, wide), BF, anywhere),
            ("lt_any", (enc, asks * nb_len), BF, anywhere),
        ]
    scratch = [
        ("dbv", pltpu.VMEM((base, nb_len, enc), BF)),
        ("qwin", pltpu.VMEM((count + 1, window, width), BF)),
        ("gwin", pltpu.VMEM((count + 1, window, width), BF)),
        ("owin", pltpu.VMEM((count + 1, window, width), BF)),
        ("dwin", pltpu.VMEM((count + 1, window, width), BF)),
        ("oprev", pltpu.VMEM((window, width), BF)),
        ("dprev", pltpu.VMEM((window, width), BF)),
        ("qblk", pltpu.VMEM((window, width), BF)),
        ("gblk", pltpu.VMEM((window, width), BF)),
        ("wts", pltpu.VMEM((enc, wide), BF)),
        ("shuffle", pltpu.VMEM((enc, enc), BF)),
        ("states", pltpu.VMEM((neigh * nb_len, enc), BF)),
        ("both", pltpu.VMEM((asks * nb_len, wide), BF)),
        ("lt", pltpu.VMEM((enc, asks * nb_len), BF)),
        ("fetch", pltpu.VMEM((slots * 3, nb_len, enc), BF)),
        ("recv0", pltpu.VMEM((shards, nb_len, enc), BF)),
        ("recv1", pltpu.VMEM((shards, nb_len, enc), BF)),
        ("recv2", pltpu.VMEM((shards, nb_len, enc), BF)),
        ("asksend", pltpu.VMEM((8, 128), jnp.int32)),
        ("askbox", pltpu.VMEM((shards, 8, 128), jnp.int32)),
        ("ask_sm", pltpu.SMEM((shards, 8, 128), jnp.int32)),
        ("rank_sm", pltpu.SMEM((asks,), jnp.int32)),
        ("load_sem", sem((12,))),
        ("ask_send", sem((3,))),
        ("ask_recv", sem((3,))),
        ("edge_send", sem((4,))),
        ("edge_recv", sem((4,))),
        ("fetch_send", sem((slots * 3,))),
        ("fetch_recv", sem((slots * 3,))),
    ]
    if fused:
        peers = seqs - 1
        scratch += [
            ("ids", pltpu.VMEM((8, 128), jnp.int32)),
            ("idbox", pltpu.VMEM((seqs, 8, 128), jnp.int32)),
            ("member", pltpu.VMEM((shards * block, seqs * asks * piece), BF)),
            ("got1", pltpu.VMEM((chunks, 4 * quarter, thin), BF)),
            ("got2", pltpu.VMEM((chunks, 2 * quarter, thin), BF)),
            ("got3", pltpu.VMEM((chunks, quarter, thin), BF)),
            ("zed", pltpu.VMEM((chunks, 2, 2, padded, thin), BF)),
            ("got4", pltpu.VMEM((chunks, 2, padded, thin), BF)),
            ("got5", pltpu.VMEM((chunks, padded, thin), BF)),
            ("arrived", pltpu.VMEM((seqs, asks * piece, enc), BF)),
            ("dgot1", pltpu.VMEM((2, block // nb_len, nb_len, enc), BF)),
            ("mine", pltpu.VMEM((2, block // nb_len, nb_len, enc), F32)),
            ("dgot2", pltpu.VMEM((block // nb_len, nb_len, enc), BF)),
            ("send_sem", sem((48,))),
            ("recv_sem", sem((48,))),
            ("across_send", sem((count, len(cuts) * peers))),
            ("across_recv", sem((count, len(cuts) * peers))),
            ("id_send", sem((peers,))),
            ("id_recv", sem((peers,))),
        ]
    names += [o[0] for o in outs] + [s[0] for s in scratch]
    plan = dict(
        names=names, fused=fused, asks=asks, neigh=neigh, slots=slots, piece=piece, cuts=cuts,
        chunks=chunks,
    )
    results = pl.pallas_call(
        functools.partial(kernel, plan),
        in_specs=specs,
        out_specs=[o[3] for o in outs],
        out_shape=[jax.ShapeDtypeStruct(o[1], o[2]) for o in outs],
        scratch_shapes=[s[1] for s in scratch],
        compiler_params=pltpu.CompilerParams(
            vmem_limit_bytes=62 << 20, collective_id=0, has_side_effects=True
        ),
        cost_estimate=pl.CostEstimate(
            flops=28 * 10**9, bytes_accessed=40 << 20, transcendentals=1 << 20
        ),
    )(*inputs)
    if fused:
        results = settle(results)
    attn_out = results[0].reshape(1, rows, width)
    grad_queries = results[1].reshape(1, rows, width)
    if fused:
        grad_database = results[4].reshape(base, piece, enc)
        return (attn_out, grad_queries, results[2], results[3], grad_database)

    both, lt = results[2:]
    own_ids = (nb_shard * base + nb_row).reshape(asks)
    ids = jnp.broadcast_to(own_ids[None], (seqs, asks))
    ids = lax.all_to_all(ids, "dp", split_axis=0, concat_axis=0, tiled=True)
    ids = ids.reshape(seqs * asks)
    member = (ids[None, :] == jnp.arange(shards * base, dtype=jnp.int32)[:, None]).astype(BF)
    steps = [("db", b) for b in bits_of("db")] + [("dp", b) for b in bits_of("dp")]
    grads = []
    for part in range(2):
        grad = dot(lt, both[:, part * width : (part + 1) * width], ((1,), (0,)))
        grads.append(halve_all(grad.astype(BF), steps))
    w_both = jnp.concatenate([w_key, w_value], axis=1)
    dstates = dot(both, w_both, ((1,), (1,))).astype(BF)
    dstates = dstates.reshape(asks, seqs, piece, enc).transpose(1, 0, 2, 3)
    arrived = lax.all_to_all(dstates, "dp", split_axis=0, concat_axis=0, tiled=True)
    dense = dot(member, arrived.reshape(seqs * asks, piece * enc), ((1,), (0,)))
    dense = dense.astype(BF).reshape(shards, base, piece, enc)
    dense = jnp.stack([dense[i] for i in reversed_order(shards)])
    grad_database = halve_all(dense, [("db", b) for b in bits_of("db")])[0].astype(BF)
    return (attn_out, grad_queries, grads[0], grads[1], grad_database)


def halve(block, axis, bit):
    size = lax.axis_size(axis)
    half = block.shape[0] // 2
    side = lax.rem(lax.axis_index(axis) // bit, 2)
    give = lax.dynamic_slice_in_dim(block, (1 - side) * half, half, 0)
    mine = lax.dynamic_slice_in_dim(block, side * half, half, 0)
    got = lax.ppermute(give, axis, [(i, i ^ bit) for i in range(size)])
    return mine.astype(F32) + got.astype(F32)


def bits_of(axis):
    size = lax.axis_size(axis)
    return [1 << b for b in range(size.bit_length() - 1)]


def halve_all(block, steps):
    for axis, bit in steps[:-1]:
        block = halve(block, axis, bit).astype(BF)
    return halve(block, *steps[-1])


def solution(mesh):
    return jax.shard_map(
        run,
        mesh=mesh,
        in_specs=(
            P("dp", "db", None),
            P("dp", "db", None),
            P(),
            P(),
            P("db", None, None),
            P("dp", "db", None),
            P("dp", "db", None),
        ),
        out_specs=(
            P("dp", "db", None),
            P("dp", "db", None),
            P(("dp", "db"), None),
            P(("dp", "db"), None),
            P("db", "dp", None),
        ),
        check_vma=False,
    )
```

```python
import functools
import math
from types import SimpleNamespace

import jax
import jax.numpy as jnp
import numpy as np
from jax import lax
from jax.experimental import pallas as pl
from jax.experimental.pallas import tpu as pltpu
from jax.sharding import PartitionSpec as P

HSIZE = 128
BF, F32 = jnp.bfloat16, jnp.float32
MESH = pl.DeviceIdType.MESH


def dot(a, b, dims):
    return lax.dot_general(a, b, (dims, ((), ())), preferred_element_type=F32)


def choose(level, wanted, a, b):
    same = jnp.full(a.shape, level, jnp.int32) == wanted
    return jnp.where(same, a.astype(F32), b.astype(F32)).astype(BF)


def add(a, b):
    return (a.astype(F32) + b.astype(F32)).astype(BF)


def attend(r, u, states, group):
    width = r.qblk.shape[1]
    span = states.shape[0]
    scale = 1.0 / math.sqrt(HSIZE)
    rows = pl.ds(pl.multiple_of(u * span, span), span)
    for first in range(0, width // HSIZE, group):
        many = slice(first * HSIZE, (first + group) * HSIZE)
        vmany = slice(width + first * HSIZE, width + (first + group) * HSIZE)
        keys = dot(states, r.wts[:, many], ((1,), (0,))).astype(BF)
        values = dot(states, r.wts[:, vmany], ((1,), (0,))).astype(BF)
        heads = range(group)
        local = [slice(h * HSIZE, (h + 1) * HSIZE) for h in heads]
        cols = [slice((first + h) * HSIZE, (first + h + 1) * HSIZE) for h in heads]
        vcols = [slice(width + (first + h) * HSIZE, width + (first + h + 1) * HSIZE) for h in heads]
        q = [r.qblk[:, cols[h]] for h in heads]
        g = [r.gblk[:, cols[h]] for h in heads]
        k = [keys[:, local[h]] for h in heads]
        v = [values[:, local[h]] for h in heads]
        scores = [dot(q[h], k[h], ((1,), (1,))) * scale for h in heads]
        dprob = [dot(g[h], v[h], ((1,), (1,))) for h in heads]
        expo = [jnp.exp(t - jnp.max(t, axis=-1, keepdims=True)) for t in scores]
        prob = [t * (1.0 / jnp.sum(t, axis=-1, keepdims=True)) for t in expo]
        rowdot = [jnp.sum(prob[h] * dprob[h], axis=-1, keepdims=True) for h in heads]
        dscore = [(prob[h] * (dprob[h] - rowdot[h]) * scale).astype(BF) for h in heads]
        prob_b = [t.astype(BF) for t in prob]
        for h in heads:
            r.owin[u, :, cols[h]] = dot(prob_b[h], v[h], ((1,), (0,))).astype(BF)
            r.dwin[u, :, cols[h]] = dot(dscore[h], k[h], ((1,), (0,))).astype(BF)
        for h in heads:
            r.both[rows, cols[h]] = dot(dscore[h], q[h], ((0,), (0,))).astype(BF)
            r.both[rows, vcols[h]] = dot(prob_b[h], g[h], ((0,), (0,))).astype(BF)


def kernel(plan, *refs):
    r = SimpleNamespace(**dict(zip(plan["names"], refs)))
    fused, asks, neigh, slots = plan["fused"], plan["asks"], plan["neigh"], plan["slots"]
    piece = plan["piece"]
    count = asks // neigh
    dp, db = lax.axis_index("dp"), lax.axis_index("db")
    shards = r.recv0.shape[0]
    nb_len = r.recv0.shape[1]
    base = r.dbv.shape[0]
    enc, wide = r.wts.shape
    half = wide // 2
    span = neigh * nb_len
    window = r.qblk.shape[0]
    recvs = [r.recv0, r.recv1, r.recv2]

    c, x = lax.rem(db, 2), db // 2
    core, far = db + 1 - 2 * c, db + 2 - 4 * x
    cross = far + 1 - 2 * c
    near = [(dp, far), (dp, cross), (dp, core)]
    after, before = (dp, lax.rem(db + 1, shards)), (dp, lax.rem(db + shards - 1, shards))
    seqs = lax.axis_size("dp")
    others = [(lax.rem(dp + d, seqs), db) for d in range(1, seqs)] if fused else []

    loads = [
        pltpu.make_async_copy(r.db_any, r.dbv, r.load_sem.at[0]),
        pltpu.make_async_copy(r.q_any, r.qwin.at[0:count], r.load_sem.at[1]),
        pltpu.make_async_copy(r.g_any, r.gwin.at[0:count], r.load_sem.at[2]),
        pltpu.make_async_copy(r.wk_any, r.wts.at[:, 0:half], r.load_sem.at[3]),
        pltpu.make_async_copy(r.wv_any, r.wts.at[:, half:wide], r.load_sem.at[4]),
        pltpu.make_async_copy(r.shuffle_any, r.shuffle, r.load_sem.at[5]),
    ]
    for load in loads:
        load.start()
    barrier = pltpu.get_barrier_semaphore()
    for peer in near + others:
        pl.semaphore_signal(barrier, inc=1, device_id=peer, device_id_type=MESH)

    def flag(condition):
        return condition.astype(jnp.int32)

    named_shard = [[r.shard_ref[n, u] for n in range(neigh)] for u in range(count)]
    named_row = [[r.row_ref[n, u] for n in range(neigh)] for u in range(count)]
    flat = [t for pair in named_shard for t in pair]
    crowded = [
        sum(flag(sum(flag(other == t) for other in flat) >= slots) for t in pair)
        for pair in named_shard
    ]
    total = sum(crowded)
    open_, is_last = jnp.int32(1), []
    for u in range(count):
        chosen = open_ * flag(crowded[u] * slots == total)
        is_last.append(chosen)
        open_ = open_ - chosen
    order, target, wanted = [], [], []

    def swapped(values, u):
        if u < count - 1:
            return values[u] + is_last[u] * (values[count - 1] - values[u])
        return sum(is_last[v] * values[v] for v in range(count))

    for u in range(count):
        order.append(swapped(list(range(count)), u))
        r.order_sm[u] = order[u]
        for n in range(neigh):
            target.append(swapped([pair[n] for pair in named_shard], u))
            wanted.append(swapped([pair[n] for pair in named_row], u))
    rank = []
    for a in range(asks):
        seen = jnp.int32(0)
        for b in range(a):
            seen = seen + flag(target[b] == target[a])
        rank.append(seen)
        r.rank_sm[a] = seen
        r.shard_sm[a] = target[a]
    row = lax.broadcasted_iota(jnp.int32, (8, 128), 0)
    lane = lax.broadcasted_iota(jnp.int32, (8, 128), 1)
    mine = jnp.zeros((8, 128), jnp.int32)
    for a in range(asks):
        mine = jnp.where((row == target[a]) & (lane == rank[a]), wanted[a], mine)
    r.asksend[...] = mine
    r.askbox[db] = mine

    def remote(src, dst, send_sem, recv_sem, peer):
        return pltpu.make_async_remote_copy(
            src_ref=src,
            dst_ref=dst,
            send_sem=send_sem,
            recv_sem=recv_sem,
            device_id=peer,
            device_id_type=MESH,
        )

    asked = [
        remote(r.asksend, r.askbox.at[db], r.ask_send.at[d], r.ask_recv.at[d], near[d])
        for d in range(3)
    ]
    edges = [
        remote(src.at[0], dst.at[count], r.edge_send.at[e], r.edge_recv.at[e], before)
        for e, (src, dst) in enumerate(((r.q_any, r.qwin), (r.g_any, r.gwin)))
    ]
    pl.semaphore_wait(barrier, len(near) + len(others))
    for copy in asked + edges:
        copy.start()

    own = jnp.zeros((8, 128), jnp.int32)
    for a in range(asks):
        own = jnp.where(lane // plan["unit"] == a, target[a] * base + wanted[a], own)
    r.ids[...] = own
    if fused:
        r.idbox[dp] = own
        named = [
            remote(r.ids, r.idbox.at[dp], r.id_send.at[d], r.id_recv.at[d], peer)
            for d, peer in enumerate(others)
        ]
        for copy in named:
            copy.start()

    for copy in asked:
        copy.wait_recv()
    to_scalar = pltpu.make_async_copy(r.askbox, r.ask_sm, r.load_sem.at[6])
    to_scalar.start()
    to_scalar.wait()
    loads[0].wait()
    rounds = []

    def entry(asker, k):
        return r.dbv[r.ask_sm[asker, db, k]]

    for k in range(slots):
        for d, peer in enumerate(near):
            r.fetch[k * 3 + d] = entry(peer[1], k)
        recvs[k][db] = entry(db, k)
        rounds.append(
            [
                remote(
                    r.fetch.at[k * 3 + d],
                    recvs[k].at[db],
                    r.fetch_send.at[k * 3 + d],
                    r.fetch_recv.at[k * 3 + d],
                    near[d],
                )
                for d in range(3)
            ]
        )
        if k == 0:
            for copy in rounds[0]:
                copy.start()
    if fused:
        block = r.gd_ref.shape[0]
        lanes = r.member.shape[1] // seqs
        for copy in named:
            copy.wait_recv()
        row = lax.broadcasted_iota(jnp.int32, (block, lanes), 0)
        lane = lax.broadcasted_iota(jnp.int32, (block, lanes), 1)
        place = jnp.where(row % piece == lane % piece, row // piece, -1)

        @pl.loop(0, shards)
        def _(i):
            rows = pl.ds(pl.multiple_of(i * block, block), block)
            for k in range(seqs):
                hit = place == r.idbox[k][0:1] - i * (block // piece)
                r.member[rows, k * lanes : (k + 1) * lanes] = jnp.where(
                    hit & (place >= 0), 1.0, 0.0
                ).astype(BF)

    for load in loads[1:]:
        load.wait()
    for copy in edges:
        copy.wait_recv()

    @pl.when(db == shards - 1)
    def _():
        r.qwin[count] = jnp.zeros((window, half), BF)
        r.gwin[count] = jnp.zeros((window, half), BF)


    cuts = plan["cuts"]

    def across(u, d):
        start = pl.multiple_of(u * neigh * piece, neigh * piece)
        rows = pl.ds(start, neigh * piece)
        return remote(
            r.dbv.at[others[d][0], rows],
            r.arrived.at[dp, rows],
            r.across_send.at[u, d],
            r.across_recv.at[u, d],
            others[d],
        )

    last = lax.broadcasted_iota(jnp.int32, (16, half), 0) == 15

    @pl.loop(0, count)
    def _(u):
        def pick(levels):
            for n in range(neigh):
                a = u * neigh + n
                t, level = r.shard_sm[a], r.rank_sm[a]
                block = recvs[levels - 1][t]
                for j in range(levels - 1):
                    block = choose(level, j, recvs[j][t], block)
                r.states[n * nb_len : (n + 1) * nb_len] = block

        @pl.when(u == 0)
        def _():
            for copy in rounds[0]:
                copy.wait_recv()
            for copy in rounds[1]:
                copy.start()
            pick(1)

        @pl.when(u == 1)
        def _():
            for copy in rounds[1]:
                copy.wait_recv()
            for copy in rounds[2]:
                copy.start()

        @pl.when((u > 0) & (u < count - 1))
        def _():
            pick(2)

        @pl.when(u == count - 1)
        def _():
            for copy in rounds[2]:
                copy.wait_recv()
            pick(3)

        place = r.order_sm[u]
        for win, blk in ((r.qwin, r.qblk), (r.gwin, r.gblk)):
            tail = slice(window - 16, window)
            blk[0 : window - 16] = win[place + 1, 0 : window - 16]
            blk[tail] = jnp.where(
                last, win[place, tail].astype(F32), win[place + 1, tail].astype(F32)
            ).astype(BF)

        states = r.states[...]
        r.lt[:, pl.ds(pl.multiple_of(u * span, span), span)] = dot(
            r.shuffle[...], states, ((1,), (1,))
        ).astype(BF)
        attend(r, u, states, 16)

        if fused:
            rows = pl.ds(pl.multiple_of(u * span, span), span)
            for h, cols in enumerate(cuts):
                out = dot(r.both[rows], r.wts[cols], ((1,), (1,))).astype(BF)
                for n in range(neigh):
                    for j in range(seqs):
                        into = pl.ds(pl.multiple_of((u * neigh + n) * piece, piece), piece)
                        start = n * nb_len + j * piece
                        r.dbv[j, into, cols] = out[start : start + piece]
                part = pl.ds(pl.multiple_of(u * neigh * piece, neigh * piece), neigh * piece)
                r.arrived[dp, part, cols] = r.dbv[dp, part, cols]
            for d in range(len(others)):
                across(u, d).start()

    r.qblk[...] = r.owin[r.order_sm[count - 1]]
    r.gblk[...] = r.dwin[r.order_sm[count - 1]]
    passed = [
        remote(blk, got, r.edge_send.at[2 + e], r.edge_recv.at[2 + e], after)
        for e, (blk, got) in enumerate(((r.qblk, r.oprev), (r.gblk, r.dprev)))
    ]
    for copy in passed:
        copy.start()

    def edge_outputs():
        writes = []
        for e, (win, got, full, out) in enumerate(
            ((r.owin, r.oprev, r.qwin, r.out_any), (r.dwin, r.dprev, r.gwin, r.dq_any))
        ):
            head, tail = slice(0, window - 16), slice(window - 16, window)
            for w in range(1, count):
                mine, back = r.order_sm[w], r.order_sm[w - 1]
                full[w, head] = win[back, head]
                full[w, tail] = jnp.where(
                    last, win[mine, tail].astype(F32), win[back, tail].astype(F32)
                ).astype(BF)
            passed[e].wait_recv()
            keep = jnp.where(db > 0, 1.0, 0.0)
            full[0, head] = (got[head].astype(F32) * keep).astype(BF)
            full[0, tail] = jnp.where(
                last, win[r.order_sm[0], tail].astype(F32), got[tail].astype(F32) * keep
            ).astype(BF)
            writes.append(pltpu.make_async_copy(full.at[0:count], out, r.load_sem.at[7 + e]))
            writes[-1].start()
        return writes

    sent = asked + edges + passed + [copy for part in rounds for copy in part]
    if fused:
        finish(r, plan, remote, across, others, named, edge_outputs, sent)
        return
    writes = edge_outputs()
    for n, (src, dst) in enumerate(((r.both, r.both_any), (r.lt, r.lt_any))):
        writes.append(pltpu.make_async_copy(src, dst, r.load_sem.at[9 + n]))
        writes[-1].start()
    for copy in writes:
        copy.wait()
    for copy in sent:
        copy.wait_send()


def finish(r, plan, remote, across, others, named, edge_outputs, sent):
    piece = plan["piece"]
    cuts = plan["cuts"]
    dp, db = lax.axis_index("dp"), lax.axis_index("db")
    seqs = r.arrived.shape[0]
    enc, wide = r.wts.shape
    half = wide // 2
    quarter = enc // 8
    c, x = lax.rem(db, 2), db // 2
    y, z0, z1 = lax.rem(dp, 2), lax.rem(dp // 2, 2), dp // 4
    pc = (dp, db + 1 - 2 * c)
    px = (dp, db + 2 - 4 * x)
    py = (dp + 1 - 2 * y, db)
    pz0 = (dp + 2 - 4 * z0, db)
    pz1 = (dp + 4 - 8 * z1, db)
    copies = []
    tile = 512

    def send(src, dst, peer):
        number = len(copies)
        copy = remote(src, dst, r.send_sem.at[number], r.recv_sem.at[number], peer)
        copy.start()
        copies.append(copy)
        return copy

    chunks = plan["chunks"]

    def part(p, row, n=1):
        rows = pl.ds(pl.multiple_of(row * quarter, quarter), n * quarter)
        return r.both.at[rows, chunks[p]]

    def weight_grad(p):
        start, stop = chunks[p].start, chunks[p].stop

        @pl.loop(0, (stop - start) // tile)
        def _(t):
            cols = pl.ds(pl.multiple_of(start + t * tile, tile), tile)
            out = jnp.dot(r.lt[...], r.both[:, cols], preferred_element_type=F32)
            r.both[0:enc, cols] = out.astype(BF)

        return send(part(p, (1 - c) * 4, 4), r.got1.at[:, chunks[p]], pc)

    def join(p, row, got):
        here = part(p, row)
        here[...] = add(here[...], got)

    def rows_of(i, n=1):
        return slice(i * quarter, (i + n) * quarter)

    def after_core(p, copy):
        copy.wait_recv()
        for i in range(4):
            join(p, c * 4 + i, r.got1[rows_of(i), chunks[p]])

    def first(p):
        if p % 2 == 0:
            src = part(p, c * 4 + (1 - y) * 2, 2)
            return [send(src, r.got2.at[:, chunks[p]], py)]
        return [
            send(part(p, c * 4 + i * 2 + 1 - z0), r.got2.at[rows_of(i), chunks[p]], pz0)
            for i in range(2)
        ]

    def second(p, arrivals):
        for copy in arrivals:
            copy.wait_recv()
        for i in range(2):
            into = c * 4 + y * 2 + i if p % 2 == 0 else c * 4 + i * 2 + z0
            join(p, into, r.got2[rows_of(i), chunks[p]])
        if p % 2 == 0:
            return send(part(p, c * 4 + y * 2 + 1 - z0), r.got3.at[:, chunks[p]], pz0)
        return send(part(p, c * 4 + (1 - y) * 2 + z0), r.got3.at[:, chunks[p]], py)

    def third(p, copy):
        copy.wait_recv()
        total = add(part(p, c * 4 + y * 2 + z0)[...], r.got3[:, chunks[p]])
        _, _, padded, _ = r.zed.shape
        r.zed[:, :, :, chunks[p]] = (
            jnp.dot(r.spread_ref[...], total, preferred_element_type=F32)
            .astype(BF)
            .reshape(2, 2, padded, total.shape[1])
        )
        return send(r.zed.at[1 - x, :, :, chunks[p]], r.got4.at[:, :, chunks[p]], px)

    def fourth(p, copy):
        copy.wait_recv()
        for j in range(2):
            r.zed[x, j, :, chunks[p]] = add(
                r.zed[x, j, :, chunks[p]], r.got4[j, :, chunks[p]]
            )
        return send(r.zed.at[x, 1 - z1, :, chunks[p]], r.got5.at[:, chunks[p]], pz1)

    def fifth(p, copy):
        copy.wait_recv()
        start, stop = chunks[p].start, chunks[p].stop
        out_ref, back = (r.gk_ref, 0) if start < half else (r.gv_ref, half)
        summed = r.zed[x, z1, :, chunks[p]].astype(F32) + r.got5[:, chunks[p]].astype(F32)
        out_ref[:, start - back : stop - back] = summed[: out_ref.shape[0]]

    block = r.gd_ref.shape[0]
    every = r.arrived.shape[0] * r.arrived.shape[1]
    count = r.across_send.shape[0]

    def dense(shard, cols):
        return jnp.dot(
            r.member[pl.ds(pl.multiple_of(shard * block, block), block)],
            r.arrived[:, :, cols].reshape(every, cols.stop - cols.start),
            preferred_element_type=F32,
        ).reshape(many, nb_len, cols.stop - cols.start)

    many, nb_len = r.dgot2.shape[0:2]
    give = [slice(seqs + n * many, seqs + (n + 1) * many) for n in range(3)]

    def core_start(h):
        cols = cuts[h]
        started = []
        for far in (1, 0):
            side = x if far == 0 else 1 - x
            r.dbv[give[far], :, cols] = dense(2 * side + 1 - c, cols).astype(BF)
            started.append(send(r.dbv.at[give[far], :, cols], r.dgot1.at[far, :, :, cols], pc))
        for far in (1, 0):
            side = x if far == 0 else 1 - x
            r.mine[far, :, :, cols] = dense(2 * side + c, cols)
        return started

    def x_start(h, started):
        cols = cuts[h]
        started[0].wait_recv()
        summed = r.mine[1, :, :, cols] + r.dgot1[1, :, :, cols].astype(F32)
        r.dbv[give[2], :, cols] = summed.astype(BF)
        copy = send(r.dbv.at[give[2], :, cols], r.dgot2.at[:, :, cols], px)
        started[1].wait_recv()
        r.mine[0, :, :, cols] = r.mine[0, :, :, cols] + r.dgot1[0, :, :, cols].astype(F32)
        return copy

    pairs = len(chunks) // 2
    way = [None] * len(chunks)
    for p in range(len(chunks)):
        way[p] = weight_grad(p)
        if p > 0:
            after_core(p - 1, way[p - 1])
            if p <= 2:
                way[p - 1] = first(p - 1)
    after_core(len(chunks) - 1, way[-1])
    if len(chunks) == 2:
        way[1] = first(1)
    writes = edge_outputs()
    for u in range(count):
        for d in range(len(others)):
            across(u, d).wait_recv()
    cores = [core_start(h) for h in range(len(cuts))]
    xcopy = [x_start(h, cores[h]) for h in range(len(cuts))]
    for i in range(pairs):
        now = (2 * i, 2 * i + 1)
        if i > 0:
            for p in (2 * i - 2, 2 * i - 1):
                way[p] = third(p, way[p])
        for p in now:
            way[p] = second(p, way[p])
        if i + 1 < pairs:
            for p in now:
                way[p + 2] = first(p + 2)
        if i > 0:
            for p in (2 * i - 2, 2 * i - 1):
                way[p] = fourth(p, way[p])
    ends = (len(chunks) - 2, len(chunks) - 1)
    for p in ends:
        way[p] = third(p, way[p])
    for h, cols in enumerate(cuts):
        xcopy[h].wait_recv()
        summed = r.mine[0, :, :, cols] + r.dgot2[:, :, cols].astype(F32)
        r.gd_ref[:, cols] = summed.astype(BF).reshape(block, cols.stop - cols.start)
    for p in ends:
        way[p] = fourth(p, way[p])
    for p in range(len(chunks)):
        fifth(p, way[p])
    for copy in copies + named + sent:
        copy.wait_send()
    for u in range(count):
        for d in range(len(others)):
            across(u, d).wait_send()
    for copy in writes:
        copy.wait()


def settle_kernel(count, pieces, *refs):
    sources, targets, held = refs[:count], refs[count : 2 * count], refs[2 * count : 3 * count]
    in_sem, out_sem = refs[3 * count :]
    loads, stores = [], []
    for src, dst, mid in zip(sources, targets, held):
        size = src.shape[0]
        cut = pieces if len(src.shape) == 3 else 1
        step = size // cut
        for i in range(cut):
            rows = pl.ds(i * step, step)
            n = len(loads)
            loads.append(pltpu.make_async_copy(src.at[rows], mid.at[rows], in_sem.at[n]))
            stores.append(pltpu.make_async_copy(mid.at[rows], dst.at[rows], out_sem.at[n]))
    for copy in loads:
        copy.start()
    for load, store in zip(loads, stores):
        load.wait()
        store.start()
    for copy in stores:
        copy.wait()


def settle(results):
    anywhere = pl.BlockSpec(memory_space=pl.ANY)
    sem = pltpu.SemaphoreType.DMA((4 * len(results),))
    return pl.pallas_call(
        functools.partial(settle_kernel, len(results), 4),
        in_specs=[anywhere] * len(results),
        out_specs=[anywhere] * len(results),
        out_shape=[jax.ShapeDtypeStruct(a.shape, a.dtype) for a in results],
        scratch_shapes=[pltpu.VMEM(a.shape, a.dtype) for a in results] + [sem, sem],
        compiler_params=pltpu.CompilerParams(vmem_limit_bytes=62 << 20),
    )(*results)


def reversed_order(count):
    bits = count.bit_length() - 1
    return np.array([int(format(i, "b").zfill(bits)[::-1], 2) if bits else 0 for i in range(count)])


def run(queries, cotangent, w_key, w_value, database, nb_shard, nb_row):
    shards, seqs = lax.axis_size("db"), lax.axis_size("dp")
    _, rows, width = queries.shape
    _, count, neigh = nb_shard.shape
    base, nb_len, enc = database.shape
    window = rows // count
    asks = count * neigh
    slots = 3 * asks // (2 * shards)
    fused = shards == 4 and seqs == 8
    devices = shards * seqs
    share = enc // devices
    piece = nb_len // seqs
    wide = 2 * width
    quarter = enc // 8
    padded = -(-share // 16) * 16
    block = base * piece
    order = reversed_order(devices)
    if fused:
        bits = np.arange(devices)[:, None] // np.array([16, 8, 4, 2, 1])[None, :] % 2
        order = bits @ np.array([1, 4, 8, 2, 16])
    chunks, start = [], 0
    for size in (8, 8):
        size = size * width // 16
        for first in (0, width):
            chunks.append(slice(first + start, first + start + size))
        start += size
    source = (order[:, None] * share + np.arange(share)[None, :]).reshape(-1)
    shuffle = (source[:, None] == np.arange(enc)[None, :]).astype(jnp.bfloat16)
    cuts = [slice(0, 512), slice(512, enc)]

    anywhere = pl.BlockSpec(memory_space=pl.ANY)
    vmem = pl.BlockSpec(memory_space=pltpu.VMEM)
    smem = pl.BlockSpec(memory_space=pltpu.SMEM)
    sem = pltpu.SemaphoreType.DMA
    names, inputs, specs = [], [], []

    def give(name, value, spec):
        names.append(name)
        inputs.append(value)
        specs.append(spec)

    give("shard_ref", nb_shard[0].T, smem)
    give("row_ref", nb_row[0].T, smem)
    give("q_any", queries.reshape(count, window, width), anywhere)
    give("g_any", cotangent.reshape(count, window, width), anywhere)
    give("wk_any", w_key, anywhere)
    give("wv_any", w_value, anywhere)
    give("db_any", database, anywhere)
    give("shuffle_any", jnp.asarray(shuffle), anywhere)
    if fused:
        row = np.arange(4 * padded)[:, None]
        col = np.arange(4 * share)[None, :]
        spread = (row // padded == col // share) & (row % padded == col % share)
        give("spread_ref", jnp.asarray(spread.astype(jnp.bfloat16)), vmem)

    outs = [
        ("out_any", (count, window, width), BF, anywhere),
        ("dq_any", (count, window, width), BF, anywhere),
    ]
    if fused:
        outs += [
            ("gk_ref", (share, width), F32, vmem),
            ("gv_ref", (share, width), F32, vmem),
            ("gd_ref", (block, enc), BF, vmem),
        ]
    else:
        outs += [
            ("both_any", (asks * nb_len, wide), BF, anywhere),
            ("lt_any", (enc, asks * nb_len), BF, anywhere),
            ("ids", (8, 128), jnp.int32, vmem),
        ]
    scratch = [
        ("dbv", pltpu.VMEM((base, nb_len, enc), BF)),
        ("qwin", pltpu.VMEM((count + 1, window, width), BF)),
        ("gwin", pltpu.VMEM((count + 1, window, width), BF)),
        ("owin", pltpu.VMEM((count, window, width), BF)),
        ("dwin", pltpu.VMEM((count, window, width), BF)),
        ("oprev", pltpu.VMEM((window, width), BF)),
        ("dprev", pltpu.VMEM((window, width), BF)),
        ("qblk", pltpu.VMEM((window, width), BF)),
        ("gblk", pltpu.VMEM((window, width), BF)),
        ("wts", pltpu.VMEM((enc, wide), BF)),
        ("shuffle", pltpu.VMEM((enc, enc), BF)),
        ("states", pltpu.VMEM((neigh * nb_len, enc), BF)),
        ("both", pltpu.VMEM((asks * nb_len, wide), BF)),
        ("lt", pltpu.VMEM((enc, asks * nb_len), BF)),
        ("fetch", pltpu.VMEM((slots * 3, nb_len, enc), BF)),
        ("recv0", pltpu.VMEM((shards, nb_len, enc), BF)),
        ("recv1", pltpu.VMEM((shards, nb_len, enc), BF)),
        ("recv2", pltpu.VMEM((shards, nb_len, enc), BF)),
        ("asksend", pltpu.VMEM((8, 128), jnp.int32)),
        ("askbox", pltpu.VMEM((shards, 8, 128), jnp.int32)),
        ("ask_sm", pltpu.SMEM((shards, 8, 128), jnp.int32)),
        ("rank_sm", pltpu.SMEM((asks,), jnp.int32)),
        ("shard_sm", pltpu.SMEM((asks,), jnp.int32)),
        ("order_sm", pltpu.SMEM((count,), jnp.int32)),
        ("load_sem", sem((12,))),
        ("ask_send", sem((3,))),
        ("ask_recv", sem((3,))),
        ("edge_send", sem((4,))),
        ("edge_recv", sem((4,))),
        ("fetch_send", sem((slots * 3,))),
        ("fetch_recv", sem((slots * 3,))),
    ]
    if fused:
        peers = seqs - 1
        scratch += [
            ("ids", pltpu.VMEM((8, 128), jnp.int32)),
            ("idbox", pltpu.VMEM((seqs, 8, 128), jnp.int32)),
            ("member", pltpu.VMEM((shards * block, seqs * asks * piece), BF)),
            ("got1", pltpu.VMEM((4 * quarter, wide), BF)),
            ("got2", pltpu.VMEM((2 * quarter, wide), BF)),
            ("got3", pltpu.VMEM((quarter, wide), BF)),
            ("zed", pltpu.VMEM((2, 2, padded, wide), BF)),
            ("got4", pltpu.VMEM((2, padded, wide), BF)),
            ("got5", pltpu.VMEM((padded, wide), BF)),
            ("arrived", pltpu.VMEM((seqs, asks * piece, enc), BF)),
            ("dgot1", pltpu.VMEM((2, block // nb_len, nb_len, enc), BF)),
            ("mine", pltpu.VMEM((2, block // nb_len, nb_len, enc), F32)),
            ("dgot2", pltpu.VMEM((block // nb_len, nb_len, enc), BF)),
            ("send_sem", sem((64,))),
            ("recv_sem", sem((64,))),
            ("across_send", sem((count, peers))),
            ("across_recv", sem((count, peers))),
            ("id_send", sem((peers,))),
            ("id_recv", sem((peers,))),
        ]
    names += [o[0] for o in outs] + [s[0] for s in scratch]
    plan = dict(
        names=names, fused=fused, asks=asks, neigh=neigh, slots=slots, piece=piece, cuts=cuts,
        chunks=chunks, unit=piece if fused else 1,
    )
    results = pl.pallas_call(
        functools.partial(kernel, plan),
        in_specs=specs,
        out_specs=[o[3] for o in outs],
        out_shape=[jax.ShapeDtypeStruct(o[1], o[2]) for o in outs],
        scratch_shapes=[s[1] for s in scratch],
        compiler_params=pltpu.CompilerParams(
            vmem_limit_bytes=62 << 20, collective_id=0, has_side_effects=True
        ),
        cost_estimate=pl.CostEstimate(
            flops=28 * 10**9, bytes_accessed=40 << 20, transcendentals=1 << 20
        ),
    )(*inputs)
    if fused:
        results = settle(results)
    attn_out = results[0].reshape(1, rows, width)
    grad_queries = results[1].reshape(1, rows, width)
    if fused:
        grad_database = results[4].reshape(base, piece, enc)
        return (attn_out, grad_queries, results[2], results[3], grad_database)

    both, lt, own_ids = results[2:]
    ids = jnp.broadcast_to(own_ids[0:1, 0:asks], (seqs, asks))
    ids = lax.all_to_all(ids, "dp", split_axis=0, concat_axis=0, tiled=True)
    ids = ids.reshape(seqs * asks)
    member = (ids[None, :] == jnp.arange(shards * base, dtype=jnp.int32)[:, None]).astype(BF)
    steps = [("db", b) for b in bits_of("db")] + [("dp", b) for b in bits_of("dp")]
    grads = []
    for part in range(2):
        grad = dot(lt, both[:, part * width : (part + 1) * width], ((1,), (0,)))
        grads.append(halve_all(grad.astype(BF), steps))
    w_both = jnp.concatenate([w_key, w_value], axis=1)
    dstates = dot(both, w_both, ((1,), (1,))).astype(BF)
    dstates = dstates.reshape(asks, seqs, piece, enc).transpose(1, 0, 2, 3)
    arrived = lax.all_to_all(dstates, "dp", split_axis=0, concat_axis=0, tiled=True)
    dense = dot(member, arrived.reshape(seqs * asks, piece * enc), ((1,), (0,)))
    dense = dense.astype(BF).reshape(shards, base, piece, enc)
    dense = jnp.stack([dense[i] for i in reversed_order(shards)])
    grad_database = halve_all(dense, [("db", b) for b in bits_of("db")])[0].astype(BF)
    return (attn_out, grad_queries, grads[0], grads[1], grad_database)


def halve(block, axis, bit):
    size = lax.axis_size(axis)
    half = block.shape[0] // 2
    side = lax.rem(lax.axis_index(axis) // bit, 2)
    give = lax.dynamic_slice_in_dim(block, (1 - side) * half, half, 0)
    mine = lax.dynamic_slice_in_dim(block, side * half, half, 0)
    got = lax.ppermute(give, axis, [(i, i ^ bit) for i in range(size)])
    return mine.astype(F32) + got.astype(F32)


def bits_of(axis):
    size = lax.axis_size(axis)
    return [1 << b for b in range(size.bit_length() - 1)]


def halve_all(block, steps):
    for axis, bit in steps[:-1]:
        block = halve(block, axis, bit).astype(BF)
    return halve(block, *steps[-1])


def solution(mesh):
    return jax.shard_map(
        run,
        mesh=mesh,
        in_specs=(
            P("dp", "db", None),
            P("dp", "db", None),
            P(),
            P(),
            P("db", None, None),
            P("dp", "db", None),
            P("dp", "db", None),
        ),
        out_specs=(
            P("dp", "db", None),
            P("dp", "db", None),
            P(("dp", "db"), None),
            P(("dp", "db"), None),
            P("db", "dp", None),
        ),
        check_vma=False,
    )
```

```python
import functools
import math
from types import SimpleNamespace

import jax
import jax.numpy as jnp
import numpy as np
from jax import lax
from jax.experimental import pallas as pl
from jax.experimental.pallas import tpu as pltpu
from jax.sharding import PartitionSpec as P

HSIZE = 128
BF, F32 = jnp.bfloat16, jnp.float32
MESH = pl.DeviceIdType.MESH


def dot(a, b, dims):
    return lax.dot_general(a, b, (dims, ((), ())), preferred_element_type=F32)


def choose(level, wanted, a, b):
    same = jnp.full(a.shape, level, jnp.int32) == wanted
    return jnp.where(same, a.astype(F32), b.astype(F32)).astype(BF)


def add(a, b):
    return (a.astype(F32) + b.astype(F32)).astype(BF)


def attend(r, u, states, group):
    width = r.qblk.shape[1]
    span = states.shape[0]
    scale = 1.0 / math.sqrt(HSIZE)
    rows = pl.ds(pl.multiple_of(u * span, span), span)
    for first in range(0, width // HSIZE, group):
        many = slice(first * HSIZE, (first + group) * HSIZE)
        vmany = slice(width + first * HSIZE, width + (first + group) * HSIZE)
        keys = dot(states, r.wts[:, many], ((1,), (0,))).astype(BF)
        values = dot(states, r.wts[:, vmany], ((1,), (0,))).astype(BF)
        heads = range(group)
        local = [slice(h * HSIZE, (h + 1) * HSIZE) for h in heads]
        cols = [slice((first + h) * HSIZE, (first + h + 1) * HSIZE) for h in heads]
        vcols = [slice(width + (first + h) * HSIZE, width + (first + h + 1) * HSIZE) for h in heads]
        q = [r.qblk[:, cols[h]] for h in heads]
        g = [r.gblk[:, cols[h]] for h in heads]
        k = [keys[:, local[h]] for h in heads]
        v = [values[:, local[h]] for h in heads]
        scores = [dot(q[h], k[h], ((1,), (1,))) * scale for h in heads]
        dprob = [dot(g[h], v[h], ((1,), (1,))) for h in heads]
        expo = [jnp.exp(t - jnp.max(t, axis=-1, keepdims=True)) for t in scores]
        prob = [t * (1.0 / jnp.sum(t, axis=-1, keepdims=True)) for t in expo]
        rowdot = [jnp.sum(prob[h] * dprob[h], axis=-1, keepdims=True) for h in heads]
        dscore = [(prob[h] * (dprob[h] - rowdot[h]) * scale).astype(BF) for h in heads]
        prob_b = [t.astype(BF) for t in prob]
        for h in heads:
            r.owin[u, :, cols[h]] = dot(prob_b[h], v[h], ((1,), (0,))).astype(BF)
            r.dwin[u, :, cols[h]] = dot(dscore[h], k[h], ((1,), (0,))).astype(BF)
        for h in heads:
            r.both[rows, cols[h]] = dot(dscore[h], q[h], ((0,), (0,))).astype(BF)
            r.both[rows, vcols[h]] = dot(prob_b[h], g[h], ((0,), (0,))).astype(BF)


def kernel(plan, *refs):
    r = SimpleNamespace(**dict(zip(plan["names"], refs)))
    fused, asks, neigh, slots = plan["fused"], plan["asks"], plan["neigh"], plan["slots"]
    piece = plan["piece"]
    count = asks // neigh
    dp, db = lax.axis_index("dp"), lax.axis_index("db")
    shards = r.recv0.shape[0]
    nb_len = r.recv0.shape[1]
    base = r.dbv.shape[0]
    enc, wide = r.wts.shape
    half = wide // 2
    span = neigh * nb_len
    window = r.qblk.shape[0]
    recvs = [r.recv0, r.recv1, r.recv2]

    c, x = lax.rem(db, 2), db // 2
    core, far = db + 1 - 2 * c, db + 2 - 4 * x
    cross = far + 1 - 2 * c
    near = [(dp, far), (dp, cross), (dp, core)]
    after, before = (dp, lax.rem(db + 1, shards)), (dp, lax.rem(db + shards - 1, shards))
    seqs = lax.axis_size("dp")
    others = [(lax.rem(dp + d, seqs), db) for d in range(1, seqs)] if fused else []

    loads = [
        pltpu.make_async_copy(r.db_any, r.dbv, r.load_sem.at[0]),
        pltpu.make_async_copy(r.q_any, r.qwin.at[0:count], r.load_sem.at[1]),
        pltpu.make_async_copy(r.g_any, r.gwin.at[0:count], r.load_sem.at[2]),
        pltpu.make_async_copy(r.wk_any, r.wts.at[:, 0:half], r.load_sem.at[3]),
        pltpu.make_async_copy(r.wv_any, r.wts.at[:, half:wide], r.load_sem.at[4]),
        pltpu.make_async_copy(r.shuffle_any, r.shuffle, r.load_sem.at[5]),
    ]
    for load in loads:
        load.start()
    barrier = pltpu.get_barrier_semaphore()
    for peer in near + others:
        pl.semaphore_signal(barrier, inc=1, device_id=peer, device_id_type=MESH)

    def flag(condition):
        return condition.astype(jnp.int32)

    named_shard = [[r.shard_ref[n, u] for n in range(neigh)] for u in range(count)]
    named_row = [[r.row_ref[n, u] for n in range(neigh)] for u in range(count)]
    flat = [t for pair in named_shard for t in pair]
    crowded = [
        sum(flag(sum(flag(other == t) for other in flat) >= slots) for t in pair)
        for pair in named_shard
    ]
    total = sum(crowded)
    open_, is_last = jnp.int32(1), []
    for u in range(count):
        chosen = open_ * flag(crowded[u] * slots == total)
        is_last.append(chosen)
        open_ = open_ - chosen
    order, target, wanted = [], [], []

    def swapped(values, u):
        if u < count - 1:
            return values[u] + is_last[u] * (values[count - 1] - values[u])
        return sum(is_last[v] * values[v] for v in range(count))

    for u in range(count):
        order.append(swapped(list(range(count)), u))
        r.order_sm[u] = order[u]
        for n in range(neigh):
            target.append(swapped([pair[n] for pair in named_shard], u))
            wanted.append(swapped([pair[n] for pair in named_row], u))
    rank = []
    for a in range(asks):
        seen = jnp.int32(0)
        for b in range(a):
            seen = seen + flag(target[b] == target[a])
        rank.append(seen)
        r.rank_sm[a] = seen
        r.shard_sm[a] = target[a]
    row = lax.broadcasted_iota(jnp.int32, (8, 128), 0)
    lane = lax.broadcasted_iota(jnp.int32, (8, 128), 1)
    mine = jnp.zeros((8, 128), jnp.int32)
    for a in range(asks):
        mine = jnp.where((row == target[a]) & (lane == rank[a]), wanted[a], mine)
    r.asksend[...] = mine
    r.askbox[db] = mine

    def remote(src, dst, send_sem, recv_sem, peer):
        return pltpu.make_async_remote_copy(
            src_ref=src,
            dst_ref=dst,
            send_sem=send_sem,
            recv_sem=recv_sem,
            device_id=peer,
            device_id_type=MESH,
        )

    asked = [
        remote(r.asksend, r.askbox.at[db], r.ask_send.at[d], r.ask_recv.at[d], near[d])
        for d in range(3)
    ]
    edges = [
        remote(src.at[0], dst.at[count], r.edge_send.at[e], r.edge_recv.at[e], before)
        for e, (src, dst) in enumerate(((r.q_any, r.qwin), (r.g_any, r.gwin)))
    ]
    pl.semaphore_wait(barrier, len(near) + len(others))
    for copy in asked + edges:
        copy.start()

    own = jnp.zeros((8, 128), jnp.int32)
    for a in range(asks):
        own = jnp.where(lane // plan["unit"] == a, target[a] * base + wanted[a], own)
    r.ids[...] = own
    if fused:
        r.idbox[dp] = own
        named = [
            remote(r.ids, r.idbox.at[dp], r.id_send.at[d], r.id_recv.at[d], peer)
            for d, peer in enumerate(others)
        ]
        for copy in named:
            copy.start()

    for copy in asked:
        copy.wait_recv()
    to_scalar = pltpu.make_async_copy(r.askbox, r.ask_sm, r.load_sem.at[6])
    to_scalar.start()
    to_scalar.wait()
    loads[0].wait()
    rounds = []

    def entry(asker, k):
        return r.dbv[r.ask_sm[asker, db, k]]

    for k in range(slots):
        for d, peer in enumerate(near):
            r.fetch[k * 3 + d] = entry(peer[1], k)
        recvs[k][db] = entry(db, k)
        rounds.append(
            [
                remote(
                    r.fetch.at[k * 3 + d],
                    recvs[k].at[db],
                    r.fetch_send.at[k * 3 + d],
                    r.fetch_recv.at[k * 3 + d],
                    near[d],
                )
                for d in range(3)
            ]
        )
        if k == 0:
            for copy in rounds[0]:
                copy.start()
    if fused:
        block = r.gd_ref.shape[0]
        lanes = r.member.shape[1] // seqs
        for copy in named:
            copy.wait_recv()
        row = lax.broadcasted_iota(jnp.int32, (block, lanes), 0)
        lane = lax.broadcasted_iota(jnp.int32, (block, lanes), 1)
        place = jnp.where(row % piece == lane % piece, row // piece, -1)

        @pl.loop(0, shards)
        def _(i):
            rows = pl.ds(pl.multiple_of(i * block, block), block)
            for k in range(seqs):
                hit = place == r.idbox[k][0:1] - i * (block // piece)
                r.member[rows, k * lanes : (k + 1) * lanes] = jnp.where(
                    hit & (place >= 0), 1.0, 0.0
                ).astype(BF)

    for load in loads[1:]:
        load.wait()
    for copy in edges:
        copy.wait_recv()

    @pl.when(db == shards - 1)
    def _():
        r.qwin[count] = jnp.zeros((window, half), BF)
        r.gwin[count] = jnp.zeros((window, half), BF)


    cuts = plan["cuts"]

    def across(u, d):
        start = pl.multiple_of(u * neigh * piece, neigh * piece)
        rows = pl.ds(start, neigh * piece)
        return remote(
            r.dbv.at[others[d][0], rows],
            r.arrived.at[dp, rows],
            r.across_send.at[u, d],
            r.across_recv.at[u, d],
            others[d],
        )

    last = lax.broadcasted_iota(jnp.int32, (16, half), 0) == 15

    @pl.loop(0, count)
    def _(u):
        def pick(levels):
            for n in range(neigh):
                a = u * neigh + n
                t, level = r.shard_sm[a], r.rank_sm[a]
                block = recvs[levels - 1][t]
                for j in range(levels - 1):
                    block = choose(level, j, recvs[j][t], block)
                r.states[n * nb_len : (n + 1) * nb_len] = block

        @pl.when(u == 0)
        def _():
            for copy in rounds[0]:
                copy.wait_recv()
            for copy in rounds[1]:
                copy.start()
            pick(1)

        @pl.when(u == 1)
        def _():
            for copy in rounds[1]:
                copy.wait_recv()
            for copy in rounds[2]:
                copy.start()

        @pl.when((u > 0) & (u < count - 1))
        def _():
            pick(2)

        @pl.when(u == count - 1)
        def _():
            for copy in rounds[2]:
                copy.wait_recv()
            pick(3)

        place = r.order_sm[u]
        for win, blk in ((r.qwin, r.qblk), (r.gwin, r.gblk)):
            tail = slice(window - 16, window)
            blk[0 : window - 16] = win[place + 1, 0 : window - 16]
            blk[tail] = jnp.where(
                last, win[place, tail].astype(F32), win[place + 1, tail].astype(F32)
            ).astype(BF)

        states = r.states[...]
        r.lt[:, pl.ds(pl.multiple_of(u * span, span), span)] = dot(
            r.shuffle[...], states, ((1,), (1,))
        ).astype(BF)
        attend(r, u, states, 16)

        if fused:
            rows = pl.ds(pl.multiple_of(u * span, span), span)
            for h, cols in enumerate(cuts):
                out = dot(r.both[rows], r.wts[cols], ((1,), (1,))).astype(BF)
                for n in range(neigh):
                    for j in range(seqs):
                        into = pl.ds(pl.multiple_of((u * neigh + n) * piece, piece), piece)
                        start = n * nb_len + j * piece
                        r.dbv[j, into, cols] = out[start : start + piece]
                part = pl.ds(pl.multiple_of(u * neigh * piece, neigh * piece), neigh * piece)
                r.arrived[dp, part, cols] = r.dbv[dp, part, cols]
            for d in range(len(others)):
                across(u, d).start()

    r.qblk[...] = r.owin[r.order_sm[count - 1]]
    r.gblk[...] = r.dwin[r.order_sm[count - 1]]
    passed = [
        remote(blk, got, r.edge_send.at[2 + e], r.edge_recv.at[2 + e], after)
        for e, (blk, got) in enumerate(((r.qblk, r.oprev), (r.gblk, r.dprev)))
    ]
    for copy in passed:
        copy.start()

    def edge_outputs():
        writes = []
        for e, (win, got, full, out) in enumerate(
            ((r.owin, r.oprev, r.qwin, r.out_any), (r.dwin, r.dprev, r.gwin, r.dq_any))
        ):
            head, tail = slice(0, window - 16), slice(window - 16, window)
            for w in range(1, count):
                mine, back = r.order_sm[w], r.order_sm[w - 1]
                full[w, head] = win[back, head]
                full[w, tail] = jnp.where(
                    last, win[mine, tail].astype(F32), win[back, tail].astype(F32)
                ).astype(BF)
            passed[e].wait_recv()
            keep = jnp.where(db > 0, 1.0, 0.0)
            full[0, head] = (got[head].astype(F32) * keep).astype(BF)
            full[0, tail] = jnp.where(
                last, win[r.order_sm[0], tail].astype(F32), got[tail].astype(F32) * keep
            ).astype(BF)
            writes.append(pltpu.make_async_copy(full.at[0:count], out, r.load_sem.at[7 + e]))
            writes[-1].start()
        return writes

    sent = asked + edges + passed + [copy for part in rounds for copy in part]
    if fused:
        finish(r, plan, remote, across, others, named, edge_outputs, sent)
        return
    writes = edge_outputs()
    for n, (src, dst) in enumerate(((r.both, r.both_any), (r.lt, r.lt_any))):
        writes.append(pltpu.make_async_copy(src, dst, r.load_sem.at[9 + n]))
        writes[-1].start()
    for copy in writes:
        copy.wait()
    for copy in sent:
        copy.wait_send()


def finish(r, plan, remote, across, others, named, edge_outputs, sent):
    piece = plan["piece"]
    cuts = plan["cuts"]
    dp, db = lax.axis_index("dp"), lax.axis_index("db")
    seqs = r.arrived.shape[0]
    enc, wide = r.wts.shape
    half = wide // 2
    quarter = enc // 8
    c, x = lax.rem(db, 2), db // 2
    y, z0, z1 = lax.rem(dp, 2), lax.rem(dp // 2, 2), dp // 4
    pc = (dp, db + 1 - 2 * c)
    px = (dp, db + 2 - 4 * x)
    py = (dp + 1 - 2 * y, db)
    pz0 = (dp + 2 - 4 * z0, db)
    pz1 = (dp + 4 - 8 * z1, db)
    copies = []
    tile = 512

    def send(src, dst, peer):
        number = len(copies)
        copy = remote(src, dst, r.send_sem.at[number], r.recv_sem.at[number], peer)
        copy.start()
        copies.append(copy)
        return copy

    chunks = plan["chunks"]

    def part(p, row, n=1):
        rows = pl.ds(pl.multiple_of(row * quarter, quarter), n * quarter)
        return r.both.at[rows, chunks[p]]

    def weight_grad(p):
        start, stop = chunks[p].start, chunks[p].stop

        @pl.loop(0, (stop - start) // tile)
        def _(t):
            cols = pl.ds(pl.multiple_of(start + t * tile, tile), tile)
            out = jnp.dot(r.lt[...], r.both[:, cols], preferred_element_type=F32)
            r.both[0:enc, cols] = out.astype(BF)

        return send(part(p, (1 - c) * 4, 4), r.got1.at[:, chunks[p]], pc)

    def join(p, row, got):
        here = part(p, row)
        here[...] = add(here[...], got)

    def rows_of(i, n=1):
        return slice(i * quarter, (i + n) * quarter)

    def after_core(p, copy):
        copy.wait_recv()
        for i in range(4):
            join(p, c * 4 + i, r.got1[rows_of(i), chunks[p]])

    def first(p):
        if p % 2 == 0:
            src = part(p, c * 4 + (1 - y) * 2, 2)
            return [send(src, r.got2.at[:, chunks[p]], py)]
        return [
            send(part(p, c * 4 + i * 2 + 1 - z0), r.got2.at[rows_of(i), chunks[p]], pz0)
            for i in range(2)
        ]

    def second(p, arrivals):
        for copy in arrivals:
            copy.wait_recv()
        for i in range(2):
            into = c * 4 + y * 2 + i if p % 2 == 0 else c * 4 + i * 2 + z0
            join(p, into, r.got2[rows_of(i), chunks[p]])
        if p % 2 == 0:
            return send(part(p, c * 4 + y * 2 + 1 - z0), r.got3.at[:, chunks[p]], pz0)
        return send(part(p, c * 4 + (1 - y) * 2 + z0), r.got3.at[:, chunks[p]], py)

    def third(p, copy):
        copy.wait_recv()
        total = add(part(p, c * 4 + y * 2 + z0)[...], r.got3[:, chunks[p]])
        _, _, padded, _ = r.zed.shape
        r.zed[:, :, :, chunks[p]] = (
            jnp.dot(r.spread_ref[...], total, preferred_element_type=F32)
            .astype(BF)
            .reshape(2, 2, padded, total.shape[1])
        )
        return send(r.zed.at[1 - x, :, :, chunks[p]], r.got4.at[:, :, chunks[p]], px)

    def fourth(p, copy):
        copy.wait_recv()
        for j in range(2):
            r.zed[x, j, :, chunks[p]] = add(
                r.zed[x, j, :, chunks[p]], r.got4[j, :, chunks[p]]
            )
        return send(r.zed.at[x, 1 - z1, :, chunks[p]], r.got5.at[:, chunks[p]], pz1)

    def fifth(p, copy):
        copy.wait_recv()
        start, stop = chunks[p].start, chunks[p].stop
        out_ref, back = (r.gk_ref, 0) if start < half else (r.gv_ref, half)
        summed = r.zed[x, z1, :, chunks[p]].astype(F32) + r.got5[:, chunks[p]].astype(F32)
        out_ref[:, start - back : stop - back] = summed[: out_ref.shape[0]]

    block = r.gd_ref.shape[0]
    every = r.arrived.shape[0] * r.arrived.shape[1]
    count = r.across_send.shape[0]

    def dense(shard, cols):
        return jnp.dot(
            r.member[pl.ds(pl.multiple_of(shard * block, block), block)],
            r.arrived[:, :, cols].reshape(every, cols.stop - cols.start),
            preferred_element_type=F32,
        ).reshape(many, nb_len, cols.stop - cols.start)

    many, nb_len = r.dgot2.shape[0:2]
    give = [slice(seqs + n * many, seqs + (n + 1) * many) for n in range(3)]

    def give_side(h, far):
        cols = cuts[h]
        side = 1 - x if far else x
        r.dbv[give[far], :, cols] = dense(2 * side + 1 - c, cols).astype(BF)
        return send(r.dbv.at[give[far], :, cols], r.dgot1.at[far, :, :, cols], pc)

    def own_side(h, far):
        side = 1 - x if far else x
        r.mine[far, :, :, cuts[h]] = dense(2 * side + c, cuts[h])

    def x_start(h, copy):
        cols = cuts[h]
        copy.wait_recv()
        summed = r.mine[1, :, :, cols] + r.dgot1[1, :, :, cols].astype(F32)
        r.dbv[give[2], :, cols] = summed.astype(BF)
        return send(r.dbv.at[give[2], :, cols], r.dgot2.at[:, :, cols], px)

    pairs = len(chunks) // 2
    way = [None] * len(chunks)
    for p in range(len(chunks)):
        way[p] = weight_grad(p)
        if p > 0:
            after_core(p - 1, way[p - 1])
            if p - 1 < 2 * 2:
                way[p - 1] = first(p - 1)
    after_core(len(chunks) - 1, way[-1])
    if len(chunks) - 1 < 2 * 2:
        way[-1] = first(len(chunks) - 1)
    writes = edge_outputs()
    for u in range(count):
        for d in range(len(others)):
            across(u, d).wait_recv()
    far_side, xcopy = [], []
    for h in range(len(cuts)):
        far_side.append(give_side(h, 1))
        if h > 0:
            xcopy.append(x_start(h - 1, far_side[h - 1]))
        own_side(h, 1)
    xcopy.append(x_start(len(cuts) - 1, far_side[-1]))
    near_side = []
    for h in range(len(cuts)):
        near_side.append(give_side(h, 0))
        own_side(h, 0)
    for i in range(pairs):
        for p in (2 * i, 2 * i + 1):
            way[p] = second(p, way[p])
        if i + 2 < pairs:
            for p in (2 * i, 2 * i + 1):
                way[p + 2 * 2] = first(p + 2 * 2)
        if i > 0:
            for p in (2 * i - 2, 2 * i - 1):
                way[p] = third(p, way[p])
        if i > 1:
            for p in (2 * i - 4, 2 * i - 3):
                way[p] = fourth(p, way[p])
    ends = (len(chunks) - 2, len(chunks) - 1)
    for p in ends:
        way[p] = third(p, way[p])
    if pairs > 1:
        for p in (ends[0] - 2, ends[0] - 1):
            way[p] = fourth(p, way[p])
    for h, cols in enumerate(cuts):
        near_side[h].wait_recv()
        xcopy[h].wait_recv()
        summed = r.mine[0, :, :, cols] + r.dgot1[0, :, :, cols].astype(F32)
        summed = summed + r.dgot2[:, :, cols].astype(F32)
        r.gd_ref[:, cols] = summed.astype(BF).reshape(block, cols.stop - cols.start)
    for p in ends:
        way[p] = fourth(p, way[p])
    for p in range(len(chunks)):
        fifth(p, way[p])
    for copy in copies + named + sent:
        copy.wait_send()
    for u in range(count):
        for d in range(len(others)):
            across(u, d).wait_send()
    for copy in writes:
        copy.wait()


def settle_kernel(count, pieces, *refs):
    sources, targets, held = refs[:count], refs[count : 2 * count], refs[2 * count : 3 * count]
    in_sem, out_sem = refs[3 * count :]
    loads, stores = [], []
    for src, dst, mid in zip(sources, targets, held):
        size = src.shape[0]
        cut = pieces if len(src.shape) == 3 else 1
        step = size // cut
        for i in range(cut):
            rows = pl.ds(i * step, step)
            n = len(loads)
            loads.append(pltpu.make_async_copy(src.at[rows], mid.at[rows], in_sem.at[n]))
            stores.append(pltpu.make_async_copy(mid.at[rows], dst.at[rows], out_sem.at[n]))
    for copy in loads:
        copy.start()
    for load, store in zip(loads, stores):
        load.wait()
        store.start()
    for copy in stores:
        copy.wait()


def settle(results):
    anywhere = pl.BlockSpec(memory_space=pl.ANY)
    sem = pltpu.SemaphoreType.DMA((4 * len(results),))
    return pl.pallas_call(
        functools.partial(settle_kernel, len(results), 4),
        in_specs=[anywhere] * len(results),
        out_specs=[anywhere] * len(results),
        out_shape=[jax.ShapeDtypeStruct(a.shape, a.dtype) for a in results],
        scratch_shapes=[pltpu.VMEM(a.shape, a.dtype) for a in results] + [sem, sem],
        compiler_params=pltpu.CompilerParams(vmem_limit_bytes=62 << 20),
    )(*results)


def reversed_order(count):
    bits = count.bit_length() - 1
    return np.array([int(format(i, "b").zfill(bits)[::-1], 2) if bits else 0 for i in range(count)])


def run(queries, cotangent, w_key, w_value, database, nb_shard, nb_row):
    shards, seqs = lax.axis_size("db"), lax.axis_size("dp")
    _, rows, width = queries.shape
    _, count, neigh = nb_shard.shape
    base, nb_len, enc = database.shape
    window = rows // count
    asks = count * neigh
    slots = 3 * asks // (2 * shards)
    fused = shards == 4 and seqs == 8
    devices = shards * seqs
    share = enc // devices
    piece = nb_len // seqs
    wide = 2 * width
    quarter = enc // 8
    padded = -(-share // 16) * 16
    block = base * piece
    order = reversed_order(devices)
    if fused:
        bits = np.arange(devices)[:, None] // np.array([16, 8, 4, 2, 1])[None, :] % 2
        order = bits @ np.array([1, 4, 8, 2, 16])
    chunks, start = [], 0
    for size in (8, 8):
        size = size * width // 16
        for first in (0, width):
            chunks.append(slice(first + start, first + start + size))
        start += size
    source = (order[:, None] * share + np.arange(share)[None, :]).reshape(-1)
    shuffle = (source[:, None] == np.arange(enc)[None, :]).astype(jnp.bfloat16)
    cuts = [slice(0, 256), slice(256, 512), slice(512, enc)]

    anywhere = pl.BlockSpec(memory_space=pl.ANY)
    vmem = pl.BlockSpec(memory_space=pltpu.VMEM)
    smem = pl.BlockSpec(memory_space=pltpu.SMEM)
    sem = pltpu.SemaphoreType.DMA
    names, inputs, specs = [], [], []

    def give(name, value, spec):
        names.append(name)
        inputs.append(value)
        specs.append(spec)

    give("shard_ref", nb_shard[0].T, smem)
    give("row_ref", nb_row[0].T, smem)
    give("q_any", queries.reshape(count, window, width), anywhere)
    give("g_any", cotangent.reshape(count, window, width), anywhere)
    give("wk_any", w_key, anywhere)
    give("wv_any", w_value, anywhere)
    give("db_any", database, anywhere)
    give("shuffle_any", jnp.asarray(shuffle), anywhere)
    if fused:
        row = np.arange(4 * padded)[:, None]
        col = np.arange(4 * share)[None, :]
        spread = (row // padded == col // share) & (row % padded == col % share)
        give("spread_ref", jnp.asarray(spread.astype(jnp.bfloat16)), vmem)

    outs = [
        ("out_any", (count, window, width), BF, anywhere),
        ("dq_any", (count, window, width), BF, anywhere),
    ]
    if fused:
        outs += [
            ("gk_ref", (share, width), F32, vmem),
            ("gv_ref", (share, width), F32, vmem),
            ("gd_ref", (block, enc), BF, vmem),
        ]
    else:
        outs += [
            ("both_any", (asks * nb_len, wide), BF, anywhere),
            ("lt_any", (enc, asks * nb_len), BF, anywhere),
            ("ids", (8, 128), jnp.int32, vmem),
        ]
    scratch = [
        ("dbv", pltpu.VMEM((base, nb_len, enc), BF)),
        ("qwin", pltpu.VMEM((count + 1, window, width), BF)),
        ("gwin", pltpu.VMEM((count + 1, window, width), BF)),
        ("owin", pltpu.VMEM((count, window, width), BF)),
        ("dwin", pltpu.VMEM((count, window, width), BF)),
        ("oprev", pltpu.VMEM((window, width), BF)),
        ("dprev", pltpu.VMEM((window, width), BF)),
        ("qblk", pltpu.VMEM((window, width), BF)),
        ("gblk", pltpu.VMEM((window, width), BF)),
        ("wts", pltpu.VMEM((enc, wide), BF)),
        ("shuffle", pltpu.VMEM((enc, enc), BF)),
        ("states", pltpu.VMEM((neigh * nb_len, enc), BF)),
        ("both", pltpu.VMEM((asks * nb_len, wide), BF)),
        ("lt", pltpu.VMEM((enc, asks * nb_len), BF)),
        ("fetch", pltpu.VMEM((slots * 3, nb_len, enc), BF)),
        ("recv0", pltpu.VMEM((shards, nb_len, enc), BF)),
        ("recv1", pltpu.VMEM((shards, nb_len, enc), BF)),
        ("recv2", pltpu.VMEM((shards, nb_len, enc), BF)),
        ("asksend", pltpu.VMEM((8, 128), jnp.int32)),
        ("askbox", pltpu.VMEM((shards, 8, 128), jnp.int32)),
        ("ask_sm", pltpu.SMEM((shards, 8, 128), jnp.int32)),
        ("rank_sm", pltpu.SMEM((asks,), jnp.int32)),
        ("shard_sm", pltpu.SMEM((asks,), jnp.int32)),
        ("order_sm", pltpu.SMEM((count,), jnp.int32)),
        ("load_sem", sem((12,))),
        ("ask_send", sem((3,))),
        ("ask_recv", sem((3,))),
        ("edge_send", sem((4,))),
        ("edge_recv", sem((4,))),
        ("fetch_send", sem((slots * 3,))),
        ("fetch_recv", sem((slots * 3,))),
    ]
    if fused:
        peers = seqs - 1
        scratch += [
            ("ids", pltpu.VMEM((8, 128), jnp.int32)),
            ("idbox", pltpu.VMEM((seqs, 8, 128), jnp.int32)),
            ("member", pltpu.VMEM((shards * block, seqs * asks * piece), BF)),
            ("got1", pltpu.VMEM((4 * quarter, wide), BF)),
            ("got2", pltpu.VMEM((2 * quarter, wide), BF)),
            ("got3", pltpu.VMEM((quarter, wide), BF)),
            ("zed", pltpu.VMEM((2, 2, padded, wide), BF)),
            ("got4", pltpu.VMEM((2, padded, wide), BF)),
            ("got5", pltpu.VMEM((padded, wide), BF)),
            ("arrived", pltpu.VMEM((seqs, asks * piece, enc), BF)),
            ("dgot1", pltpu.VMEM((2, block // nb_len, nb_len, enc), BF)),
            ("mine", pltpu.VMEM((2, block // nb_len, nb_len, enc), F32)),
            ("dgot2", pltpu.VMEM((block // nb_len, nb_len, enc), BF)),
            ("send_sem", sem((64,))),
            ("recv_sem", sem((64,))),
            ("across_send", sem((count, peers))),
            ("across_recv", sem((count, peers))),
            ("id_send", sem((peers,))),
            ("id_recv", sem((peers,))),
        ]
    names += [o[0] for o in outs] + [s[0] for s in scratch]
    plan = dict(
        names=names, fused=fused, asks=asks, neigh=neigh, slots=slots, piece=piece, cuts=cuts,
        chunks=chunks, unit=piece if fused else 1,
    )
    results = pl.pallas_call(
        functools.partial(kernel, plan),
        in_specs=specs,
        out_specs=[o[3] for o in outs],
        out_shape=[jax.ShapeDtypeStruct(o[1], o[2]) for o in outs],
        scratch_shapes=[s[1] for s in scratch],
        compiler_params=pltpu.CompilerParams(
            vmem_limit_bytes=62 << 20, collective_id=0, has_side_effects=True
        ),
        cost_estimate=pl.CostEstimate(
            flops=28 * 10**9, bytes_accessed=40 << 20, transcendentals=1 << 20
        ),
    )(*inputs)
    if fused:
        results = settle(results)
    attn_out = results[0].reshape(1, rows, width)
    grad_queries = results[1].reshape(1, rows, width)
    if fused:
        grad_database = results[4].reshape(base, piece, enc)
        return (attn_out, grad_queries, results[2], results[3], grad_database)

    both, lt, own_ids = results[2:]
    ids = jnp.broadcast_to(own_ids[0:1, 0:asks], (seqs, asks))
    ids = lax.all_to_all(ids, "dp", split_axis=0, concat_axis=0, tiled=True)
    ids = ids.reshape(seqs * asks)
    member = (ids[None, :] == jnp.arange(shards * base, dtype=jnp.int32)[:, None]).astype(BF)
    steps = [("db", b) for b in bits_of("db")] + [("dp", b) for b in bits_of("dp")]
    grads = []
    for part in range(2):
        grad = dot(lt, both[:, part * width : (part + 1) * width], ((1,), (0,)))
        grads.append(halve_all(grad.astype(BF), steps))
    w_both = jnp.concatenate([w_key, w_value], axis=1)
    dstates = dot(both, w_both, ((1,), (1,))).astype(BF)
    dstates = dstates.reshape(asks, seqs, piece, enc).transpose(1, 0, 2, 3)
    arrived = lax.all_to_all(dstates, "dp", split_axis=0, concat_axis=0, tiled=True)
    dense = dot(member, arrived.reshape(seqs * asks, piece * enc), ((1,), (0,)))
    dense = dense.astype(BF).reshape(shards, base, piece, enc)
    dense = jnp.stack([dense[i] for i in reversed_order(shards)])
    grad_database = halve_all(dense, [("db", b) for b in bits_of("db")])[0].astype(BF)
    return (attn_out, grad_queries, grads[0], grads[1], grad_database)


def halve(block, axis, bit):
    size = lax.axis_size(axis)
    half = block.shape[0] // 2
    side = lax.rem(lax.axis_index(axis) // bit, 2)
    give = lax.dynamic_slice_in_dim(block, (1 - side) * half, half, 0)
    mine = lax.dynamic_slice_in_dim(block, side * half, half, 0)
    got = lax.ppermute(give, axis, [(i, i ^ bit) for i in range(size)])
    return mine.astype(F32) + got.astype(F32)


def bits_of(axis):
    size = lax.axis_size(axis)
    return [1 << b for b in range(size.bit_length() - 1)]


def halve_all(block, steps):
    for axis, bit in steps[:-1]:
        block = halve(block, axis, bit).astype(BF)
    return halve(block, *steps[-1])


def solution(mesh):
    return jax.shard_map(
        run,
        mesh=mesh,
        in_specs=(
            P("dp", "db", None),
            P("dp", "db", None),
            P(),
            P(),
            P("db", None, None),
            P("dp", "db", None),
            P("dp", "db", None),
        ),
        out_specs=(
            P("dp", "db", None),
            P("dp", "db", None),
            P(("dp", "db"), None),
            P(("dp", "db"), None),
            P("db", "dp", None),
        ),
        check_vma=False,
    )
```

```python
import functools
import math
from types import SimpleNamespace

import jax
import jax.numpy as jnp
import numpy as np
from jax import lax
from jax.experimental import pallas as pl
from jax.experimental.pallas import tpu as pltpu
from jax.sharding import PartitionSpec as P

HSIZE = 128
BF, F32 = jnp.bfloat16, jnp.float32
MESH = pl.DeviceIdType.MESH


def dot(a, b, dims):
    return lax.dot_general(a, b, (dims, ((), ())), preferred_element_type=F32)


def choose(level, wanted, a, b):
    same = jnp.full(a.shape, level, jnp.int32) == wanted
    return jnp.where(same, a.astype(F32), b.astype(F32)).astype(BF)


def add(a, b):
    return (a.astype(F32) + b.astype(F32)).astype(BF)


def attend(r, u, states, group):
    width = r.qblk.shape[1]
    span = states.shape[0]
    scale = 1.0 / math.sqrt(HSIZE)
    rows = pl.ds(pl.multiple_of(u * span, span), span)
    for first in range(0, width // HSIZE, group):
        many = slice(first * HSIZE, (first + group) * HSIZE)
        vmany = slice(width + first * HSIZE, width + (first + group) * HSIZE)
        keys = dot(states, r.wts[:, many], ((1,), (0,))).astype(BF)
        values = dot(states, r.wts[:, vmany], ((1,), (0,))).astype(BF)
        heads = range(group)
        local = [slice(h * HSIZE, (h + 1) * HSIZE) for h in heads]
        cols = [slice((first + h) * HSIZE, (first + h + 1) * HSIZE) for h in heads]
        vcols = [slice(width + (first + h) * HSIZE, width + (first + h + 1) * HSIZE) for h in heads]
        q = [r.qblk[:, cols[h]] for h in heads]
        g = [r.gblk[:, cols[h]] for h in heads]
        k = [keys[:, local[h]] for h in heads]
        v = [values[:, local[h]] for h in heads]
        scores = [dot(q[h], k[h], ((1,), (1,))) * scale for h in heads]
        dprob = [dot(g[h], v[h], ((1,), (1,))) for h in heads]
        expo = [jnp.exp(t - jnp.max(t, axis=-1, keepdims=True)) for t in scores]
        prob = [t * (1.0 / jnp.sum(t, axis=-1, keepdims=True)) for t in expo]
        rowdot = [jnp.sum(prob[h] * dprob[h], axis=-1, keepdims=True) for h in heads]
        dscore = [(prob[h] * (dprob[h] - rowdot[h]) * scale).astype(BF) for h in heads]
        prob_b = [t.astype(BF) for t in prob]
        for h in heads:
            r.owin[u, :, cols[h]] = dot(prob_b[h], v[h], ((1,), (0,))).astype(BF)
            r.dwin[u, :, cols[h]] = dot(dscore[h], k[h], ((1,), (0,))).astype(BF)
        for h in heads:
            r.both[rows, cols[h]] = dot(dscore[h], q[h], ((0,), (0,))).astype(BF)
            r.both[rows, vcols[h]] = dot(prob_b[h], g[h], ((0,), (0,))).astype(BF)


def kernel(plan, *refs):
    r = SimpleNamespace(**dict(zip(plan["names"], refs)))
    fused, asks, neigh, slots = plan["fused"], plan["asks"], plan["neigh"], plan["slots"]
    piece = plan["piece"]
    count = asks // neigh
    dp, db = lax.axis_index("dp"), lax.axis_index("db")
    shards = r.recv0.shape[0]
    nb_len = r.recv0.shape[1]
    base = r.dbv.shape[0]
    enc, wide = r.wts.shape
    half = wide // 2
    span = neigh * nb_len
    window = r.qblk.shape[0]
    recvs = [r.recv0, r.recv1, r.recv2]

    c, x = lax.rem(db, 2), db // 2
    core, far = db + 1 - 2 * c, db + 2 - 4 * x
    cross = far + 1 - 2 * c
    near = [(dp, far), (dp, cross), (dp, core)]
    after, before = (dp, lax.rem(db + 1, shards)), (dp, lax.rem(db + shards - 1, shards))
    seqs = lax.axis_size("dp")
    others = [(lax.rem(dp + d, seqs), db) for d in range(1, seqs)] if fused else []

    loads = [
        pltpu.make_async_copy(r.db_any, r.dbv, r.load_sem.at[0]),
        pltpu.make_async_copy(r.q_any, r.qwin.at[0:count], r.load_sem.at[1]),
        pltpu.make_async_copy(r.g_any, r.gwin.at[0:count], r.load_sem.at[2]),
        pltpu.make_async_copy(r.wk_any, r.wts.at[:, 0:half], r.load_sem.at[3]),
        pltpu.make_async_copy(r.wv_any, r.wts.at[:, half:wide], r.load_sem.at[4]),
        pltpu.make_async_copy(r.shuffle_any, r.shuffle, r.load_sem.at[5]),
    ]
    for load in loads:
        load.start()
    barrier = pltpu.get_barrier_semaphore()
    for peer in near + others:
        pl.semaphore_signal(barrier, inc=1, device_id=peer, device_id_type=MESH)

    def flag(condition):
        return condition.astype(jnp.int32)

    named_shard = [[r.shard_ref[n, u] for n in range(neigh)] for u in range(count)]
    named_row = [[r.row_ref[n, u] for n in range(neigh)] for u in range(count)]
    flat = [t for pair in named_shard for t in pair]
    crowded = [
        sum(flag(sum(flag(other == t) for other in flat) >= slots) for t in pair)
        for pair in named_shard
    ]
    total = sum(crowded)
    open_, is_last = jnp.int32(1), []
    for u in range(count):
        chosen = open_ * flag(crowded[u] * slots == total)
        is_last.append(chosen)
        open_ = open_ - chosen
    order, target, wanted = [], [], []

    def swapped(values, u):
        if u < count - 1:
            return values[u] + is_last[u] * (values[count - 1] - values[u])
        return sum(is_last[v] * values[v] for v in range(count))

    for u in range(count):
        order.append(swapped(list(range(count)), u))
        r.order_sm[u] = order[u]
        for n in range(neigh):
            target.append(swapped([pair[n] for pair in named_shard], u))
            wanted.append(swapped([pair[n] for pair in named_row], u))
    rank = []
    for a in range(asks):
        seen = jnp.int32(0)
        for b in range(a):
            seen = seen + flag(target[b] == target[a])
        rank.append(seen)
        r.rank_sm[a] = seen
        r.shard_sm[a] = target[a]
    row = lax.broadcasted_iota(jnp.int32, (8, 128), 0)
    lane = lax.broadcasted_iota(jnp.int32, (8, 128), 1)
    mine = jnp.zeros((8, 128), jnp.int32)
    for a in range(asks):
        mine = jnp.where((row == target[a]) & (lane == rank[a]), wanted[a], mine)
    r.asksend[...] = mine
    r.askbox[db] = mine

    def remote(src, dst, send_sem, recv_sem, peer):
        return pltpu.make_async_remote_copy(
            src_ref=src,
            dst_ref=dst,
            send_sem=send_sem,
            recv_sem=recv_sem,
            device_id=peer,
            device_id_type=MESH,
        )

    asked = [
        remote(r.asksend, r.askbox.at[db], r.ask_send.at[d], r.ask_recv.at[d], near[d])
        for d in range(3)
    ]
    edges = [
        remote(src.at[0], dst.at[count], r.edge_send.at[e], r.edge_recv.at[e], before)
        for e, (src, dst) in enumerate(((r.q_any, r.qwin), (r.g_any, r.gwin)))
    ]
    pl.semaphore_wait(barrier, len(near) + len(others))
    for copy in asked + edges:
        copy.start()

    own = jnp.zeros((8, 128), jnp.int32)
    for a in range(asks):
        own = jnp.where(lane // plan["unit"] == a, target[a] * base + wanted[a], own)
    r.ids[...] = own
    if fused:
        r.idbox[dp] = own
        named = [
            remote(r.ids, r.idbox.at[dp], r.id_send.at[d], r.id_recv.at[d], peer)
            for d, peer in enumerate(others)
        ]
        for copy in named:
            copy.start()

    for copy in asked:
        copy.wait_recv()
    to_scalar = pltpu.make_async_copy(r.askbox, r.ask_sm, r.load_sem.at[6])
    to_scalar.start()
    to_scalar.wait()
    loads[0].wait()
    rounds = []

    def entry(asker, k):
        return r.dbv[r.ask_sm[asker, db, k]]

    for k in range(slots):
        for d, peer in enumerate(near):
            r.fetch[k * 3 + d] = entry(peer[1], k)
        recvs[k][db] = entry(db, k)
        rounds.append(
            [
                remote(
                    r.fetch.at[k * 3 + d],
                    recvs[k].at[db],
                    r.fetch_send.at[k * 3 + d],
                    r.fetch_recv.at[k * 3 + d],
                    near[d],
                )
                for d in range(3)
            ]
        )
        if k == 0:
            for copy in rounds[0]:
                copy.start()
    if fused:
        block = r.gd_ref.shape[0]
        lanes = r.member.shape[1] // seqs
        for copy in named:
            copy.wait_recv()
        row = lax.broadcasted_iota(jnp.int32, (block, lanes), 0)
        lane = lax.broadcasted_iota(jnp.int32, (block, lanes), 1)
        place = jnp.where(row % piece == lane % piece, row // piece, -1)

        @pl.loop(0, shards)
        def _(i):
            rows = pl.ds(pl.multiple_of(i * block, block), block)
            for k in range(seqs):
                hit = place == r.idbox[k][0:1] - i * (block // piece)
                r.member[rows, k * lanes : (k + 1) * lanes] = jnp.where(
                    hit & (place >= 0), 1.0, 0.0
                ).astype(BF)

    for load in loads[1:]:
        load.wait()
    for copy in edges:
        copy.wait_recv()

    @pl.when(db == shards - 1)
    def _():
        r.qwin[count] = jnp.zeros((window, half), BF)
        r.gwin[count] = jnp.zeros((window, half), BF)


    cuts = plan["cuts"]

    def across(u, d):
        start = pl.multiple_of(u * neigh * piece, neigh * piece)
        rows = pl.ds(start, neigh * piece)
        return remote(
            r.dbv.at[others[d][0], rows],
            r.arrived.at[dp, rows],
            r.across_send.at[u, d],
            r.across_recv.at[u, d],
            others[d],
        )

    last = lax.broadcasted_iota(jnp.int32, (16, half), 0) == 15

    @pl.loop(0, count)
    def _(u):
        def pick(levels):
            for n in range(neigh):
                a = u * neigh + n
                t, level = r.shard_sm[a], r.rank_sm[a]
                block = recvs[levels - 1][t]
                for j in range(levels - 1):
                    block = choose(level, j, recvs[j][t], block)
                r.states[n * nb_len : (n + 1) * nb_len] = block

        @pl.when(u == 0)
        def _():
            for copy in rounds[0]:
                copy.wait_recv()
            for copy in rounds[1]:
                copy.start()
            pick(1)

        @pl.when(u == 1)
        def _():
            for copy in rounds[1]:
                copy.wait_recv()
            for copy in rounds[2]:
                copy.start()

        @pl.when((u > 0) & (u < count - 1))
        def _():
            pick(2)

        @pl.when(u == count - 1)
        def _():
            for copy in rounds[2]:
                copy.wait_recv()
            pick(3)

        place = r.order_sm[u]
        for win, blk in ((r.qwin, r.qblk), (r.gwin, r.gblk)):
            tail = slice(window - 16, window)
            blk[0 : window - 16] = win[place + 1, 0 : window - 16]
            blk[tail] = jnp.where(
                last, win[place, tail].astype(F32), win[place + 1, tail].astype(F32)
            ).astype(BF)

        states = r.states[...]
        attend(r, u, states, 16)

        if fused:
            rows = pl.ds(pl.multiple_of(u * span, span), span)
            for h, cols in enumerate(cuts):
                out = dot(r.both[rows], r.wts[cols], ((1,), (1,))).astype(BF)
                for n in range(neigh):
                    for j in range(seqs):
                        into = pl.ds(pl.multiple_of((u * neigh + n) * piece, piece), piece)
                        start = n * nb_len + j * piece
                        r.dbv[j, into, cols] = out[start : start + piece]
                part = pl.ds(pl.multiple_of(u * neigh * piece, neigh * piece), neigh * piece)
                r.arrived[dp, part, cols] = r.dbv[dp, part, cols]
            for d in range(len(others)):
                across(u, d).start()
        r.lt[:, pl.ds(pl.multiple_of(u * span, span), span)] = dot(
            r.shuffle[...], states, ((1,), (1,))
        ).astype(BF)

    r.qblk[...] = r.owin[r.order_sm[count - 1]]
    r.gblk[...] = r.dwin[r.order_sm[count - 1]]
    passed = [
        remote(blk, got, r.edge_send.at[2 + e], r.edge_recv.at[2 + e], after)
        for e, (blk, got) in enumerate(((r.qblk, r.oprev), (r.gblk, r.dprev)))
    ]
    for copy in passed:
        copy.start()

    def edge_outputs():
        writes = []
        for e, (win, got, full, out) in enumerate(
            ((r.owin, r.oprev, r.qwin, r.out_any), (r.dwin, r.dprev, r.gwin, r.dq_any))
        ):
            head, tail = slice(0, window - 16), slice(window - 16, window)
            for w in range(1, count):
                mine, back = r.order_sm[w], r.order_sm[w - 1]
                full[w, head] = win[back, head]
                full[w, tail] = jnp.where(
                    last, win[mine, tail].astype(F32), win[back, tail].astype(F32)
                ).astype(BF)
            passed[e].wait_recv()
            keep = jnp.where(db > 0, 1.0, 0.0)
            full[0, head] = (got[head].astype(F32) * keep).astype(BF)
            full[0, tail] = jnp.where(
                last, win[r.order_sm[0], tail].astype(F32), got[tail].astype(F32) * keep
            ).astype(BF)
            writes.append(pltpu.make_async_copy(full.at[0:count], out, r.load_sem.at[7 + e]))
            writes[-1].start()
        return writes

    sent = asked + edges + passed + [copy for part in rounds for copy in part]
    if fused:
        finish(r, plan, remote, across, others, named, edge_outputs, sent)
        return
    writes = edge_outputs()
    for n, (src, dst) in enumerate(((r.both, r.both_any), (r.lt, r.lt_any))):
        writes.append(pltpu.make_async_copy(src, dst, r.load_sem.at[9 + n]))
        writes[-1].start()
    for copy in writes:
        copy.wait()
    for copy in sent:
        copy.wait_send()


def finish(r, plan, remote, across, others, named, edge_outputs, sent):
    piece = plan["piece"]
    cuts = plan["cuts"]
    dp, db = lax.axis_index("dp"), lax.axis_index("db")
    seqs = r.arrived.shape[0]
    enc, wide = r.wts.shape
    half = wide // 2
    quarter = enc // 8
    c, x = lax.rem(db, 2), db // 2
    y, z0, z1 = lax.rem(dp, 2), lax.rem(dp // 2, 2), dp // 4
    pc = (dp, db + 1 - 2 * c)
    px = (dp, db + 2 - 4 * x)
    py = (dp + 1 - 2 * y, db)
    pz0 = (dp + 2 - 4 * z0, db)
    pz1 = (dp + 4 - 8 * z1, db)
    copies = []
    tile = 512

    def send(src, dst, peer):
        number = len(copies)
        copy = remote(src, dst, r.send_sem.at[number], r.recv_sem.at[number], peer)
        copy.start()
        copies.append(copy)
        return copy

    chunks = plan["chunks"]

    def part(p, row, n=1):
        rows = pl.ds(pl.multiple_of(row * quarter, quarter), n * quarter)
        return r.both.at[rows, chunks[p]]

    def weight_grad(p):
        start, stop = chunks[p].start, chunks[p].stop

        @pl.loop(0, (stop - start) // tile)
        def _(t):
            cols = pl.ds(pl.multiple_of(start + t * tile, tile), tile)
            out = jnp.dot(r.lt[...], r.both[:, cols], preferred_element_type=F32)
            r.both[0:enc, cols] = out.astype(BF)

        return send(part(p, (1 - c) * 4, 4), r.got1.at[:, chunks[p]], pc)

    def join(p, row, got):
        here = part(p, row)
        here[...] = add(here[...], got)

    def rows_of(i, n=1):
        return slice(i * quarter, (i + n) * quarter)

    def after_core(p, copy):
        copy.wait_recv()
        for i in range(4):
            join(p, c * 4 + i, r.got1[rows_of(i), chunks[p]])

    def first(p):
        if p % 2 == 0:
            src = part(p, c * 4 + (1 - y) * 2, 2)
            return [send(src, r.got2.at[:, chunks[p]], py)]
        return [
            send(part(p, c * 4 + i * 2 + 1 - z0), r.got2.at[rows_of(i), chunks[p]], pz0)
            for i in range(2)
        ]

    def second(p, arrivals):
        for copy in arrivals:
            copy.wait_recv()
        for i in range(2):
            into = c * 4 + y * 2 + i if p % 2 == 0 else c * 4 + i * 2 + z0
            join(p, into, r.got2[rows_of(i), chunks[p]])
        if p % 2 == 0:
            return send(part(p, c * 4 + y * 2 + 1 - z0), r.got3.at[:, chunks[p]], pz0)
        return send(part(p, c * 4 + (1 - y) * 2 + z0), r.got3.at[:, chunks[p]], py)

    def third(p, copy):
        copy.wait_recv()
        total = add(part(p, c * 4 + y * 2 + z0)[...], r.got3[:, chunks[p]])
        _, _, padded, _ = r.zed.shape
        r.zed[:, :, :, chunks[p]] = (
            jnp.dot(r.spread_ref[...], total, preferred_element_type=F32)
            .astype(BF)
            .reshape(2, 2, padded, total.shape[1])
        )
        return send(r.zed.at[1 - x, :, :, chunks[p]], r.got4.at[:, :, chunks[p]], px)

    def fourth(p, copy):
        copy.wait_recv()
        for j in range(2):
            r.zed[x, j, :, chunks[p]] = add(
                r.zed[x, j, :, chunks[p]], r.got4[j, :, chunks[p]]
            )
        return send(r.zed.at[x, 1 - z1, :, chunks[p]], r.got5.at[:, chunks[p]], pz1)

    def fifth(p, copy):
        copy.wait_recv()
        start, stop = chunks[p].start, chunks[p].stop
        out_ref, back = (r.gk_ref, 0) if start < half else (r.gv_ref, half)
        summed = r.zed[x, z1, :, chunks[p]].astype(F32) + r.got5[:, chunks[p]].astype(F32)
        out_ref[:, start - back : stop - back] = summed[: out_ref.shape[0]]

    block = r.gd_ref.shape[0]
    every = r.arrived.shape[0] * r.arrived.shape[1]
    count = r.across_send.shape[0]

    def dense(shard, cols):
        return jnp.dot(
            r.member[pl.ds(pl.multiple_of(shard * block, block), block)],
            r.arrived[:, :, cols].reshape(every, cols.stop - cols.start),
            preferred_element_type=F32,
        ).reshape(many, nb_len, cols.stop - cols.start)

    many, nb_len = r.dgot2.shape[0:2]
    give = [slice(seqs + n * many, seqs + (n + 1) * many) for n in range(3)]

    def give_side(h, far):
        cols = cuts[h]
        side = 1 - x if far else x
        r.dbv[give[far], :, cols] = dense(2 * side + 1 - c, cols).astype(BF)
        return send(r.dbv.at[give[far], :, cols], r.dgot1.at[far, :, :, cols], pc)

    def own_side(h, far):
        side = 1 - x if far else x
        r.mine[far, :, :, cuts[h]] = dense(2 * side + c, cuts[h])

    def x_start(h, copy):
        cols = cuts[h]
        copy.wait_recv()
        summed = r.mine[1, :, :, cols] + r.dgot1[1, :, :, cols].astype(F32)
        r.dbv[give[2], :, cols] = summed.astype(BF)
        return send(r.dbv.at[give[2], :, cols], r.dgot2.at[:, :, cols], px)

    pairs = len(chunks) // 2
    way = [None] * len(chunks)
    for p in range(len(chunks)):
        way[p] = weight_grad(p)
        if p > 0:
            after_core(p - 1, way[p - 1])
            if p - 1 < 2 * 2:
                way[p - 1] = first(p - 1)
    after_core(len(chunks) - 1, way[-1])
    if len(chunks) - 1 < 2 * 2:
        way[-1] = first(len(chunks) - 1)
    writes = edge_outputs()
    for u in range(count):
        for d in range(len(others)):
            across(u, d).wait_recv()
    far_side, xcopy = [], []
    for h in range(len(cuts)):
        far_side.append(give_side(h, 1))
        if h > 0:
            xcopy.append(x_start(h - 1, far_side[h - 1]))
        own_side(h, 1)
    xcopy.append(x_start(len(cuts) - 1, far_side[-1]))
    near_side = []
    for h in range(len(cuts)):
        near_side.append(give_side(h, 0))
        own_side(h, 0)
    for i in range(pairs):
        for p in (2 * i, 2 * i + 1):
            way[p] = second(p, way[p])
        if i + 2 < pairs:
            for p in (2 * i, 2 * i + 1):
                way[p + 2 * 2] = first(p + 2 * 2)
        if i > 0:
            for p in (2 * i - 2, 2 * i - 1):
                way[p] = third(p, way[p])
        if i > 1:
            for p in (2 * i - 4, 2 * i - 3):
                way[p] = fourth(p, way[p])
    ends = (len(chunks) - 2, len(chunks) - 1)
    for p in ends:
        way[p] = third(p, way[p])
    if pairs > 1:
        for p in (ends[0] - 2, ends[0] - 1):
            way[p] = fourth(p, way[p])
    for h, cols in enumerate(cuts):
        near_side[h].wait_recv()
        xcopy[h].wait_recv()
        summed = r.mine[0, :, :, cols] + r.dgot1[0, :, :, cols].astype(F32)
        summed = summed + r.dgot2[:, :, cols].astype(F32)
        r.gd_ref[:, cols] = summed.astype(BF).reshape(block, cols.stop - cols.start)
    writes.append(pltpu.make_async_copy(r.gd_ref, r.gd_any, r.load_sem.at[9]))
    writes[-1].start()
    for p in ends:
        way[p] = fourth(p, way[p])
    for p in range(len(chunks)):
        fifth(p, way[p])
    for copy in copies + named + sent:
        copy.wait_send()
    for u in range(count):
        for d in range(len(others)):
            across(u, d).wait_send()
    for copy in writes:
        copy.wait()


def settle_kernel(count, pieces, *refs):
    sources, targets, held = refs[:count], refs[count : 2 * count], refs[2 * count : 3 * count]
    in_sem, out_sem = refs[3 * count :]
    loads, stores = [], []
    for src, dst, mid in zip(sources, targets, held):
        size = src.shape[0]
        cut = pieces if len(src.shape) == 3 else 1
        step = size // cut
        for i in range(cut):
            rows = pl.ds(i * step, step)
            n = len(loads)
            loads.append(pltpu.make_async_copy(src.at[rows], mid.at[rows], in_sem.at[n]))
            stores.append(pltpu.make_async_copy(mid.at[rows], dst.at[rows], out_sem.at[n]))
    for copy in loads:
        copy.start()
    for load, store in zip(loads, stores):
        load.wait()
        store.start()
    for copy in stores:
        copy.wait()


def settle(results):
    anywhere = pl.BlockSpec(memory_space=pl.ANY)
    sem = pltpu.SemaphoreType.DMA((4 * len(results),))
    return pl.pallas_call(
        functools.partial(settle_kernel, len(results), 4),
        in_specs=[anywhere] * len(results),
        out_specs=[anywhere] * len(results),
        out_shape=[jax.ShapeDtypeStruct(a.shape, a.dtype) for a in results],
        scratch_shapes=[pltpu.VMEM(a.shape, a.dtype) for a in results] + [sem, sem],
        compiler_params=pltpu.CompilerParams(vmem_limit_bytes=62 << 20),
    )(*results)


def reversed_order(count):
    bits = count.bit_length() - 1
    return np.array([int(format(i, "b").zfill(bits)[::-1], 2) if bits else 0 for i in range(count)])


def run(queries, cotangent, w_key, w_value, database, nb_shard, nb_row):
    shards, seqs = lax.axis_size("db"), lax.axis_size("dp")
    _, rows, width = queries.shape
    _, count, neigh = nb_shard.shape
    base, nb_len, enc = database.shape
    window = rows // count
    asks = count * neigh
    slots = 3 * asks // (2 * shards)
    fused = shards == 4 and seqs == 8
    devices = shards * seqs
    share = enc // devices
    piece = nb_len // seqs
    wide = 2 * width
    quarter = enc // 8
    padded = -(-share // 16) * 16
    block = base * piece
    order = reversed_order(devices)
    if fused:
        bits = np.arange(devices)[:, None] // np.array([16, 8, 4, 2, 1])[None, :] % 2
        order = bits @ np.array([1, 4, 8, 2, 16])
    chunks, start = [], 0
    for size in (8, 8):
        size = size * width // 16
        for first in (0, width):
            chunks.append(slice(first + start, first + start + size))
        start += size
    source = (order[:, None] * share + np.arange(share)[None, :]).reshape(-1)
    shuffle = (source[:, None] == np.arange(enc)[None, :]).astype(jnp.bfloat16)
    cuts = [slice(0, 256), slice(256, 512), slice(512, enc)]

    anywhere = pl.BlockSpec(memory_space=pl.ANY)
    vmem = pl.BlockSpec(memory_space=pltpu.VMEM)
    smem = pl.BlockSpec(memory_space=pltpu.SMEM)
    sem = pltpu.SemaphoreType.DMA
    names, inputs, specs = [], [], []

    def give(name, value, spec):
        names.append(name)
        inputs.append(value)
        specs.append(spec)

    give("shard_ref", nb_shard[0].T, smem)
    give("row_ref", nb_row[0].T, smem)
    give("q_any", queries.reshape(count, window, width), anywhere)
    give("g_any", cotangent.reshape(count, window, width), anywhere)
    give("wk_any", w_key, anywhere)
    give("wv_any", w_value, anywhere)
    give("db_any", database, anywhere)
    give("shuffle_any", jnp.asarray(shuffle), anywhere)
    if fused:
        row = np.arange(4 * padded)[:, None]
        col = np.arange(4 * share)[None, :]
        spread = (row // padded == col // share) & (row % padded == col % share)
        give("spread_ref", jnp.asarray(spread.astype(jnp.bfloat16)), vmem)

    outs = [
        ("out_any", (count, window, width), BF, anywhere),
        ("dq_any", (count, window, width), BF, anywhere),
    ]
    if fused:
        outs += [
            ("gk_ref", (share, width), F32, vmem),
            ("gv_ref", (share, width), F32, vmem),
            ("gd_any", (block, enc), BF, anywhere),
        ]
    else:
        outs += [
            ("both_any", (asks * nb_len, wide), BF, anywhere),
            ("lt_any", (enc, asks * nb_len), BF, anywhere),
            ("ids", (8, 128), jnp.int32, vmem),
        ]
    scratch = [
        ("dbv", pltpu.VMEM((base, nb_len, enc), BF)),
        ("qwin", pltpu.VMEM((count + 1, window, width), BF)),
        ("gwin", pltpu.VMEM((count + 1, window, width), BF)),
        ("owin", pltpu.VMEM((count, window, width), BF)),
        ("dwin", pltpu.VMEM((count, window, width), BF)),
        ("oprev", pltpu.VMEM((window, width), BF)),
        ("dprev", pltpu.VMEM((window, width), BF)),
        ("qblk", pltpu.VMEM((window, width), BF)),
        ("gblk", pltpu.VMEM((window, width), BF)),
        ("wts", pltpu.VMEM((enc, wide), BF)),
        ("shuffle", pltpu.VMEM((enc, enc), BF)),
        ("states", pltpu.VMEM((neigh * nb_len, enc), BF)),
        ("both", pltpu.VMEM((asks * nb_len, wide), BF)),
        ("lt", pltpu.VMEM((enc, asks * nb_len), BF)),
        ("fetch", pltpu.VMEM((slots * 3, nb_len, enc), BF)),
        ("recv0", pltpu.VMEM((shards, nb_len, enc), BF)),
        ("recv1", pltpu.VMEM((shards, nb_len, enc), BF)),
        ("recv2", pltpu.VMEM((shards, nb_len, enc), BF)),
        ("asksend", pltpu.VMEM((8, 128), jnp.int32)),
        ("askbox", pltpu.VMEM((shards, 8, 128), jnp.int32)),
        ("ask_sm", pltpu.SMEM((shards, 8, 128), jnp.int32)),
        ("rank_sm", pltpu.SMEM((asks,), jnp.int32)),
        ("shard_sm", pltpu.SMEM((asks,), jnp.int32)),
        ("order_sm", pltpu.SMEM((count,), jnp.int32)),
        ("load_sem", sem((12,))),
        ("ask_send", sem((3,))),
        ("ask_recv", sem((3,))),
        ("edge_send", sem((4,))),
        ("edge_recv", sem((4,))),
        ("fetch_send", sem((slots * 3,))),
        ("fetch_recv", sem((slots * 3,))),
    ]
    if fused:
        peers = seqs - 1
        scratch += [
            ("ids", pltpu.VMEM((8, 128), jnp.int32)),
            ("gd_ref", pltpu.VMEM((block, enc), BF)),
            ("idbox", pltpu.VMEM((seqs, 8, 128), jnp.int32)),
            ("member", pltpu.VMEM((shards * block, seqs * asks * piece), BF)),
            ("got1", pltpu.VMEM((4 * quarter, wide), BF)),
            ("got2", pltpu.VMEM((2 * quarter, wide), BF)),
            ("got3", pltpu.VMEM((quarter, wide), BF)),
            ("zed", pltpu.VMEM((2, 2, padded, wide), BF)),
            ("got4", pltpu.VMEM((2, padded, wide), BF)),
            ("got5", pltpu.VMEM((padded, wide), BF)),
            ("arrived", pltpu.VMEM((seqs, asks * piece, enc), BF)),
            ("dgot1", pltpu.VMEM((2, block // nb_len, nb_len, enc), BF)),
            ("mine", pltpu.VMEM((2, block // nb_len, nb_len, enc), F32)),
            ("dgot2", pltpu.VMEM((block // nb_len, nb_len, enc), BF)),
            ("send_sem", sem((64,))),
            ("recv_sem", sem((64,))),
            ("across_send", sem((count, peers))),
            ("across_recv", sem((count, peers))),
            ("id_send", sem((peers,))),
            ("id_recv", sem((peers,))),
        ]
    names += [o[0] for o in outs] + [s[0] for s in scratch]
    plan = dict(
        names=names, fused=fused, asks=asks, neigh=neigh, slots=slots, piece=piece, cuts=cuts,
        chunks=chunks, unit=piece if fused else 1,
    )
    results = pl.pallas_call(
        functools.partial(kernel, plan),
        in_specs=specs,
        out_specs=[o[3] for o in outs],
        out_shape=[jax.ShapeDtypeStruct(o[1], o[2]) for o in outs],
        scratch_shapes=[s[1] for s in scratch],
        compiler_params=pltpu.CompilerParams(
            vmem_limit_bytes=62 << 20, collective_id=0, has_side_effects=True
        ),
        cost_estimate=pl.CostEstimate(
            flops=28 * 10**9, bytes_accessed=40 << 20, transcendentals=1 << 20
        ),
    )(*inputs)
    if fused:
        results = settle(results)
    attn_out = results[0].reshape(1, rows, width)
    grad_queries = results[1].reshape(1, rows, width)
    if fused:
        grad_database = results[4].reshape(base, piece, enc)
        return (attn_out, grad_queries, results[2], results[3], grad_database)

    both, lt, own_ids = results[2:]
    ids = jnp.broadcast_to(own_ids[0:1, 0:asks], (seqs, asks))
    ids = lax.all_to_all(ids, "dp", split_axis=0, concat_axis=0, tiled=True)
    ids = ids.reshape(seqs * asks)
    member = (ids[None, :] == jnp.arange(shards * base, dtype=jnp.int32)[:, None]).astype(BF)
    steps = [("db", b) for b in bits_of("db")] + [("dp", b) for b in bits_of("dp")]
    grads = []
    for part in range(2):
        grad = dot(lt, both[:, part * width : (part + 1) * width], ((1,), (0,)))
        grads.append(halve_all(grad.astype(BF), steps))
    w_both = jnp.concatenate([w_key, w_value], axis=1)
    dstates = dot(both, w_both, ((1,), (1,))).astype(BF)
    dstates = dstates.reshape(asks, seqs, piece, enc).transpose(1, 0, 2, 3)
    arrived = lax.all_to_all(dstates, "dp", split_axis=0, concat_axis=0, tiled=True)
    dense = dot(member, arrived.reshape(seqs * asks, piece * enc), ((1,), (0,)))
    dense = dense.astype(BF).reshape(shards, base, piece, enc)
    dense = jnp.stack([dense[i] for i in reversed_order(shards)])
    grad_database = halve_all(dense, [("db", b) for b in bits_of("db")])[0].astype(BF)
    return (attn_out, grad_queries, grads[0], grads[1], grad_database)


def halve(block, axis, bit):
    size = lax.axis_size(axis)
    half = block.shape[0] // 2
    side = lax.rem(lax.axis_index(axis) // bit, 2)
    give = lax.dynamic_slice_in_dim(block, (1 - side) * half, half, 0)
    mine = lax.dynamic_slice_in_dim(block, side * half, half, 0)
    got = lax.ppermute(give, axis, [(i, i ^ bit) for i in range(size)])
    return mine.astype(F32) + got.astype(F32)


def bits_of(axis):
    size = lax.axis_size(axis)
    return [1 << b for b in range(size.bit_length() - 1)]


def halve_all(block, steps):
    for axis, bit in steps[:-1]:
        block = halve(block, axis, bit).astype(BF)
    return halve(block, *steps[-1])


def solution(mesh):
    return jax.shard_map(
        run,
        mesh=mesh,
        in_specs=(
            P("dp", "db", None),
            P("dp", "db", None),
            P(),
            P(),
            P("db", None, None),
            P("dp", "db", None),
            P("dp", "db", None),
        ),
        out_specs=(
            P("dp", "db", None),
            P("dp", "db", None),
            P(("dp", "db"), None),
            P(("dp", "db"), None),
            P("db", "dp", None),
        ),
        check_vma=False,
    )
```

```python
import functools
import math
from types import SimpleNamespace

import jax
import jax.numpy as jnp
import numpy as np
from jax import lax
from jax.experimental import pallas as pl
from jax.experimental.pallas import tpu as pltpu
from jax.sharding import PartitionSpec as P

HSIZE = 128
BF, F32 = jnp.bfloat16, jnp.float32
MESH = pl.DeviceIdType.MESH


def dot(a, b, dims):
    return lax.dot_general(a, b, (dims, ((), ())), preferred_element_type=F32)


def choose(level, wanted, a, b):
    same = jnp.full(a.shape, level, jnp.int32) == wanted
    return jnp.where(same, a.astype(F32), b.astype(F32)).astype(BF)


def add(a, b):
    return (a.astype(F32) + b.astype(F32)).astype(BF)


def attend(r, u, states, group):
    width = r.qblk.shape[1]
    span = states.shape[0]
    scale = 1.0 / math.sqrt(HSIZE)
    rows = pl.ds(pl.multiple_of(u * span, span), span)
    for first in range(0, width // HSIZE, group):
        many = slice(first * HSIZE, (first + group) * HSIZE)
        vmany = slice(width + first * HSIZE, width + (first + group) * HSIZE)
        keys = dot(states, r.wts[:, many], ((1,), (0,))).astype(BF)
        values = dot(states, r.wts[:, vmany], ((1,), (0,))).astype(BF)
        heads = range(group)
        local = [slice(h * HSIZE, (h + 1) * HSIZE) for h in heads]
        cols = [slice((first + h) * HSIZE, (first + h + 1) * HSIZE) for h in heads]
        vcols = [slice(width + (first + h) * HSIZE, width + (first + h + 1) * HSIZE) for h in heads]
        q = [r.qblk[:, cols[h]] for h in heads]
        g = [r.gblk[:, cols[h]] for h in heads]
        k = [keys[:, local[h]] for h in heads]
        v = [values[:, local[h]] for h in heads]
        scores = [dot(q[h], k[h], ((1,), (1,))) * scale for h in heads]
        dprob = [dot(g[h], v[h], ((1,), (1,))) for h in heads]
        expo = [jnp.exp(t - jnp.max(t, axis=-1, keepdims=True)) for t in scores]
        prob = [t * (1.0 / jnp.sum(t, axis=-1, keepdims=True)) for t in expo]
        rowdot = [jnp.sum(prob[h] * dprob[h], axis=-1, keepdims=True) for h in heads]
        dscore = [(prob[h] * (dprob[h] - rowdot[h]) * scale).astype(BF) for h in heads]
        prob_b = [t.astype(BF) for t in prob]
        for h in heads:
            r.owin[u, :, cols[h]] = dot(prob_b[h], v[h], ((1,), (0,))).astype(BF)
            r.dwin[u, :, cols[h]] = dot(dscore[h], k[h], ((1,), (0,))).astype(BF)
        for h in heads:
            r.both[rows, cols[h]] = dot(dscore[h], q[h], ((0,), (0,))).astype(BF)
            r.both[rows, vcols[h]] = dot(prob_b[h], g[h], ((0,), (0,))).astype(BF)


def kernel(plan, *refs):
    r = SimpleNamespace(**dict(zip(plan["names"], refs)))
    fused, asks, neigh, slots = plan["fused"], plan["asks"], plan["neigh"], plan["slots"]
    piece = plan["piece"]
    count = asks // neigh
    dp, db = lax.axis_index("dp"), lax.axis_index("db")
    shards = r.recv0.shape[0]
    nb_len = r.recv0.shape[1]
    base = r.dbv.shape[0]
    enc, wide = r.wts.shape
    half = wide // 2
    span = neigh * nb_len
    window = r.qblk.shape[0]
    recvs = [r.recv0, r.recv1, r.recv2]

    c, x = lax.rem(db, 2), db // 2
    core, far = db + 1 - 2 * c, db + 2 - 4 * x
    cross = far + 1 - 2 * c
    near = [(dp, far), (dp, cross), (dp, core)]
    after, before = (dp, lax.rem(db + 1, shards)), (dp, lax.rem(db + shards - 1, shards))
    seqs = lax.axis_size("dp")
    others = [(lax.rem(dp + d, seqs), db) for d in range(1, seqs)] if fused else []

    loads = [
        pltpu.make_async_copy(r.db_any, r.dbv, r.load_sem.at[0]),
        pltpu.make_async_copy(r.q_any, r.qwin.at[0:count], r.load_sem.at[1]),
        pltpu.make_async_copy(r.g_any, r.gwin.at[0:count], r.load_sem.at[2]),
        pltpu.make_async_copy(r.wk_any, r.wts.at[:, 0:half], r.load_sem.at[3]),
        pltpu.make_async_copy(r.wv_any, r.wts.at[:, half:wide], r.load_sem.at[4]),
        pltpu.make_async_copy(r.shuffle_any, r.shuffle, r.load_sem.at[5]),
    ]
    for load in loads:
        load.start()
    barrier = pltpu.get_barrier_semaphore()
    for peer in near + others:
        pl.semaphore_signal(barrier, inc=1, device_id=peer, device_id_type=MESH)

    def flag(condition):
        return condition.astype(jnp.int32)

    named_shard = [[r.shard_ref[n, u] for n in range(neigh)] for u in range(count)]
    named_row = [[r.row_ref[n, u] for n in range(neigh)] for u in range(count)]
    flat = [t for pair in named_shard for t in pair]
    crowded = [
        sum(flag(sum(flag(other == t) for other in flat) >= slots) for t in pair)
        for pair in named_shard
    ]
    total = sum(crowded)
    open_, is_last = jnp.int32(1), []
    for u in range(count):
        chosen = open_ * flag(crowded[u] * slots == total)
        is_last.append(chosen)
        open_ = open_ - chosen
    order, target, wanted = [], [], []

    def swapped(values, u):
        if u < count - 1:
            return values[u] + is_last[u] * (values[count - 1] - values[u])
        return sum(is_last[v] * values[v] for v in range(count))

    for u in range(count):
        order.append(swapped(list(range(count)), u))
        r.order_sm[u] = order[u]
        for n in range(neigh):
            target.append(swapped([pair[n] for pair in named_shard], u))
            wanted.append(swapped([pair[n] for pair in named_row], u))
    rank = []
    for a in range(asks):
        seen = jnp.int32(0)
        for b in range(a):
            seen = seen + flag(target[b] == target[a])
        rank.append(seen)
        r.rank_sm[a] = seen
        r.shard_sm[a] = target[a]
    row = lax.broadcasted_iota(jnp.int32, (8, 128), 0)
    lane = lax.broadcasted_iota(jnp.int32, (8, 128), 1)
    mine = jnp.zeros((8, 128), jnp.int32)
    for a in range(asks):
        mine = jnp.where((row == target[a]) & (lane == rank[a]), wanted[a], mine)
    r.asksend[...] = mine
    r.askbox[db] = mine

    def remote(src, dst, send_sem, recv_sem, peer):
        return pltpu.make_async_remote_copy(
            src_ref=src,
            dst_ref=dst,
            send_sem=send_sem,
            recv_sem=recv_sem,
            device_id=peer,
            device_id_type=MESH,
        )

    asked = [
        remote(r.asksend, r.askbox.at[db], r.ask_send.at[d], r.ask_recv.at[d], near[d])
        for d in range(3)
    ]
    edges = [
        remote(src.at[0], dst.at[count], r.edge_send.at[e], r.edge_recv.at[e], before)
        for e, (src, dst) in enumerate(((r.q_any, r.qwin), (r.g_any, r.gwin)))
    ]
    pl.semaphore_wait(barrier, len(near) + len(others))
    for copy in asked + edges:
        copy.start()

    own = jnp.zeros((8, 128), jnp.int32)
    for a in range(asks):
        own = jnp.where(lane // plan["unit"] == a, target[a] * base + wanted[a], own)
    r.ids[...] = own
    if fused:
        r.idbox[dp] = own
        named = [
            remote(r.ids, r.idbox.at[dp], r.id_send.at[d], r.id_recv.at[d], peer)
            for d, peer in enumerate(others)
        ]
        for copy in named:
            copy.start()

    for copy in asked:
        copy.wait_recv()
    to_scalar = pltpu.make_async_copy(r.askbox, r.ask_sm, r.load_sem.at[6])
    to_scalar.start()
    to_scalar.wait()
    loads[0].wait()
    rounds = []

    def entry(asker, k):
        return r.dbv[r.ask_sm[asker, db, k]]

    for k in range(slots):
        for d, peer in enumerate(near):
            r.fetch[k * 3 + d] = entry(peer[1], k)
        recvs[k][db] = entry(db, k)
        rounds.append(
            [
                remote(
                    r.fetch.at[k * 3 + d],
                    recvs[k].at[db],
                    r.fetch_send.at[k * 3 + d],
                    r.fetch_recv.at[k * 3 + d],
                    near[d],
                )
                for d in range(3)
            ]
        )
        if k == 0:
            for copy in rounds[0]:
                copy.start()
    if fused:
        block = r.gd_ref.shape[0]
        lanes = r.member.shape[1] // seqs
        for copy in named:
            copy.wait_recv()
        row = lax.broadcasted_iota(jnp.int32, (block, lanes), 0)
        lane = lax.broadcasted_iota(jnp.int32, (block, lanes), 1)
        place = jnp.where(row % piece == lane % piece, row // piece, -1)

        @pl.loop(0, shards)
        def _(i):
            rows = pl.ds(pl.multiple_of(i * block, block), block)
            for k in range(seqs):
                hit = place == r.idbox[k][0:1] - i * (block // piece)
                r.member[rows, k * lanes : (k + 1) * lanes] = jnp.where(
                    hit & (place >= 0), 1.0, 0.0
                ).astype(BF)

    for load in loads[1:]:
        load.wait()
    for copy in edges:
        copy.wait_recv()

    @pl.when(db == shards - 1)
    def _():
        r.qwin[count] = jnp.zeros((window, half), BF)
        r.gwin[count] = jnp.zeros((window, half), BF)


    cuts = plan["cuts"]

    def across(u, d):
        start = pl.multiple_of(u * neigh * piece, neigh * piece)
        rows = pl.ds(start, neigh * piece)
        return remote(
            r.dbv.at[others[d][0], rows],
            r.arrived.at[dp, rows],
            r.across_send.at[u, d],
            r.across_recv.at[u, d],
            others[d],
        )

    last = lax.broadcasted_iota(jnp.int32, (16, half), 0) == 15

    @pl.loop(0, count)
    def _(u):
        def pick(levels):
            for n in range(neigh):
                a = u * neigh + n
                t, level = r.shard_sm[a], r.rank_sm[a]
                block = recvs[levels - 1][t]
                for j in range(levels - 1):
                    block = choose(level, j, recvs[j][t], block)
                r.states[n * nb_len : (n + 1) * nb_len] = block

        @pl.when(u == 0)
        def _():
            for copy in rounds[0]:
                copy.wait_recv()
            for copy in rounds[1]:
                copy.start()
            pick(1)

        @pl.when(u == 1)
        def _():
            for copy in rounds[1]:
                copy.wait_recv()
            for copy in rounds[2]:
                copy.start()

        @pl.when((u > 0) & (u < count - 1))
        def _():
            pick(2)

        @pl.when(u == count - 1)
        def _():
            for copy in rounds[2]:
                copy.wait_recv()
            pick(3)

        place = r.order_sm[u]
        for win, blk in ((r.qwin, r.qblk), (r.gwin, r.gblk)):
            tail = slice(window - 16, window)
            blk[0 : window - 16] = win[place + 1, 0 : window - 16]
            blk[tail] = jnp.where(
                last, win[place, tail].astype(F32), win[place + 1, tail].astype(F32)
            ).astype(BF)

        states = r.states[...]
        attend(r, u, states, 16)

        if fused:
            rows = pl.ds(pl.multiple_of(u * span, span), span)
            for h, cols in enumerate(cuts):
                out = dot(r.both[rows], r.wts[cols], ((1,), (1,))).astype(BF)
                for n in range(neigh):
                    for j in range(seqs):
                        into = pl.ds(pl.multiple_of((u * neigh + n) * piece, piece), piece)
                        start = n * nb_len + j * piece
                        r.dbv[j, into, cols] = out[start : start + piece]
                part = pl.ds(pl.multiple_of(u * neigh * piece, neigh * piece), neigh * piece)
                r.arrived[dp, part, cols] = r.dbv[dp, part, cols]
            for d in range(len(others)):
                across(u, d).start()
        r.lt[:, pl.ds(pl.multiple_of(u * span, span), span)] = dot(
            r.shuffle[...], states, ((1,), (1,))
        ).astype(BF)

    r.qblk[...] = r.owin[r.order_sm[count - 1]]
    r.gblk[...] = r.dwin[r.order_sm[count - 1]]
    passed = [
        remote(blk, got, r.edge_send.at[2 + e], r.edge_recv.at[2 + e], after)
        for e, (blk, got) in enumerate(((r.qblk, r.oprev), (r.gblk, r.dprev)))
    ]
    for copy in passed:
        copy.start()

    def edge_outputs():
        writes = []
        for e, (win, got, full, out) in enumerate(
            ((r.owin, r.oprev, r.qwin, r.out_any), (r.dwin, r.dprev, r.gwin, r.dq_any))
        ):
            head, tail = slice(0, window - 16), slice(window - 16, window)
            for w in range(1, count):
                mine, back = r.order_sm[w], r.order_sm[w - 1]
                full[w, head] = win[back, head]
                full[w, tail] = jnp.where(
                    last, win[mine, tail].astype(F32), win[back, tail].astype(F32)
                ).astype(BF)
            passed[e].wait_recv()
            keep = jnp.where(db > 0, 1.0, 0.0)
            full[0, head] = (got[head].astype(F32) * keep).astype(BF)
            full[0, tail] = jnp.where(
                last, win[r.order_sm[0], tail].astype(F32), got[tail].astype(F32) * keep
            ).astype(BF)
            writes.append(pltpu.make_async_copy(full.at[0:count], out, r.load_sem.at[7 + e]))
            writes[-1].start()
        return writes

    sent = asked + edges + passed + [copy for part in rounds for copy in part]
    if fused:
        finish(r, plan, remote, across, others, named, edge_outputs, sent)
        return
    writes = edge_outputs()
    for n, (src, dst) in enumerate(((r.both, r.both_any), (r.lt, r.lt_any))):
        writes.append(pltpu.make_async_copy(src, dst, r.load_sem.at[9 + n]))
        writes[-1].start()
    for copy in writes:
        copy.wait()
    for copy in sent:
        copy.wait_send()


def finish(r, plan, remote, across, others, named, edge_outputs, sent):
    piece = plan["piece"]
    cuts = plan["cuts"]
    dp, db = lax.axis_index("dp"), lax.axis_index("db")
    seqs = r.arrived.shape[0]
    enc, wide = r.wts.shape
    half = wide // 2
    quarter = enc // 8
    c, x = lax.rem(db, 2), db // 2
    y, z0, z1 = lax.rem(dp, 2), lax.rem(dp // 2, 2), dp // 4
    pc = (dp, db + 1 - 2 * c)
    px = (dp, db + 2 - 4 * x)
    py = (dp + 1 - 2 * y, db)
    pz0 = (dp + 2 - 4 * z0, db)
    pz1 = (dp + 4 - 8 * z1, db)
    copies = []
    tile = 1024

    def send(src, dst, peer):
        number = len(copies)
        copy = remote(src, dst, r.send_sem.at[number], r.recv_sem.at[number], peer)
        copy.start()
        copies.append(copy)
        return copy

    chunks = plan["chunks"]

    def part(p, row, n=1):
        rows = pl.ds(pl.multiple_of(row * quarter, quarter), n * quarter)
        return r.both.at[rows, chunks[p]]

    def weight_grad(p):
        start, stop = chunks[p].start, chunks[p].stop

        @pl.loop(0, (stop - start) // tile)
        def _(t):
            cols = pl.ds(pl.multiple_of(start + t * tile, tile), tile)
            out = jnp.dot(r.lt[...], r.both[:, cols], preferred_element_type=F32)
            r.both[0:enc, cols] = out.astype(BF)

        return send(part(p, (1 - c) * 4, 4), r.got1.at[:, chunks[p]], pc)

    def join(p, row, got):
        here = part(p, row)
        here[...] = add(here[...], got)

    def rows_of(i, n=1):
        return slice(i * quarter, (i + n) * quarter)

    def after_core(p, copy):
        copy.wait_recv()
        for i in range(4):
            join(p, c * 4 + i, r.got1[rows_of(i), chunks[p]])

    def first(p):
        if p % 2 == 0:
            src = part(p, c * 4 + (1 - y) * 2, 2)
            return [send(src, r.got2.at[:, chunks[p]], py)]
        return [
            send(part(p, c * 4 + i * 2 + 1 - z0), r.got2.at[rows_of(i), chunks[p]], pz0)
            for i in range(2)
        ]

    def second(p, arrivals):
        for copy in arrivals:
            copy.wait_recv()
        for i in range(2):
            into = c * 4 + y * 2 + i if p % 2 == 0 else c * 4 + i * 2 + z0
            join(p, into, r.got2[rows_of(i), chunks[p]])
        if p % 2 == 0:
            return send(part(p, c * 4 + y * 2 + 1 - z0), r.got3.at[:, chunks[p]], pz0)
        return send(part(p, c * 4 + (1 - y) * 2 + z0), r.got3.at[:, chunks[p]], py)

    def third(p, copy):
        copy.wait_recv()
        total = add(part(p, c * 4 + y * 2 + z0)[...], r.got3[:, chunks[p]])
        _, _, padded, _ = r.zed.shape
        r.zed[:, :, :, chunks[p]] = (
            jnp.dot(r.spread_ref[...], total, preferred_element_type=F32)
            .astype(BF)
            .reshape(2, 2, padded, total.shape[1])
        )
        return send(r.zed.at[1 - x, :, :, chunks[p]], r.got4.at[:, :, chunks[p]], px)

    def fourth(p, copy):
        copy.wait_recv()
        for j in range(2):
            r.zed[x, j, :, chunks[p]] = add(
                r.zed[x, j, :, chunks[p]], r.got4[j, :, chunks[p]]
            )
        return send(r.zed.at[x, 1 - z1, :, chunks[p]], r.got5.at[:, chunks[p]], pz1)

    def fifth(p, copy):
        copy.wait_recv()
        start, stop = chunks[p].start, chunks[p].stop
        out_ref, back = (r.gk_ref, 0) if start < half else (r.gv_ref, half)
        summed = r.zed[x, z1, :, chunks[p]].astype(F32) + r.got5[:, chunks[p]].astype(F32)
        out_ref[:, start - back : stop - back] = summed[: out_ref.shape[0]]

    block = r.gd_ref.shape[0]
    every = r.arrived.shape[0] * r.arrived.shape[1]
    count = r.across_send.shape[0]

    def dense(shard, cols):
        return jnp.dot(
            r.member[pl.ds(pl.multiple_of(shard * block, block), block)],
            r.arrived[:, :, cols].reshape(every, cols.stop - cols.start),
            preferred_element_type=F32,
        ).reshape(many, nb_len, cols.stop - cols.start)

    many, nb_len = r.dgot2.shape[0:2]
    give = [slice(seqs + n * many, seqs + (n + 1) * many) for n in range(3)]

    def give_side(h, far):
        cols = cuts[h]
        side = 1 - x if far else x
        r.dbv[give[far], :, cols] = dense(2 * side + 1 - c, cols).astype(BF)
        return send(r.dbv.at[give[far], :, cols], r.dgot1.at[far, :, :, cols], pc)

    def own_side(h, far):
        side = 1 - x if far else x
        r.mine[far, :, :, cuts[h]] = dense(2 * side + c, cuts[h])

    def x_start(h, copy):
        cols = cuts[h]
        copy.wait_recv()
        summed = r.mine[1, :, :, cols] + r.dgot1[1, :, :, cols].astype(F32)
        r.dbv[give[2], :, cols] = summed.astype(BF)
        return send(r.dbv.at[give[2], :, cols], r.dgot2.at[:, :, cols], px)

    pairs = len(chunks) // 2
    way = [None] * len(chunks)
    for p in range(len(chunks)):
        way[p] = weight_grad(p)
        if p > 0:
            after_core(p - 1, way[p - 1])
            if p - 1 < 2 * 2:
                way[p - 1] = first(p - 1)
    after_core(len(chunks) - 1, way[-1])
    if len(chunks) - 1 < 2 * 2:
        way[-1] = first(len(chunks) - 1)
    writes = edge_outputs()
    for u in range(count):
        for d in range(len(others)):
            across(u, d).wait_recv()
    far_side, xcopy = [], []
    for h in range(len(cuts)):
        far_side.append(give_side(h, 1))
        if h > 0:
            xcopy.append(x_start(h - 1, far_side[h - 1]))
        own_side(h, 1)
    xcopy.append(x_start(len(cuts) - 1, far_side[-1]))
    near_side = []
    for h in range(len(cuts)):
        near_side.append(give_side(h, 0))
        own_side(h, 0)
    for i in range(pairs):
        for p in (2 * i, 2 * i + 1):
            way[p] = second(p, way[p])
        if i + 2 < pairs:
            for p in (2 * i, 2 * i + 1):
                way[p + 2 * 2] = first(p + 2 * 2)
        if i > 0:
            for p in (2 * i - 2, 2 * i - 1):
                way[p] = third(p, way[p])
        if i > 1:
            for p in (2 * i - 4, 2 * i - 3):
                way[p] = fourth(p, way[p])
    ends = (len(chunks) - 2, len(chunks) - 1)
    for p in ends:
        way[p] = third(p, way[p])
    if pairs > 1:
        for p in (ends[0] - 2, ends[0] - 1):
            way[p] = fourth(p, way[p])
    for h, cols in enumerate(cuts):
        near_side[h].wait_recv()
        xcopy[h].wait_recv()
        summed = r.mine[0, :, :, cols] + r.dgot1[0, :, :, cols].astype(F32)
        summed = summed + r.dgot2[:, :, cols].astype(F32)
        r.gd_ref[:, cols] = summed.astype(BF).reshape(block, cols.stop - cols.start)
    writes.append(pltpu.make_async_copy(r.gd_ref, r.gd_any, r.load_sem.at[9]))
    writes[-1].start()
    for p in ends:
        way[p] = fourth(p, way[p])
    for p in range(len(chunks)):
        fifth(p, way[p])
    for copy in copies + named + sent:
        copy.wait_send()
    for u in range(count):
        for d in range(len(others)):
            across(u, d).wait_send()
    for copy in writes:
        copy.wait()


def settle_kernel(count, pieces, *refs):
    sources, targets, held = refs[:count], refs[count : 2 * count], refs[2 * count : 3 * count]
    in_sem, out_sem = refs[3 * count :]
    loads, stores = [], []
    for src, dst, mid in zip(sources, targets, held):
        size = src.shape[0]
        cut = pieces if len(src.shape) == 3 else 1
        step = size // cut
        for i in range(cut):
            rows = pl.ds(i * step, step)
            n = len(loads)
            loads.append(pltpu.make_async_copy(src.at[rows], mid.at[rows], in_sem.at[n]))
            stores.append(pltpu.make_async_copy(mid.at[rows], dst.at[rows], out_sem.at[n]))
    for copy in loads:
        copy.start()
    for load, store in zip(loads, stores):
        load.wait()
        store.start()
    for copy in stores:
        copy.wait()


def settle(results):
    anywhere = pl.BlockSpec(memory_space=pl.ANY)
    sem = pltpu.SemaphoreType.DMA((4 * len(results),))
    return pl.pallas_call(
        functools.partial(settle_kernel, len(results), 4),
        in_specs=[anywhere] * len(results),
        out_specs=[anywhere] * len(results),
        out_shape=[jax.ShapeDtypeStruct(a.shape, a.dtype) for a in results],
        scratch_shapes=[pltpu.VMEM(a.shape, a.dtype) for a in results] + [sem, sem],
        compiler_params=pltpu.CompilerParams(vmem_limit_bytes=62 << 20),
    )(*results)


def reversed_order(count):
    bits = count.bit_length() - 1
    return np.array([int(format(i, "b").zfill(bits)[::-1], 2) if bits else 0 for i in range(count)])


def run(queries, cotangent, w_key, w_value, database, nb_shard, nb_row):
    shards, seqs = lax.axis_size("db"), lax.axis_size("dp")
    _, rows, width = queries.shape
    _, count, neigh = nb_shard.shape
    base, nb_len, enc = database.shape
    window = rows // count
    asks = count * neigh
    slots = 3 * asks // (2 * shards)
    fused = shards == 4 and seqs == 8
    devices = shards * seqs
    share = enc // devices
    piece = nb_len // seqs
    wide = 2 * width
    quarter = enc // 8
    padded = -(-share // 16) * 16
    block = base * piece
    order = reversed_order(devices)
    if fused:
        bits = np.arange(devices)[:, None] // np.array([16, 8, 4, 2, 1])[None, :] % 2
        order = bits @ np.array([1, 4, 8, 2, 16])
    chunks, start = [], 0
    for size in (8, 8):
        size = size * width // 16
        for first in (0, width):
            chunks.append(slice(first + start, first + start + size))
        start += size
    source = (order[:, None] * share + np.arange(share)[None, :]).reshape(-1)
    shuffle = (source[:, None] == np.arange(enc)[None, :]).astype(jnp.bfloat16)
    cuts = [slice(0, 256), slice(256, 512), slice(512, enc)]

    anywhere = pl.BlockSpec(memory_space=pl.ANY)
    vmem = pl.BlockSpec(memory_space=pltpu.VMEM)
    smem = pl.BlockSpec(memory_space=pltpu.SMEM)
    sem = pltpu.SemaphoreType.DMA
    names, inputs, specs = [], [], []

    def give(name, value, spec):
        names.append(name)
        inputs.append(value)
        specs.append(spec)

    give("shard_ref", nb_shard[0].T, smem)
    give("row_ref", nb_row[0].T, smem)
    give("q_any", queries.reshape(count, window, width), anywhere)
    give("g_any", cotangent.reshape(count, window, width), anywhere)
    give("wk_any", w_key, anywhere)
    give("wv_any", w_value, anywhere)
    give("db_any", database, anywhere)
    give("shuffle_any", jnp.asarray(shuffle), anywhere)
    if fused:
        row = np.arange(4 * padded)[:, None]
        col = np.arange(4 * share)[None, :]
        spread = (row // padded == col // share) & (row % padded == col % share)
        give("spread_ref", jnp.asarray(spread.astype(jnp.bfloat16)), vmem)

    outs = [
        ("out_any", (count, window, width), BF, anywhere),
        ("dq_any", (count, window, width), BF, anywhere),
    ]
    if fused:
        outs += [
            ("gk_ref", (share, width), F32, vmem),
            ("gv_ref", (share, width), F32, vmem),
            ("gd_any", (block, enc), BF, anywhere),
        ]
    else:
        outs += [
            ("both_any", (asks * nb_len, wide), BF, anywhere),
            ("lt_any", (enc, asks * nb_len), BF, anywhere),
            ("ids", (8, 128), jnp.int32, vmem),
        ]
    scratch = [
        ("dbv", pltpu.VMEM((base, nb_len, enc), BF)),
        ("qwin", pltpu.VMEM((count + 1, window, width), BF)),
        ("gwin", pltpu.VMEM((count + 1, window, width), BF)),
        ("owin", pltpu.VMEM((count, window, width), BF)),
        ("dwin", pltpu.VMEM((count, window, width), BF)),
        ("oprev", pltpu.VMEM((window, width), BF)),
        ("dprev", pltpu.VMEM((window, width), BF)),
        ("qblk", pltpu.VMEM((window, width), BF)),
        ("gblk", pltpu.VMEM((window, width), BF)),
        ("wts", pltpu.VMEM((enc, wide), BF)),
        ("shuffle", pltpu.VMEM((enc, enc), BF)),
        ("states", pltpu.VMEM((neigh * nb_len, enc), BF)),
        ("both", pltpu.VMEM((asks * nb_len, wide), BF)),
        ("lt", pltpu.VMEM((enc, asks * nb_len), BF)),
        ("fetch", pltpu.VMEM((slots * 3, nb_len, enc), BF)),
        ("recv0", pltpu.VMEM((shards, nb_len, enc), BF)),
        ("recv1", pltpu.VMEM((shards, nb_len, enc), BF)),
        ("recv2", pltpu.VMEM((shards, nb_len, enc), BF)),
        ("asksend", pltpu.VMEM((8, 128), jnp.int32)),
        ("askbox", pltpu.VMEM((shards, 8, 128), jnp.int32)),
        ("ask_sm", pltpu.SMEM((shards, 8, 128), jnp.int32)),
        ("rank_sm", pltpu.SMEM((asks,), jnp.int32)),
        ("shard_sm", pltpu.SMEM((asks,), jnp.int32)),
        ("order_sm", pltpu.SMEM((count,), jnp.int32)),
        ("load_sem", sem((12,))),
        ("ask_send", sem((3,))),
        ("ask_recv", sem((3,))),
        ("edge_send", sem((4,))),
        ("edge_recv", sem((4,))),
        ("fetch_send", sem((slots * 3,))),
        ("fetch_recv", sem((slots * 3,))),
    ]
    if fused:
        peers = seqs - 1
        scratch += [
            ("ids", pltpu.VMEM((8, 128), jnp.int32)),
            ("gd_ref", pltpu.VMEM((block, enc), BF)),
            ("idbox", pltpu.VMEM((seqs, 8, 128), jnp.int32)),
            ("member", pltpu.VMEM((shards * block, seqs * asks * piece), BF)),
            ("got1", pltpu.VMEM((4 * quarter, wide), BF)),
            ("got2", pltpu.VMEM((2 * quarter, wide), BF)),
            ("got3", pltpu.VMEM((quarter, wide), BF)),
            ("zed", pltpu.VMEM((2, 2, padded, wide), BF)),
            ("got4", pltpu.VMEM((2, padded, wide), BF)),
            ("got5", pltpu.VMEM((padded, wide), BF)),
            ("arrived", pltpu.VMEM((seqs, asks * piece, enc), BF)),
            ("dgot1", pltpu.VMEM((2, block // nb_len, nb_len, enc), BF)),
            ("mine", pltpu.VMEM((2, block // nb_len, nb_len, enc), F32)),
            ("dgot2", pltpu.VMEM((block // nb_len, nb_len, enc), BF)),
            ("send_sem", sem((64,))),
            ("recv_sem", sem((64,))),
            ("across_send", sem((count, peers))),
            ("across_recv", sem((count, peers))),
            ("id_send", sem((peers,))),
            ("id_recv", sem((peers,))),
        ]
    names += [o[0] for o in outs] + [s[0] for s in scratch]
    plan = dict(
        names=names, fused=fused, asks=asks, neigh=neigh, slots=slots, piece=piece, cuts=cuts,
        chunks=chunks, unit=piece if fused else 1,
    )
    results = pl.pallas_call(
        functools.partial(kernel, plan),
        in_specs=specs,
        out_specs=[o[3] for o in outs],
        out_shape=[jax.ShapeDtypeStruct(o[1], o[2]) for o in outs],
        scratch_shapes=[s[1] for s in scratch],
        compiler_params=pltpu.CompilerParams(
            vmem_limit_bytes=62 << 20, collective_id=0, has_side_effects=True
        ),
        cost_estimate=pl.CostEstimate(
            flops=28 * 10**9, bytes_accessed=40 << 20, transcendentals=1 << 20
        ),
    )(*inputs)
    if fused:
        results = settle(results)
    attn_out = results[0].reshape(1, rows, width)
    grad_queries = results[1].reshape(1, rows, width)
    if fused:
        grad_database = results[4].reshape(base, piece, enc)
        return (attn_out, grad_queries, results[2], results[3], grad_database)

    both, lt, own_ids = results[2:]
    ids = jnp.broadcast_to(own_ids[0:1, 0:asks], (seqs, asks))
    ids = lax.all_to_all(ids, "dp", split_axis=0, concat_axis=0, tiled=True)
    ids = ids.reshape(seqs * asks)
    member = (ids[None, :] == jnp.arange(shards * base, dtype=jnp.int32)[:, None]).astype(BF)
    steps = [("db", b) for b in bits_of("db")] + [("dp", b) for b in bits_of("dp")]
    grads = []
    for part in range(2):
        grad = dot(lt, both[:, part * width : (part + 1) * width], ((1,), (0,)))
        grads.append(halve_all(grad.astype(BF), steps))
    w_both = jnp.concatenate([w_key, w_value], axis=1)
    dstates = dot(both, w_both, ((1,), (1,))).astype(BF)
    dstates = dstates.reshape(asks, seqs, piece, enc).transpose(1, 0, 2, 3)
    arrived = lax.all_to_all(dstates, "dp", split_axis=0, concat_axis=0, tiled=True)
    dense = dot(member, arrived.reshape(seqs * asks, piece * enc), ((1,), (0,)))
    dense = dense.astype(BF).reshape(shards, base, piece, enc)
    dense = jnp.stack([dense[i] for i in reversed_order(shards)])
    grad_database = halve_all(dense, [("db", b) for b in bits_of("db")])[0].astype(BF)
    return (attn_out, grad_queries, grads[0], grads[1], grad_database)


def halve(block, axis, bit):
    size = lax.axis_size(axis)
    half = block.shape[0] // 2
    side = lax.rem(lax.axis_index(axis) // bit, 2)
    give = lax.dynamic_slice_in_dim(block, (1 - side) * half, half, 0)
    mine = lax.dynamic_slice_in_dim(block, side * half, half, 0)
    got = lax.ppermute(give, axis, [(i, i ^ bit) for i in range(size)])
    return mine.astype(F32) + got.astype(F32)


def bits_of(axis):
    size = lax.axis_size(axis)
    return [1 << b for b in range(size.bit_length() - 1)]


def halve_all(block, steps):
    for axis, bit in steps[:-1]:
        block = halve(block, axis, bit).astype(BF)
    return halve(block, *steps[-1])


def solution(mesh):
    return jax.shard_map(
        run,
        mesh=mesh,
        in_specs=(
            P("dp", "db", None),
            P("dp", "db", None),
            P(),
            P(),
            P("db", None, None),
            P("dp", "db", None),
            P("dp", "db", None),
        ),
        out_specs=(
            P("dp", "db", None),
            P("dp", "db", None),
            P(("dp", "db"), None),
            P(("dp", "db"), None),
            P("db", "dp", None),
        ),
        check_vma=False,
    )
```
